32 devices in a mesh: group: 4 (over z), seq: 2 (over x), head: 4 (over y, core).
Axes of the slice: x: 2, y: 2, z: 4, core: 2. Of those that a mesh axis runs over, the one named last changes fastest.
Arguments:
- latents: bfloat16 [256, 64], P('seq'), may hold values from -6 to 6
- noise: bfloat16 [256, 64], P('seq'), may hold values from -6 to 6
- step: int32 [1], replicated, may hold values from 50 to 950
- stream: bfloat16 [256, 5120], P('seq'), may hold values from -6 to 6
- patch_embed_weight: bfloat16 [64, 5120], replicated, may hold values from -0.75 to 0.75
- prenorm_gain_vector: float32 [5120], replicated, may hold values from 0.5 to 1.5
- query_matrix: bfloat16 [5120, 4096], P('seq', ('group', 'head')), may hold values from -0.08385255 to 0.08385255
- key_matrix: bfloat16 [5120, 4096], P('seq', ('group', 'head')), may hold values from -1.0481569 to 1.0481569
- value_matrix: bfloat16 [5120, 4096], P('seq', ('group', 'head')), may hold values from -0.078125 to 0.078125
- output_matrix: bfloat16 [4096, 5120], P(('group', 'head'), 'seq'), may hold values from -0.09375 to 0.09375
- velocity_readout_weight: bfloat16 [64, 5120], replicated, may hold values from -0.078125 to 0.078125
- adapter_query_down: bfloat16 [5120, 128], P('seq'), may hold values from -0.078125 to 0.078125
- adapter_query_up: bfloat16 [128, 4096], P(None, ('group', 'head')), may hold values from -0.5 to 0.5
- adapter_output_down: bfloat16 [4096, 128], P(('group', 'head')), may hold values from -0.09375 to 0.09375
- adapter_output_up: bfloat16 [128, 5120], replicated, may hold values from -0.5 to 0.5
Outputs:
- latent_grad: float32 [256, 64], P('seq')
The draws below stay inside these ranges and needn't reach their ends.
All inputs are finite; a program needn't handle non-finite values. Where the reference program divides by a largest or mean magnitude, that divisor is 1e-20 or more.
Results may differ from the reference program's by a relative error of at most 0.015.
Values may be sent and summed in bfloat16 or wider, within the bound.
No kernel may reach another device: no remote copies, remote signals or barrier semaphores. Data moves between devices by JAX's collectives and lax.ppermute only.
A program may use at most 64 MiB of HBM per device.

```python
import jax
import jax.numpy as jnp
from jax import lax

MODEL_WIDTH = 5120
ATTENTION_HEADS = 32
HEAD_SIZE = 128
CHANNELS = 64
ADAPTER_RANK = 128
SEQ_LEN = 256


def paired_draw(key):
    first = jnp.clip(jax.random.normal(jax.random.fold_in(key, 7), (MODEL_WIDTH, ATTENTION_HEADS * HEAD_SIZE), jnp.float32), -6.0, 6.0)
    second = jnp.clip(jax.random.normal(jax.random.fold_in(key, 8), (MODEL_WIDTH, ATTENTION_HEADS * HEAD_SIZE), jnp.float32), -6.0, 6.0)
    return (first * MODEL_WIDTH ** (-0.5), second * MODEL_WIDTH ** (-0.5))


def draw_query_matrix(key, part):
    first, second = paired_draw(key)
    return first.astype(jnp.bfloat16)


def draw_key_matrix(key, part):
    first, second = paired_draw(key)
    return second.astype(jnp.bfloat16)


def block_scale(rng, extent, shards, low, top_value):
    gain, own = 1.0, jax.random.fold_in(rng, 6)
    for dim, parts in shards:
        steps = jnp.exp(jax.random.uniform(jax.random.fold_in(own, dim), (parts,), jnp.float32, low / len(shards), top_value / len(shards)))
        gain = gain * jnp.repeat(steps, extent[dim] // parts).reshape([-1 if axis == dim else 1 for axis in range(len(extent))])
    return gain


def normal_values(key, dims, width, most, split=(), kind=jnp.bfloat16):
    gain = block_scale(key, dims, split, -0.22, 0.18) if split else 1.0
    array = jax.random.normal(key, dims, jnp.float32) * width * gain
    return jnp.minimum(jnp.maximum(array, -most), most).astype(kind)


def setup_inputs(seed: int = 0) -> dict:
    key_of = jax.random.split(jax.random.key(seed), 16)
    return {
        "latents": normal_values(key_of[0], (SEQ_LEN, CHANNELS), 1.0, 6.0, ((0, 2),)),
        "noise": normal_values(key_of[1], (SEQ_LEN, CHANNELS), 1.0, 6.0, ((0, 2),)),
        "step": jax.random.randint(key_of[2], (1,), 50, 951).astype(jnp.int32),
        "stream": normal_values(key_of[3], (SEQ_LEN, MODEL_WIDTH), 1.0, 6.0, ((0, 2),)),
        "patch_embed_weight": normal_values(key_of[4], (CHANNELS, MODEL_WIDTH), CHANNELS ** -0.5, 0.75),
        "prenorm_gain_vector": jnp.clip(1.0 + 0.1 * jax.random.normal(key_of[5], (MODEL_WIDTH,), jnp.float32), 0.5, 1.5),
        "query_matrix": draw_query_matrix(jax.random.fold_in(key_of[15], 71), 0),
        "key_matrix": draw_key_matrix(jax.random.fold_in(key_of[15], 71), 0),
        "value_matrix": normal_values(key_of[8], (MODEL_WIDTH, ATTENTION_HEADS * HEAD_SIZE), MODEL_WIDTH ** -0.5, 0.078125, ((0, 2), (1, 16))),
        "output_matrix": normal_values(key_of[9], (ATTENTION_HEADS * HEAD_SIZE, MODEL_WIDTH), (ATTENTION_HEADS * HEAD_SIZE) ** -0.5, 0.09375, ((0, 16), (1, 2))),
        "velocity_readout_weight": normal_values(key_of[10], (CHANNELS, MODEL_WIDTH), MODEL_WIDTH ** -0.5, 0.078125),
        "adapter_query_down": normal_values(key_of[11], (MODEL_WIDTH, ADAPTER_RANK), MODEL_WIDTH ** -0.5, 0.078125, ((0, 2),)),
        "adapter_query_up": normal_values(key_of[12], (ADAPTER_RANK, ATTENTION_HEADS * HEAD_SIZE), ADAPTER_RANK ** -0.5, 0.5, ((1, 16),)),
        "adapter_output_down": normal_values(key_of[13], (ATTENTION_HEADS * HEAD_SIZE, ADAPTER_RANK), (ATTENTION_HEADS * HEAD_SIZE) ** -0.5, 0.09375, ((0, 16),)),
        "adapter_output_up": normal_values(key_of[14], (ADAPTER_RANK, MODEL_WIDTH), ADAPTER_RANK ** -0.5, 0.5),
    }


def attend_head(items):
    first, second, keys, values = items
    outs = []
    for query in (first, second):
        scores = jnp.dot(query, keys.T, preferred_element_type=jnp.float32)
        top = lax.optimization_barrier(jnp.max(scores, axis=-1, keepdims=True))
        weights = jnp.exp(scores - top)
        total = lax.optimization_barrier(jnp.sum(weights, axis=-1, keepdims=True))
        outs.append(jnp.dot(weights.astype(jnp.bfloat16), values, preferred_element_type=jnp.float32) / total)
    return jnp.stack(outs).astype(jnp.bfloat16)

def split_heads(matrix):
    return matrix.reshape(SEQ_LEN, ATTENTION_HEADS, HEAD_SIZE).transpose(1, 0, 2)

def reference(latents, noise, step, stream, patch_embed_weight, prenorm_gain_vector, query_matrix, key_matrix, value_matrix, output_matrix, velocity_readout_weight, adapter_query_down, adapter_query_up, adapter_output_down, adapter_output_up):
    level = (step[0].astype(jnp.float32) + 1.0) / 1000.0
    sigma = 5.0 * level / (1.0 + 4.0 * level)
    noisy = ((1.0 - sigma) * latents.astype(jnp.float32) + sigma * noise.astype(jnp.float32)).astype(jnp.bfloat16)
    hidden = (stream.astype(jnp.float32) + jnp.dot(noisy, patch_embed_weight, preferred_element_type=jnp.float32)).astype(jnp.bfloat16)
    hidden_wide = hidden.astype(jnp.float32)
    normalized_tokens = (hidden_wide * lax.rsqrt(lax.optimization_barrier(jnp.mean(hidden_wide * hidden_wide, axis=-1, keepdims=True)) + 1e-06) * prenorm_gain_vector).astype(jnp.bfloat16)
    logit_scale = HEAD_SIZE ** (-0.5)
    base_query_rows = jnp.dot(normalized_tokens, query_matrix, preferred_element_type=jnp.float32)
    adapter_hidden_rows = jnp.dot(normalized_tokens, adapter_query_down, preferred_element_type=jnp.float32).astype(jnp.bfloat16)
    adapter_query_delta = jnp.dot(adapter_hidden_rows, adapter_query_up, preferred_element_type=jnp.float32)
    queries = (base_query_rows * logit_scale).astype(jnp.bfloat16)
    fake_query_rows = ((base_query_rows + adapter_query_delta) * logit_scale).astype(jnp.bfloat16)
    keys = jnp.dot(normalized_tokens, key_matrix, preferred_element_type=jnp.float32).astype(jnp.bfloat16)
    values = jnp.dot(normalized_tokens, value_matrix, preferred_element_type=jnp.float32).astype(jnp.bfloat16)
    heads_out = lax.map(attend_head, (split_heads(queries), split_heads(fake_query_rows), split_heads(keys), split_heads(values)))
    attn = heads_out.transpose(1, 2, 0, 3).reshape(2, SEQ_LEN, ATTENTION_HEADS * HEAD_SIZE)
    blended_heads_whole = jnp.dot(output_matrix, velocity_readout_weight.T, preferred_element_type=jnp.float32)
    adapter_readout_delta = jnp.dot(adapter_output_up, velocity_readout_weight.T, preferred_element_type=jnp.float32).astype(jnp.bfloat16)
    mix = blended_heads_whole.astype(jnp.bfloat16)
    fake_head_blend = (blended_heads_whole + jnp.dot(adapter_output_down, adapter_readout_delta, preferred_element_type=jnp.float32)).astype(jnp.bfloat16)
    base = jnp.dot(hidden, velocity_readout_weight.T, preferred_element_type=jnp.float32)
    v_real = base + jnp.dot(attn[0], mix, preferred_element_type=jnp.float32)
    v_fake = base + jnp.dot(attn[1], fake_head_blend, preferred_element_type=jnp.float32)
    noisy_wide = noisy.astype(jnp.float32)
    x0_real = noisy_wide - sigma * v_real
    x0_fake = noisy_wide - sigma * v_fake
    weight = jnp.mean(jnp.abs(latents.astype(jnp.float32) - x0_real))
    return (x0_fake - x0_real) / weight
```

```python
import itertools

import jax
import jax.numpy as jnp
from jax import lax
from jax.sharding import PartitionSpec as P

HEAD_SIZE = 128
F32 = jnp.float32
BF16 = jnp.bfloat16


def contract_final_axis(left, right):
    return lax.dot_general(
        left, right, (((1,), (1,)), ((), ())), preferred_element_type=F32
    )


def dot(left, right):
    return jnp.dot(left, right, preferred_element_type=F32)


def noise_level(step):
    level = (step[0].astype(F32) + 1.0) / 1000.0
    return 5.0 * level / (1.0 + 4.0 * level)


def pairs(sizes, partner):
    def linear(coordinate):
        index = 0
        for value, size in zip(coordinate, sizes):
            index = index * size + value
        return index

    return [
        (linear(c), linear(partner(*c)))
        for c in itertools.product(*[range(n) for n in sizes])
    ]


def split_high_low(x):
    high = lax.reduce_precision(x, 8, 7)
    return high.astype(BF16), (x - high).astype(BF16)


def rows_of(x, index, count):
    return lax.dynamic_slice_in_dim(x, index * count, count, 0)


def columns_of(x, index, count):
    return lax.dynamic_slice_in_dim(x, index * count, count, 1)


def fold(x):
    half = x.shape[0] // 2
    return jnp.concatenate([x[:half], x[half:]], axis=1)


def unfold(x):
    half = x.shape[1] // 2
    return jnp.concatenate([x[:, :half], x[:, half:]], axis=0)


def paired_local(
    sizes,
    latents,
    noise,
    step,
    stream,
    patch_embed_weight,
    prenorm_gain_vector,
    query_matrix,
    key_matrix,
    value_matrix,
    output_matrix,
    velocity_readout_weight,
    adapter_query_down,
    adapter_query_up,
    adapter_output_down,
    adapter_output_up,
):
    groups, _, heads = sizes
    seq = lax.axis_index("seq")
    head = lax.axis_index("head")
    group = lax.axis_index("group")
    core = head % 2
    tokens, channels = latents.shape
    half_width = query_matrix.shape[0]
    quarter = half_width // 2
    columns = query_matrix.shape[1] // 2
    to_x = pairs((2,), lambda s: (s ^ 1,))
    to_core = pairs((heads,), lambda h: (h ^ 1,))
    to_y = pairs((heads,), lambda h: (h ^ 2,))
    to_xy = pairs((2, heads), lambda s, h: (s ^ 1, h ^ 2))

    sigma = noise_level(step)
    latents_wide = latents.astype(F32)
    noisy = ((1.0 - sigma) * latents_wide + sigma * noise.astype(F32)).astype(BF16)
    hidden = (stream.astype(F32) + dot(noisy, patch_embed_weight)).astype(BF16)
    hidden_wide = hidden.astype(F32)
    normed = (
        hidden_wide
        * lax.rsqrt(jnp.mean(hidden_wide * hidden_wide, axis=-1, keepdims=True) + 1e-06)
        * prenorm_gain_vector
    ).astype(BF16)

    message = jnp.concatenate(
        [columns_of(normed, (1 - seq) * 2 + core, quarter), noisy, latents], axis=1
    )
    received = lax.ppermute(message, "seq", to_x)
    near = received[:, :quarter]
    far = lax.ppermute(near, "head", to_core)
    other_noisy = received[:, quarter : quarter + channels]
    other_latents = received[:, quarter + channels :]

    own = columns_of(normed, seq, half_width)
    weights = (query_matrix, key_matrix, value_matrix)

    readout_half = columns_of(velocity_readout_weight, seq, half_width)
    mix_part = contract_final_axis(output_matrix, readout_half)

    def payload(q, k, v, lora, extra):
        def theirs(x):
            return columns_of(x, 1 - seq, columns)

        blocks = [
            *split_high_low(theirs(q)),
            *split_high_low(theirs(k)),
            theirs(v).astype(BF16),
            *split_high_low(lora),
            *extra,
        ]
        return jnp.concatenate(blocks, axis=1)

    def combined(q, k, v, lora, message):
        def mine(x):
            return columns_of(x, seq, columns)

        def part(index):
            return message[:, index * columns : (index + 1) * columns].astype(F32)

        rank = lora.shape[1]
        base = 5 * columns
        return (
            mine(q) + (part(0) + part(1)),
            (mine(k) + (part(2) + part(3))).astype(BF16),
            (mine(v) + part(4)).astype(BF16),
            (
                lora
                + (
                    message[:, base : base + rank].astype(F32)
                    + message[:, base + rank : base + 2 * rank].astype(F32)
                )
            ).astype(BF16),
        )

    own_parts = [dot(own, w) for w in (*weights, adapter_query_down)]
    mix_theirs = rows_of(mix_part, 1 - seq, columns)
    own_sent = payload(*own_parts, split_high_low(mix_theirs))
    own_received = lax.ppermute(own_sent, "seq", to_x)

    near_start = core * quarter
    far_start = (1 - core) * quarter

    def other_part(w):
        return dot(near, lax.dynamic_slice_in_dim(w, near_start, quarter, 0)) + dot(
            far, lax.dynamic_slice_in_dim(w, far_start, quarter, 0)
        )

    other_parts = [other_part(w) for w in (*weights, adapter_query_down)]
    other_sent = payload(*other_parts, ())
    other_received = lax.ppermute(other_sent, "seq", to_x)

    q_own, k_own, v_own, lora_own = combined(*own_parts, other_received)
    q_oth, k_oth, v_oth, lora_oth = combined(*other_parts, own_received)
    base_query = jnp.concatenate([q_own, q_oth], axis=0)
    keys = jnp.concatenate([k_own, k_oth], axis=0)
    values = jnp.concatenate([v_own, v_oth], axis=0)
    lora_hidden = jnp.concatenate([lora_own, lora_oth], axis=0)
    up = columns_of(adapter_query_up, seq, columns)
    scale = HEAD_SIZE ** (-0.5)
    queries = (base_query * scale).astype(BF16)
    fake_queries = ((base_query + dot(lora_hidden, up)) * scale).astype(BF16)

    def attend(query):
        outs = []
        for start in range(0, columns, HEAD_SIZE):
            part = slice(start, start + HEAD_SIZE)
            scores = contract_final_axis(query[:, part], keys[:, part])
            top = jnp.max(scores, axis=-1, keepdims=True)
            probs = jnp.exp(scores - top)
            mass = jnp.sum(probs, axis=-1, keepdims=True)
            outs.append((dot(probs.astype(BF16), values[:, part]) / mass).astype(BF16))
        return jnp.concatenate(outs, axis=1)

    mix_message = own_received[:, -2 * channels :].astype(F32)
    mix_full = rows_of(mix_part, seq, columns) + (
        mix_message[:, :channels] + mix_message[:, channels:]
    )
    lora_readout = contract_final_axis(adapter_output_up, velocity_readout_weight).astype(BF16)
    mix = mix_full.astype(BF16)
    fake_mix = (
        mix_full + dot(rows_of(adapter_output_down, seq, columns), lora_readout)
    ).astype(BF16)
    real = dot(attend(queries), mix)
    delta = dot(attend(fake_queries), fake_mix) - real

    base = contract_final_axis(hidden, velocity_readout_weight)
    base = jnp.where((group == 0) & (head == 0), base, 0.0)
    terms_own = jnp.concatenate([real[:tokens] + base, delta[:tokens]], axis=1)
    terms_oth = jnp.concatenate([real[tokens:], delta[tokens:]], axis=1)

    share = tokens // 2
    sent = jnp.concatenate(
        [rows_of(terms_own, 1 - core, share), rows_of(terms_oth, 1 - core, share)], axis=0
    )
    got = lax.ppermute(sent, "head", to_core)
    mine = rows_of(terms_own, core, share) + got[:share]
    theirs = rows_of(terms_oth, core, share) + got[share:]
    same = jnp.concatenate([mine, fold(theirs[:, :channels])], axis=0)
    cross = jnp.concatenate([theirs, fold(mine[:, :channels])], axis=0)
    from_x = lax.ppermute(cross, "seq", to_x)
    from_y = lax.ppermute(same, "head", to_y)
    from_xy = lax.ppermute(cross, ("seq", "head"), to_xy)
    total = (same + from_y) + (from_x + from_xy)
    stage = 1
    parts = [total] + [
        lax.ppermute(total, "group", pairs((groups,), lambda g, k=k: (g ^ k,)))
        for k in range(1, groups)
    ]
    while len(parts) > 1:
        parts = [a + b for a, b in zip(parts[::2], parts[1::2])]
    total = parts[0]

    real_own = total[:share, :channels]
    delta_own = total[:share, channels:]
    real_oth = unfold(total[share:])

    def error(latents_all, noisy_all, real_part):
        x0_real = rows_of(noisy_all, core, share).astype(F32) - sigma * real_part
        return jnp.sum(jnp.abs(rows_of(latents_all, core, share).astype(F32) - x0_real))

    local_error = error(latents, noisy, real_own) + error(other_latents, other_noisy, real_oth)
    packet = jnp.concatenate(
        [fold(delta_own), jnp.broadcast_to(local_error, (8, 2 * channels))], axis=0
    )
    answer = lax.ppermute(packet, "head", to_core)
    weight = (local_error + answer[-1, 0]) / (2 * tokens * channels)
    delta_partner = unfold(answer[: share // 2])
    first = jnp.where(core == 0, delta_own, delta_partner)
    second = jnp.where(core == 0, delta_partner, delta_own)
    return jnp.concatenate([first, second], axis=0) * (-sigma) / weight


def gathered_local(
    latents,
    noise,
    step,
    stream,
    patch_embed_weight,
    prenorm_gain_vector,
    query_matrix,
    key_matrix,
    value_matrix,
    output_matrix,
    velocity_readout_weight,
    adapter_query_down,
    adapter_query_up,
    adapter_output_down,
    adapter_output_up,
):
    tokens = latents.shape[0]
    width = query_matrix.shape[1]
    local_heads = width // HEAD_SIZE
    channels = velocity_readout_weight.shape[0]
    sigma = noise_level(step)
    noisy = (
        (1.0 - sigma) * latents.astype(F32) + sigma * noise.astype(F32)
    ).astype(BF16)
    hidden = (stream.astype(F32) + dot(noisy, patch_embed_weight)).astype(BF16)
    hidden_wide = hidden.astype(F32)
    normed = (
        hidden_wide
        * lax.rsqrt(jnp.mean(hidden_wide * hidden_wide, axis=-1, keepdims=True) + 1e-06)
        * prenorm_gain_vector
    ).astype(BF16)
    base_query, keys, values, lora_hidden = (
        dot(normed, lax.all_gather(piece, "seq", axis=0, tiled=True))
        for piece in (query_matrix, key_matrix, value_matrix, adapter_query_down)
    )
    scale = HEAD_SIZE ** (-0.5)
    lora_delta = dot(lora_hidden.astype(BF16), adapter_query_up)
    queries = (base_query * scale).astype(BF16)
    fake_queries = ((base_query + lora_delta) * scale).astype(BF16)
    both_sets = jnp.stack([queries, fake_queries]).reshape(2, tokens, local_heads, HEAD_SIZE)
    key_rows = lax.all_gather(keys.astype(BF16), "seq", axis=0, tiled=True)
    value_rows = lax.all_gather(values.astype(BF16), "seq", axis=0, tiled=True)
    key_rows = key_rows.reshape(-1, local_heads, HEAD_SIZE)
    value_rows = value_rows.reshape(-1, local_heads, HEAD_SIZE)
    scores = jnp.einsum("sthd,khd->shtk", both_sets, key_rows, preferred_element_type=F32)
    weights = jnp.exp(scores - jnp.max(scores, axis=-1, keepdims=True))
    mass = jnp.sum(weights, axis=-1)
    added = jnp.einsum(
        "shtk,khd->sthd", weights.astype(BF16), value_rows, preferred_element_type=F32
    )
    attn = (added / mass.transpose(0, 2, 1)[..., None]).astype(BF16).reshape(2, tokens, width)
    columns = output_matrix.shape[1]
    readout_part = columns_of(velocity_readout_weight, lax.axis_index("seq"), columns)
    mix_full = lax.psum(contract_final_axis(output_matrix, readout_part), "seq")
    lora_readout = contract_final_axis(adapter_output_up, velocity_readout_weight).astype(BF16)
    fake_mix = (mix_full + dot(adapter_output_down, lora_readout)).astype(BF16)
    real_sum, fake_sum = lax.psum(
        (dot(attn[0], mix_full.astype(BF16)), dot(attn[1], fake_mix)), ("group", "head")
    )
    base = contract_final_axis(hidden, velocity_readout_weight)
    noisy_wide = noisy.astype(F32)
    x0_real = noisy_wide - sigma * (base + real_sum)
    x0_fake = noisy_wide - sigma * (base + fake_sum)
    local_error = jnp.sum(jnp.abs(latents.astype(F32) - x0_real))
    weight = lax.psum(local_error, "seq") / (tokens * lax.axis_size("seq") * channels)
    return (x0_fake - x0_real) / weight


def solution(mesh):
    sizes = tuple(mesh.shape[name] for name in ("group", "seq", "head"))

    def local(*args):
        query_columns = args[6].shape[1]
        power = sizes[0] & (sizes[0] - 1) == 0
        paired = sizes[1] == 2 and sizes[2] == 4 and power
        if paired and (query_columns // HEAD_SIZE) % 2 == 0:
            return paired_local(sizes, *args)
        return gathered_local(*args)

    split = ("group", "head")
    in_specs = (
        P("seq", None),
        P("seq", None),
        P(),
        P("seq", None),
        P(),
        P(),
        P("seq", split),
        P("seq", split),
        P("seq", split),
        P(split, "seq"),
        P(),
        P("seq", None),
        P(None, split),
        P(split, None),
        P(),
    )
    return jax.shard_map(
        local, mesh=mesh, in_specs=in_specs, out_specs=P("seq", None), check_vma=False
    )
```

```python
import itertools

import jax
import jax.numpy as jnp
from jax import lax
from jax.experimental import pallas as pl
from jax.experimental.pallas import tpu as pltpu
from jax.sharding import PartitionSpec as P

HEAD_SIZE = 128
F32 = jnp.float32
BF16 = jnp.bfloat16


def contract_final_axis(left, right):
    return lax.dot_general(
        left, right, (((1,), (1,)), ((), ())), preferred_element_type=F32
    )


def dot(left, right):
    return jnp.dot(left, right, preferred_element_type=F32)


def noise_level(step):
    level = (step[0].astype(F32) + 1.0) / 1000.0
    return 5.0 * level / (1.0 + 4.0 * level)


def pairs(sizes, partner):
    def linear(coordinate):
        index = 0
        for value, size in zip(coordinate, sizes):
            index = index * size + value
        return index

    return [
        (linear(c), linear(partner(*c)))
        for c in itertools.product(*[range(n) for n in sizes])
    ]


def columns_of(x, index, count):
    return lax.dynamic_slice_in_dim(x, index * count, count, 1)


VMEM = pl.BlockSpec(memory_space=pltpu.VMEM)
SMEM = pl.BlockSpec(memory_space=pltpu.SMEM)
HBM = pl.BlockSpec(memory_space=pltpu.HBM)


def run(kernel, outs, args, specs=None, scratch=(), flops=0, limit=8 << 20, moved=None):
    shapes = [jax.ShapeDtypeStruct(shape, kind) for shape, kind in outs]
    if moved is None:
        moved = sum(a.size * a.dtype.itemsize for a in (*args, *shapes))
    return pl.pallas_call(
        kernel,
        out_shape=shapes,
        in_specs=specs or [VMEM] * len(args),
        out_specs=[VMEM] * len(shapes),
        scratch_shapes=list(scratch),
        cost_estimate=pl.CostEstimate(flops=flops, bytes_accessed=moved, transcendentals=0),
        compiler_params=pltpu.CompilerParams(vmem_limit_bytes=limit),
    )(*args)


def aligned(index, count):
    return pl.ds(pl.multiple_of(index * count, count), count)


def fold(low, high):
    lane = lax.broadcasted_iota(jnp.int32, low.shape, 1)
    return jnp.where(lane < low.shape[1] // 2, low, high)


def swap_halves(x):
    return pltpu.roll(x, x.shape[1] // 2, 1)


def high_low(x):
    high = x.astype(BF16)
    return high, (x - high.astype(F32)).astype(BF16)


def first_kernel(
    step_hbm, latents_hbm, noise_hbm, gain_hbm, stream_hbm, patch_hbm,
    message_ref, hidden_ref, inverse_ref, gap_ref, sigma_ref,
    step_s, latents_v, noise_v, gain_v, stream_v, patch_v, sems,
):
    parts, tokens, quarter = hidden_ref.shape
    channels = latents_v.shape[1]
    seq = lax.axis_index("seq")
    core = lax.axis_index("head") % 2
    small = [
        pltpu.make_async_copy(step_hbm, step_s, sems.at[0]),
        pltpu.make_async_copy(latents_hbm, latents_v, sems.at[1]),
        pltpu.make_async_copy(noise_hbm, noise_v, sems.at[2]),
    ]
    large = []
    for j in range(parts):
        span = pl.ds(j * quarter, quarter)
        large.append((
            pltpu.make_async_copy(stream_hbm.at[:, span], stream_v.at[j], sems.at[4 + 2 * j]),
            pltpu.make_async_copy(patch_hbm.at[:, span], patch_v.at[j], sems.at[5 + 2 * j]),
        ))
    gain_copy = pltpu.make_async_copy(gain_hbm, gain_v, sems.at[3])
    for copy in small:
        copy.start()
    for pair in large:
        for copy in pair:
            copy.start()
    gain_copy.start()
    for copy in small:
        copy.wait()
    level = (jnp.full((8, 128), step_s[0], jnp.int32).astype(F32) + 1.0) / 1000.0
    sigma = 5.0 * level / (1.0 + 4.0 * level)
    sigma_ref[...] = sigma
    sigma = jnp.broadcast_to(sigma[:1, :1], (tokens, channels))
    latents = latents_v[...].astype(F32)
    noisy = ((1.0 - sigma) * latents + sigma * noise_v[...].astype(F32)).astype(BF16)
    noisy_wide = noisy.astype(F32)
    gap_ref[...] = latents - noisy_wide
    message_ref[:, quarter:] = jnp.concatenate([noisy_wide, latents], axis=1).astype(BF16)
    squares = jnp.zeros((tokens, 128), F32)
    for j in range(parts):
        for copy in large[j]:
            copy.wait()
        hidden = (stream_v[j].astype(F32) + dot(noisy, patch_v[j])).astype(BF16)
        hidden_ref[j] = hidden
        wide = hidden.astype(F32)
        wide = wide * wide
        for i in range(quarter // 128):
            squares = squares + wide[:, i * 128 : (i + 1) * 128]
    mean = jnp.sum(squares, axis=1, keepdims=True) / (parts * quarter)
    inverse = lax.rsqrt(mean + 1e-06)
    inverse_ref[...] = jnp.broadcast_to(inverse, inverse_ref.shape)
    gain_copy.wait()
    target = (1 - seq) * 2 + core
    for j in range(parts):

        @pl.when(target == j)
        def _(j=j):
            gain = gain_v[j * quarter : (j + 1) * quarter][None, :]
            message_ref[:, :quarter] = (hidden_ref[j].astype(F32) * inverse * gain).astype(BF16)


def pick(index, x):
    half = x.shape[1] // 2
    return jnp.where(index == 0, x[:, :half], x[:, half:])


def partial_outputs(parts, seq, sent_ref, kept_ref):
    q, k, v, lora = parts
    columns = q.shape[1] // 2
    blocks = [*high_low(pick(1 - seq, q)), *high_low(pick(1 - seq, k))]
    blocks += [pick(1 - seq, v).astype(BF16), *high_low(lora)]
    for i, block in enumerate(blocks):
        sent_ref[:, i * columns : (i + 1) * columns] = block
    for i, block in enumerate((pick(seq, q), pick(seq, k), pick(seq, v), lora)):
        kept_ref[:, i * columns : (i + 1) * columns] = block


def own_kernel(
    hidden_ref, inverse_ref, gain_ref, q_ref, k_ref, v_ref, down_ref, output_ref, readout_ref,
    sent_ref, kept_ref, mix_ref, normed_v, mix_v,
):
    _, tokens, quarter = hidden_ref.shape
    seq = lax.axis_index("seq")
    inverse = inverse_ref[:, :1]
    for i in range(2):
        gain = gain_ref[pl.ds(2 * seq + i, 1), :]
        hidden = hidden_ref[2 * seq + i].astype(F32)
        normed_v[:, i * quarter : (i + 1) * quarter] = (hidden * inverse * gain).astype(BF16)
    normed = normed_v[...]
    parts = [dot(normed, w[...]) for w in (q_ref, k_ref, v_ref, down_ref)]
    partial_outputs(parts, seq, sent_ref, kept_ref)
    half_width = 2 * quarter
    readout = readout_ref[:, aligned(seq, half_width)]
    mix_v[...] = contract_final_axis(output_ref[...], readout)
    rows, channels = mix_ref.shape
    theirs = mix_v[aligned(1 - seq, rows), :]
    high = theirs.astype(BF16).astype(F32)
    both = jnp.concatenate([high, theirs - high], axis=1)
    sent_ref[:, -2 * channels :] = both.astype(BF16)
    mix_ref[...] = mix_v[aligned(seq, rows), :]


def side_kernel(hidden_ref, up_ref, readout_ref, readout_of_up_ref, base_ref):
    parts, tokens, quarter = hidden_ref.shape
    readout_of_up_ref[...] = contract_final_axis(up_ref[...], readout_ref[...]).astype(BF16)
    base = jnp.zeros(base_ref.shape, F32)
    for j in range(parts):
        base += contract_final_axis(
            hidden_ref[j], readout_ref[:, j * quarter : (j + 1) * quarter]
        )
    once = (lax.axis_index("group") == 0) & (lax.axis_index("head") == 0)
    base_ref[...] = jnp.where(once, base, 0.0)


def other_kernel(near_ref, far_ref, q_ref, k_ref, v_ref, down_ref, sent_ref, kept_ref):
    quarter = q_ref.shape[0] // 2
    core = lax.axis_index("head") % 2
    near = near_ref[:, :quarter]
    far = far_ref[:, :quarter]
    parts = [
        dot(near, w[aligned(core, quarter), :]) + dot(far, w[aligned(1 - core, quarter), :])
        for w in (q_ref, k_ref, v_ref, down_ref)
    ]
    partial_outputs(parts, lax.axis_index("seq"), sent_ref, kept_ref)


def finish(kept_ref, got_ref, up):
    tokens = kept_ref.shape[0]
    columns = up.shape[1]

    def got(i):
        return got_ref[:, i * columns : (i + 1) * columns].astype(F32)

    def kept(i):
        return kept_ref[:, i * columns : (i + 1) * columns]

    scale = HEAD_SIZE ** (-0.5)
    base = kept(0) + (got(0) + got(1))
    lora = (kept(3) + (got(5) + got(6))).astype(BF16)
    return (
        (base * scale).astype(BF16),
        ((base + dot(lora, up)) * scale).astype(BF16),
        (kept(1) + (got(2) + got(3))).astype(BF16),
        (kept(2) + got(4)).astype(BF16),
    )


def half_kernel(
    kept_ref, got_ref, up_ref, mix_ref, down_ref, readout_of_up_ref, near_ref,
    set_ref, mixes_ref, gap_ref,
):
    seq = lax.axis_index("seq")
    rows, channels = mix_ref.shape
    up = up_ref[:, aligned(seq, rows)]
    for i, block in enumerate(finish(kept_ref, got_ref, up)):
        set_ref[i] = block
    got = got_ref[:, -2 * channels :].astype(F32)
    mix_full = mix_ref[...] + (got[:, :channels] + swap_halves(got)[:, :channels])
    low_rank = dot(down_ref[aligned(seq, rows), :], readout_of_up_ref[...])
    mix = mix_full.astype(BF16).astype(F32)
    fake = (mix_full + low_rank).astype(BF16).astype(F32)
    mixes_ref[0] = jnp.concatenate([mix, -mix], axis=1).astype(BF16)
    mixes_ref[1] = jnp.concatenate([jnp.zeros_like(fake), fake], axis=1).astype(BF16)
    pair = near_ref[:, -2 * channels :].astype(F32)
    gap_ref[...] = (swap_halves(pair) - pair)[:, :channels]


def attention_kernel(
    kept_ref, got_ref, up_ref, set_ref, mixes_ref, base_ref,
    sent_ref, stay_ref, sets_v, terms_v,
):
    seq = lax.axis_index("seq")
    core = lax.axis_index("head") % 2
    tokens, channels = base_ref.shape
    columns = set_ref.shape[2]
    up = up_ref[:, aligned(seq, columns)]
    for i, block in enumerate(finish(kept_ref, got_ref, up)):
        sets_v[i, :tokens] = block
        sets_v[i, tokens:] = set_ref[i]
    terms = jnp.zeros(terms_v.shape, F32)
    for start in range(0, columns, HEAD_SIZE):
        span = slice(start, start + HEAD_SIZE)
        keys, values = sets_v[2, :, span], sets_v[3, :, span]
        for kind in range(2):
            scores = contract_final_axis(sets_v[kind, :, span], keys)
            top = jnp.max(scores, axis=1, keepdims=True)
            probs = jnp.exp(scores - top)
            mass = jnp.sum(probs, axis=1, keepdims=True)
            attn = (dot(probs.astype(BF16), values) / mass).astype(BF16)
            terms = terms + dot(attn, mixes_ref[kind, span, :])
    terms_v[...] = terms
    terms_v[:tokens, :channels] = terms[:tokens, :channels] + base_ref[...]
    share = tokens // 2
    sent_ref[:share] = terms_v[aligned(1 - core, share), :]
    sent_ref[share:] = terms_v[aligned(3 - core, share), :]
    stay_ref[:share] = terms_v[aligned(core, share), :]
    stay_ref[share:] = terms_v[aligned(2 + core, share), :]


def pack_kernel(stay_ref, got_ref, same_ref, cross_ref):
    share = stay_ref.shape[0] // 2
    mine = stay_ref[:share] + got_ref[:share]
    theirs = stay_ref[share:] + got_ref[share:]
    half = share // 2
    same_ref[:share] = mine
    same_ref[share:] = fold(theirs[:half], swap_halves(theirs[half:]))
    cross_ref[:share] = theirs
    cross_ref[share:] = fold(mine[:half], swap_halves(mine[half:]))


def error_kernel(*refs):
    *parts, gap_own_ref, gap_other_ref, sigma_ref, packet_ref = refs
    parts = [ref[...] for ref in parts]
    while len(parts) > 1:
        parts = [a + b for a, b in zip(parts[::2], parts[1::2])]
    total = parts[0]
    core = lax.axis_index("head") % 2
    tokens, channels = gap_own_ref.shape
    share = tokens // 2
    half = share // 2
    sigma = sigma_ref[:1, :1]
    own = total[:share]
    gap = gap_other_ref[aligned(core, share), :]
    folded = total[share:]
    error = jnp.abs(gap_own_ref[aligned(core, share), :] + sigma * own[:, :channels])
    low = jnp.abs(gap[:half] + sigma * folded[:, :channels])
    high = jnp.abs(gap[half:] + sigma * swap_halves(folded)[:, :channels])
    error = error[:half] + error[half:] + low + high
    packet_ref[:half] = fold(swap_halves(own[:half]), own[half:])
    packet_ref[half:] = jnp.full((8, 2 * channels), jnp.sum(error), F32)


def last_kernel(mine_ref, theirs_ref, sigma_ref, out_ref):
    core = lax.axis_index("head") % 2
    tokens, channels = out_ref.shape
    share = tokens // 2
    half = share // 2
    weight = (mine_ref[half:] + theirs_ref[half:]) / (2 * tokens * channels)
    factor = (-sigma_ref[...] / weight)[:1, :1]
    for ref, index in ((mine_ref, core), (theirs_ref, 1 - core)):
        packet = ref[:half] * factor
        both = jnp.concatenate([packet, swap_halves(packet)], axis=0)
        out_ref[aligned(index, share), :] = both[:, :channels]


def paired_local(
    sizes,
    latents,
    noise,
    step,
    stream,
    patch_embed_weight,
    prenorm_gain_vector,
    query_matrix,
    key_matrix,
    value_matrix,
    output_matrix,
    velocity_readout_weight,
    adapter_query_down,
    adapter_query_up,
    adapter_output_down,
    adapter_output_up,
):
    groups, _, heads = sizes
    tokens, channels = latents.shape
    half_width, local_columns = query_matrix.shape
    quarter = half_width // 2
    columns = local_columns // 2
    rank = adapter_query_down.shape[1]
    share = tokens // 2
    to_x = pairs((2,), lambda s: (s ^ 1,))
    to_core = pairs((heads,), lambda h: (h ^ 1,))
    to_y = pairs((heads,), lambda h: (h ^ 2,))
    to_xy = pairs((2, heads), lambda s, h: (s ^ 1, h ^ 2))
    weights = (query_matrix, key_matrix, value_matrix, adapter_query_down)
    partial_flops = 2 * tokens * half_width * (3 * local_columns + rank)

    copies = 4 + 2 * 4
    message, hidden, inverse, gap_own, sigma = run(
        first_kernel,
        [
            ((tokens, quarter + 2 * channels), BF16),
            ((4, tokens, quarter), BF16),
            ((tokens, 128), F32),
            ((tokens, channels), F32),
            ((8, 128), F32),
        ],
        (step, latents, noise, prenorm_gain_vector, stream, patch_embed_weight),
        [HBM] * 6,
        [
            pltpu.SMEM((1,), jnp.int32),
            pltpu.VMEM((tokens, channels), BF16),
            pltpu.VMEM((tokens, channels), BF16),
            pltpu.VMEM((4 * quarter,), F32),
            pltpu.VMEM((4, tokens, quarter), BF16),
            pltpu.VMEM((4, channels, quarter), BF16),
            pltpu.SemaphoreType.DMA((copies,)),
        ],
    )
    near = lax.ppermute(message, "seq", to_x)
    own_sent, own_kept, mix_part = run(
        own_kernel,
        [
            ((tokens, 7 * columns + 2 * channels), BF16),
            ((tokens, 4 * columns), F32),
            ((columns, channels), F32),
        ],
        (
            hidden, inverse, prenorm_gain_vector.reshape(4, quarter), *weights,
            output_matrix, velocity_readout_weight,
        ),
        scratch=[
            pltpu.VMEM((tokens, half_width), BF16),
            pltpu.VMEM((local_columns, channels), F32),
        ],
        flops=partial_flops,
    )
    own_got = lax.ppermute(own_sent, "seq", to_x)
    readout_of_up, base = run(
        side_kernel,
        [((rank, channels), BF16), ((tokens, channels), F32)],
        (hidden, adapter_output_up, velocity_readout_weight),
        flops=8 * tokens * half_width * channels,
    )
    far = lax.ppermute(near, "head", to_core)
    other_sent, other_kept = run(
        other_kernel,
        [((tokens, 7 * columns), BF16), ((tokens, 4 * columns), F32)],
        (near, far, *weights),
        flops=partial_flops,
    )
    other_got = lax.ppermute(other_sent, "seq", to_x)
    half_set, mixes, gap_other = run(
        half_kernel,
        [
            ((4, tokens, columns), BF16),
            ((2, columns, 2 * channels), BF16),
            ((tokens, channels), F32),
        ],
        (
            other_kept, own_got, adapter_query_up, mix_part,
            adapter_output_down, readout_of_up, near,
        ),
    )
    sent, stay = run(
        attention_kernel,
        [((tokens, 2 * channels), F32)] * 2,
        (own_kept, other_got, adapter_query_up, half_set, mixes, base),
        scratch=[
            pltpu.VMEM((4, 2 * tokens, columns), BF16),
            pltpu.VMEM((2 * tokens, 2 * channels), F32),
        ],
    )

    got = lax.ppermute(sent, "head", to_core)
    packed = ((share + share // 2, 2 * channels), F32)
    same, cross = run(pack_kernel, [packed, packed], (stay, got))
    from_x = lax.ppermute(cross, "seq", to_x)
    from_y = lax.ppermute(same, "head", to_y)
    from_xy = lax.ppermute(cross, ("seq", "head"), to_xy)
    total = (same + from_y) + (from_x + from_xy)
    totals = [total] + [
        lax.ppermute(total, "group", pairs((groups,), lambda g, k=k: (g ^ k,)))
        for k in range(1, groups)
    ]
    (packet,) = run(
        error_kernel,
        [((share // 2 + 8, 2 * channels), F32)],
        (*totals, gap_own, gap_other, sigma),
    )
    answer = lax.ppermute(packet, "head", to_core)
    (out,) = run(last_kernel, [((tokens, channels), F32)], (packet, answer, sigma))
    return out


def gathered_local(
    latents,
    noise,
    step,
    stream,
    patch_embed_weight,
    prenorm_gain_vector,
    query_matrix,
    key_matrix,
    value_matrix,
    output_matrix,
    velocity_readout_weight,
    adapter_query_down,
    adapter_query_up,
    adapter_output_down,
    adapter_output_up,
):
    tokens = latents.shape[0]
    width = query_matrix.shape[1]
    local_heads = width // HEAD_SIZE
    channels = velocity_readout_weight.shape[0]
    sigma = noise_level(step)
    noisy = (
        (1.0 - sigma) * latents.astype(F32) + sigma * noise.astype(F32)
    ).astype(BF16)
    hidden = (stream.astype(F32) + dot(noisy, patch_embed_weight)).astype(BF16)
    hidden_wide = hidden.astype(F32)
    normed = (
        hidden_wide
        * lax.rsqrt(jnp.mean(hidden_wide * hidden_wide, axis=-1, keepdims=True) + 1e-06)
        * prenorm_gain_vector
    ).astype(BF16)
    base_query, keys, values, lora_hidden = (
        dot(normed, lax.all_gather(piece, "seq", axis=0, tiled=True))
        for piece in (query_matrix, key_matrix, value_matrix, adapter_query_down)
    )
    scale = HEAD_SIZE ** (-0.5)
    lora_delta = dot(lora_hidden.astype(BF16), adapter_query_up)
    queries = (base_query * scale).astype(BF16)
    fake_queries = ((base_query + lora_delta) * scale).astype(BF16)
    both_sets = jnp.stack([queries, fake_queries]).reshape(2, tokens, local_heads, HEAD_SIZE)
    key_rows = lax.all_gather(keys.astype(BF16), "seq", axis=0, tiled=True)
    value_rows = lax.all_gather(values.astype(BF16), "seq", axis=0, tiled=True)
    key_rows = key_rows.reshape(-1, local_heads, HEAD_SIZE)
    value_rows = value_rows.reshape(-1, local_heads, HEAD_SIZE)
    scores = jnp.einsum("sthd,khd->shtk", both_sets, key_rows, preferred_element_type=F32)
    weights = jnp.exp(scores - jnp.max(scores, axis=-1, keepdims=True))
    mass = jnp.sum(weights, axis=-1)
    added = jnp.einsum(
        "shtk,khd->sthd", weights.astype(BF16), value_rows, preferred_element_type=F32
    )
    attn = (added / mass.transpose(0, 2, 1)[..., None]).astype(BF16).reshape(2, tokens, width)
    columns = output_matrix.shape[1]
    readout_part = columns_of(velocity_readout_weight, lax.axis_index("seq"), columns)
    mix_full = lax.psum(contract_final_axis(output_matrix, readout_part), "seq")
    lora_readout = contract_final_axis(adapter_output_up, velocity_readout_weight).astype(BF16)
    fake_mix = (mix_full + dot(adapter_output_down, lora_readout)).astype(BF16)
    real_sum, fake_sum = lax.psum(
        (dot(attn[0], mix_full.astype(BF16)), dot(attn[1], fake_mix)), ("group", "head")
    )
    base = contract_final_axis(hidden, velocity_readout_weight)
    noisy_wide = noisy.astype(F32)
    x0_real = noisy_wide - sigma * (base + real_sum)
    x0_fake = noisy_wide - sigma * (base + fake_sum)
    local_error = jnp.sum(jnp.abs(latents.astype(F32) - x0_real))
    weight = lax.psum(local_error, "seq") / (tokens * lax.axis_size("seq") * channels)
    return (x0_fake - x0_real) / weight


def solution(mesh):
    sizes = tuple(mesh.shape[name] for name in ("group", "seq", "head"))

    def local(*args):
        query_columns = args[6].shape[1]
        power = sizes[0] & (sizes[0] - 1) == 0
        paired = sizes[1] == 2 and sizes[2] == 4 and power
        if paired and (query_columns // HEAD_SIZE) % 2 == 0:
            return paired_local(sizes, *args)
        return gathered_local(*args)

    split = ("group", "head")
    in_specs = (
        P("seq", None),
        P("seq", None),
        P(),
        P("seq", None),
        P(),
        P(),
        P("seq", split),
        P("seq", split),
        P("seq", split),
        P(split, "seq"),
        P(),
        P("seq", None),
        P(None, split),
        P(split, None),
        P(),
    )
    return jax.shard_map(
        local, mesh=mesh, in_specs=in_specs, out_specs=P("seq", None), check_vma=False
    )
```

```python
import itertools

import jax
import jax.numpy as jnp
from jax import lax
from jax.experimental import pallas as pl
from jax.experimental.pallas import tpu as pltpu
from jax.sharding import PartitionSpec as P


HEAD_SIZE = 128
F32 = jnp.float32
BF16 = jnp.bfloat16


def contract_final_axis(left, right):
    return lax.dot_general(
        left, right, (((1,), (1,)), ((), ())), preferred_element_type=F32
    )


def dot(left, right):
    return jnp.dot(left, right, preferred_element_type=F32)


def noise_level(step):
    level = (step[0].astype(F32) + 1.0) / 1000.0
    return 5.0 * level / (1.0 + 4.0 * level)


def pairs(sizes, partner):
    def linear(coordinate):
        index = 0
        for value, size in zip(coordinate, sizes):
            index = index * size + value
        return index

    return [
        (linear(c), linear(partner(*c)))
        for c in itertools.product(*[range(n) for n in sizes])
    ]


def columns_of(x, index, count):
    return lax.dynamic_slice_in_dim(x, index * count, count, 1)


VMEM = pl.BlockSpec(memory_space=pltpu.VMEM)
SMEM = pl.BlockSpec(memory_space=pltpu.SMEM)
HBM = pl.BlockSpec(memory_space=pltpu.HBM)


def run(kernel, outs, args, specs=None, scratch=(), flops=0, limit=8 << 20, moved=None):
    shapes = [jax.ShapeDtypeStruct(shape, kind) for shape, kind in outs]
    if moved is None:
        moved = sum(a.size * a.dtype.itemsize for a in (*args, *shapes))
    return pl.pallas_call(
        kernel,
        out_shape=shapes,
        in_specs=specs or [VMEM] * len(args),
        out_specs=[VMEM] * len(shapes),
        scratch_shapes=list(scratch),
        cost_estimate=pl.CostEstimate(flops=flops, bytes_accessed=moved, transcendentals=0),
        compiler_params=pltpu.CompilerParams(vmem_limit_bytes=limit),
    )(*args)


def aligned(index, count):
    return pl.ds(pl.multiple_of(index * count, count), count)


def fold(low, high):
    lane = lax.broadcasted_iota(jnp.int32, low.shape, 1)
    return jnp.where(lane < low.shape[1] // 2, low, high)


def swap_halves(x):
    return pltpu.roll(x, x.shape[1] // 2, 1)


def high_low(x):
    high = x.astype(BF16)
    return high, (x - high.astype(F32)).astype(BF16)


def first_kernel(
    step_ref, latents_hbm, noise_hbm, gain_hbm, stream_hbm, patch_hbm,
    message_ref, hidden_ref, inverse_ref, gap_ref,
    latents_v, noise_v, gain_v, stream_v, patch_v, sems,
):
    parts, tokens, quarter = hidden_ref.shape
    seq = lax.axis_index("seq")
    core = lax.axis_index("head") % 2
    small = [
        pltpu.make_async_copy(latents_hbm, latents_v, sems.at[0]),
        pltpu.make_async_copy(noise_hbm, noise_v, sems.at[1]),
    ]
    large = []
    for j in range(parts):
        span = pl.ds(j * quarter, quarter)
        large.append((
            pltpu.make_async_copy(stream_hbm.at[:, span], stream_v.at[j], sems.at[3 + 2 * j]),
            pltpu.make_async_copy(patch_hbm.at[:, span], patch_v.at[j], sems.at[4 + 2 * j]),
        ))
    gain_copy = pltpu.make_async_copy(gain_hbm, gain_v, sems.at[2])
    for copy in small:
        copy.start()
    for pair in large:
        for copy in pair:
            copy.start()
    gain_copy.start()
    for copy in small:
        copy.wait()
    level = (jnp.full((8, 128), step_ref[0], jnp.int32).astype(F32) + 1.0) / 1000.0
    sigma = (5.0 * level / (1.0 + 4.0 * level))[:1, :1]
    latents = latents_v[...].astype(F32)
    noisy = ((1.0 - sigma) * latents + sigma * noise_v[...].astype(F32)).astype(BF16)
    gap_ref[...] = (latents - noisy.astype(F32)) / sigma
    squares = jnp.zeros((tokens, 128), F32)
    for j in range(parts):
        for copy in large[j]:
            copy.wait()
        embedded = lax.dot_general(
            noisy, patch_v[j], (((0,), (0,)), ((), ())), preferred_element_type=F32
        )
        hidden = (stream_v[j].astype(F32) + embedded).astype(BF16)
        hidden_ref[j] = hidden
        wide = hidden.astype(F32)
        wide = wide * wide
        for i in range(quarter // 128):
            squares = squares + wide[:, i * 128 : (i + 1) * 128]
    mean = jnp.sum(squares, axis=1, keepdims=True) / (parts * quarter)
    inverse = lax.rsqrt(mean + 1e-06)
    inverse_ref[...] = jnp.broadcast_to(inverse, inverse_ref.shape)
    gain_copy.wait()
    target = (1 - seq) * 2 + core
    for j in range(parts):

        @pl.when(target == j)
        def _(j=j):
            gain = gain_v[j * quarter : (j + 1) * quarter][None, :]
            message_ref[...] = (hidden_ref[j].astype(F32) * inverse * gain).astype(BF16)


def pick(index, x):
    half = x.shape[1] // 2
    return jnp.where(index == 0, x[:, :half], x[:, half:])


def partial_outputs(parts, seq, sent_ref, kept_ref):
    q, k, v, lora = parts
    columns = q.shape[1] // 2
    blocks = [*high_low(pick(1 - seq, q)), *high_low(pick(1 - seq, k))]
    blocks += [pick(1 - seq, v).astype(BF16), *high_low(lora)]
    for i, block in enumerate(blocks):
        sent_ref[:, i * columns : (i + 1) * columns] = block
    for i, block in enumerate((pick(seq, q), pick(seq, k), pick(seq, v), lora)):
        kept_ref[:, i * columns : (i + 1) * columns] = block


def own_kernel(
    hidden_ref, inverse_ref, gain_ref, q_ref, k_ref, v_ref, down_ref, output_ref, readout_ref,
    sent_ref, kept_ref, mix_ref, normed_v, mix_v,
):
    _, _, quarter = hidden_ref.shape
    seq = lax.axis_index("seq")
    inverse = inverse_ref[:, :1]
    for i in range(2):
        gain = gain_ref[pl.ds(2 * seq + i, 1), :]
        hidden = hidden_ref[2 * seq + i].astype(F32)
        normed_v[:, i * quarter : (i + 1) * quarter] = (hidden * inverse * gain).astype(BF16)
    normed = normed_v[...]
    parts = [dot(normed, w[...]) for w in (q_ref, k_ref, v_ref, down_ref)]
    partial_outputs(parts, seq, sent_ref, kept_ref)
    half_width = 2 * quarter
    readout = readout_ref[:, aligned(seq, half_width)]
    mix_v[...] = contract_final_axis(output_ref[...], readout)
    rows, channels = mix_ref.shape
    theirs = mix_v[aligned(1 - seq, rows), :]
    high = theirs.astype(BF16).astype(F32)
    both = jnp.concatenate([high, theirs - high], axis=1)
    sent_ref[:, -2 * channels :] = both.astype(BF16)
    mix_ref[...] = mix_v[aligned(seq, rows), :]


def side_kernel(hidden_ref, up_ref, readout_ref, gap_ref, readout_of_up_ref, base_ref):
    parts, _, quarter = hidden_ref.shape
    readout_of_up_ref[...] = contract_final_axis(up_ref[...], readout_ref[...]).astype(BF16)
    base = gap_ref[...]
    for j in range(parts):
        base += contract_final_axis(
            readout_ref[:, j * quarter : (j + 1) * quarter], hidden_ref[j]
        )
    once = (lax.axis_index("group") == 0) & (lax.axis_index("head") == 0)
    base_ref[...] = jnp.where(once, base, 0.0).T


def other_kernel(near_ref, far_ref, q_ref, k_ref, v_ref, down_ref, sent_ref, kept_ref):
    quarter = q_ref.shape[0] // 2
    core = lax.axis_index("head") % 2
    near = near_ref[...]
    far = far_ref[...]
    parts = [
        dot(near, w[aligned(core, quarter), :]) + dot(far, w[aligned(1 - core, quarter), :])
        for w in (q_ref, k_ref, v_ref, down_ref)
    ]
    partial_outputs(parts, lax.axis_index("seq"), sent_ref, kept_ref)


def finish(kept_ref, got_ref, up):
    columns = up.shape[1]

    def got(i):
        return got_ref[:, i * columns : (i + 1) * columns].astype(F32)

    def kept(i):
        return kept_ref[:, i * columns : (i + 1) * columns]

    scale = HEAD_SIZE ** (-0.5)
    base = kept(0) + (got(0) + got(1))
    lora = (kept(3) + (got(5) + got(6))).astype(BF16)
    return (
        (base * scale).astype(BF16),
        ((base + dot(lora, up)) * scale).astype(BF16),
        (kept(1) + (got(2) + got(3))).astype(BF16),
        (kept(2) + got(4)).astype(BF16),
    )


def half_kernel(
    kept_ref, got_ref, up_ref, mix_ref, down_ref, readout_of_up_ref,
    set_ref, mixes_ref,
):
    seq = lax.axis_index("seq")
    rows, channels = mix_ref.shape
    up = up_ref[:, aligned(seq, rows)]
    for i, block in enumerate(finish(kept_ref, got_ref, up)):
        set_ref[i] = block
    got = got_ref[:, -2 * channels :].astype(F32)
    mix_full = mix_ref[...] + (got[:, :channels] + swap_halves(got)[:, :channels])
    low_rank = dot(down_ref[aligned(seq, rows), :], readout_of_up_ref[...])
    mix = mix_full.astype(BF16).astype(F32)
    fake = (mix_full + low_rank).astype(BF16).astype(F32)
    mixes_ref[0] = jnp.concatenate([mix, -mix], axis=1).astype(BF16)
    mixes_ref[1] = jnp.concatenate([jnp.zeros_like(fake), fake], axis=1).astype(BF16)


def attention_kernel(
    kept_ref, got_ref, up_ref, set_ref, mixes_ref, base_ref,
    sent_ref, stay_ref, sets_v, terms_v,
):
    seq = lax.axis_index("seq")
    core = lax.axis_index("head") % 2
    tokens, channels = base_ref.shape
    columns = set_ref.shape[2]
    up = up_ref[:, aligned(seq, columns)]
    for i, block in enumerate(finish(kept_ref, got_ref, up)):
        sets_v[i, :tokens] = block
        sets_v[i, tokens:] = set_ref[i]
    terms = jnp.zeros(terms_v.shape, F32)
    for start in range(0, columns, HEAD_SIZE):
        span = slice(start, start + HEAD_SIZE)
        keys, values = sets_v[2, :, span], sets_v[3, :, span]
        for kind in range(2):
            scores = contract_final_axis(sets_v[kind, :, span], keys)
            top = jnp.max(scores, axis=1, keepdims=True)
            probs = jnp.exp(scores - top)
            mass = jnp.sum(probs, axis=1, keepdims=True)
            attn = (dot(probs.astype(BF16), values) / mass).astype(BF16)
            terms = terms + dot(attn, mixes_ref[kind, span, :])
    terms_v[...] = terms
    terms_v[:tokens, :channels] = terms[:tokens, :channels] + base_ref[...]
    share = tokens // 2
    sent_ref[:share] = terms_v[aligned(1 - core, share), :]
    sent_ref[share:] = terms_v[aligned(3 - core, share), :]
    stay_ref[:share] = terms_v[aligned(core, share), :]
    stay_ref[share:] = terms_v[aligned(2 + core, share), :]


def pack_kernel(stay_ref, got_ref, same_ref, cross_ref):
    share = stay_ref.shape[0] // 2
    mine = stay_ref[:share] + got_ref[:share]
    theirs = stay_ref[share:] + got_ref[share:]
    half = share // 2
    same_ref[:share] = mine.astype(BF16)
    same_ref[share:] = fold(theirs[:half], swap_halves(theirs[half:])).astype(BF16)
    cross_ref[:share] = theirs.astype(BF16)
    cross_ref[share:] = fold(mine[:half], swap_halves(mine[half:])).astype(BF16)


def error_kernel(*refs):
    *parts, packet_ref = refs
    parts = [ref[...].astype(F32) for ref in parts]
    while len(parts) > 1:
        parts = [a + b for a, b in zip(parts[::2], parts[1::2])]
    total = parts[0]
    half = packet_ref.shape[0] - 8
    share = 2 * half
    own = jnp.abs(total[:half]) + jnp.abs(total[half:share])
    own = fold(own, jnp.zeros_like(own)) + jnp.abs(total[share:])
    packet_ref[:half] = fold(swap_halves(total[:half]), total[half:share])
    packet_ref[half:] = jnp.full((8, packet_ref.shape[1]), jnp.sum(own), F32)


def last_kernel(mine_ref, theirs_ref, out_ref, both_v):
    core = lax.axis_index("head") % 2
    channels, tokens = out_ref.shape
    share = tokens // 2
    half = share // 2
    weight = (mine_ref[half:] + theirs_ref[half:]) / (2 * tokens * channels)
    weight = weight[:1, :1]
    for ref, index in ((mine_ref, core), (theirs_ref, 1 - core)):
        packet = -ref[:half] / weight
        start = pl.multiple_of(index * share, share)
        both_v[pl.ds(start, half)] = packet
        both_v[pl.ds(start + half, half)] = swap_halves(packet)
    out_ref[...] = both_v[...].T[:channels]


def paired_local(
    sizes,
    latents,
    noise,
    step,
    stream,
    patch_embed_weight,
    prenorm_gain_vector,
    query_matrix,
    key_matrix,
    value_matrix,
    output_matrix,
    velocity_readout_weight,
    adapter_query_down,
    adapter_query_up,
    adapter_output_down,
    adapter_output_up,
):
    groups, _, heads = sizes
    tokens, channels = latents.shape
    half_width, local_columns = query_matrix.shape
    quarter = half_width // 2
    columns = local_columns // 2
    rank = adapter_query_down.shape[1]
    share = tokens // 2
    to_x = pairs((2,), lambda s: (s ^ 1,))
    to_core = pairs((heads,), lambda h: (h ^ 1,))
    to_y = pairs((heads,), lambda h: (h ^ 2,))
    to_xy = pairs((2, heads), lambda s, h: (s ^ 1, h ^ 2))
    weights = (query_matrix, key_matrix, value_matrix, adapter_query_down)
    partial_flops = 2 * tokens * half_width * (3 * local_columns + rank)

    copies = 3 + 2 * 4
    inputs = (step, latents.T, noise.T, prenorm_gain_vector, stream, patch_embed_weight)
    message, hidden, inverse, gap = run(
        first_kernel,
        [
            ((tokens, quarter), BF16),
            ((4, tokens, quarter), BF16),
            ((tokens, 128), F32),
            ((channels, tokens), F32),
        ],
        [inputs[0]]
        + [pltpu.with_memory_space_constraint(x, pltpu.HBM) for x in inputs[1:]],
        [SMEM] + [HBM] * 5,
        [
            pltpu.VMEM((channels, tokens), BF16),
            pltpu.VMEM((channels, tokens), BF16),
            pltpu.VMEM((4 * quarter,), F32),
            pltpu.VMEM((4, tokens, quarter), BF16),
            pltpu.VMEM((4, channels, quarter), BF16),
            pltpu.SemaphoreType.DMA((copies,)),
        ],
    )
    near = lax.ppermute(message, "seq", to_x)
    own_sent, own_kept, mix_part = run(
        own_kernel,
        [
            ((tokens, 7 * columns + 2 * channels), BF16),
            ((tokens, 4 * columns), F32),
            ((columns, channels), F32),
        ],
        (
            hidden, inverse, prenorm_gain_vector.reshape(4, quarter), *weights,
            output_matrix, velocity_readout_weight,
        ),
        scratch=[
            pltpu.VMEM((tokens, half_width), BF16),
            pltpu.VMEM((local_columns, channels), F32),
        ],
        flops=partial_flops,
    )
    own_got = lax.ppermute(own_sent, "seq", to_x)
    readout_of_up, base = run(
        side_kernel,
        [((rank, channels), BF16), ((tokens, channels), F32)],
        (hidden, adapter_output_up, velocity_readout_weight, gap),
        flops=8 * tokens * half_width * channels,
    )
    far = lax.ppermute(near, "head", to_core)
    other_sent, other_kept = run(
        other_kernel,
        [((tokens, 7 * columns), BF16), ((tokens, 4 * columns), F32)],
        (near, far, *weights),
        flops=partial_flops,
    )
    other_got = lax.ppermute(other_sent, "seq", to_x)
    half_set, mixes = run(
        half_kernel,
        [((4, tokens, columns), BF16), ((2, columns, 2 * channels), BF16)],
        (
            other_kept, own_got, adapter_query_up, mix_part,
            adapter_output_down, readout_of_up,
        ),
    )
    sent, stay = run(
        attention_kernel,
        [((tokens, 2 * channels), F32)] * 2,
        (own_kept, other_got, adapter_query_up, half_set, mixes, base),
        scratch=[
            pltpu.VMEM((4, 2 * tokens, columns), BF16),
            pltpu.VMEM((2 * tokens, 2 * channels), F32),
        ],
    )

    got = lax.ppermute(sent, "head", to_core)
    packed = ((share + share // 2, 2 * channels), BF16)
    same, cross = run(pack_kernel, [packed, packed], (stay, got))
    from_x = lax.ppermute(cross, "seq", to_x)
    from_y = lax.ppermute(same, "head", to_y)
    from_xy = lax.ppermute(cross, ("seq", "head"), to_xy)
    total = (same.astype(F32) + from_y.astype(F32)) + (
        from_x.astype(F32) + from_xy.astype(F32)
    )
    total = total.astype(BF16)
    totals = [total] + [
        lax.ppermute(total, "group", pairs((groups,), lambda g, k=k: (g ^ k,)))
        for k in range(1, groups)
    ]
    (packet,) = run(error_kernel, [((share // 2 + 8, 2 * channels), F32)], totals)
    answer = lax.ppermute(packet, "head", to_core)
    (out,) = run(
        last_kernel,
        [((channels, tokens), F32)],
        (packet, answer),
        scratch=[pltpu.VMEM((tokens, 2 * channels), F32)],
    )
    return out.T


def gathered_local(
    latents,
    noise,
    step,
    stream,
    patch_embed_weight,
    prenorm_gain_vector,
    query_matrix,
    key_matrix,
    value_matrix,
    output_matrix,
    velocity_readout_weight,
    adapter_query_down,
    adapter_query_up,
    adapter_output_down,
    adapter_output_up,
):
    tokens = latents.shape[0]
    width = query_matrix.shape[1]
    local_heads = width // HEAD_SIZE
    channels = velocity_readout_weight.shape[0]
    sigma = noise_level(step)
    noisy = (
        (1.0 - sigma) * latents.astype(F32) + sigma * noise.astype(F32)
    ).astype(BF16)
    hidden = (stream.astype(F32) + dot(noisy, patch_embed_weight)).astype(BF16)
    hidden_wide = hidden.astype(F32)
    normed = (
        hidden_wide
        * lax.rsqrt(jnp.mean(hidden_wide * hidden_wide, axis=-1, keepdims=True) + 1e-06)
        * prenorm_gain_vector
    ).astype(BF16)
    base_query, keys, values, lora_hidden = (
        dot(normed, lax.all_gather(piece, "seq", axis=0, tiled=True))
        for piece in (query_matrix, key_matrix, value_matrix, adapter_query_down)
    )
    scale = HEAD_SIZE ** (-0.5)
    lora_delta = dot(lora_hidden.astype(BF16), adapter_query_up)
    queries = (base_query * scale).astype(BF16)
    fake_queries = ((base_query + lora_delta) * scale).astype(BF16)
    both_sets = jnp.stack([queries, fake_queries]).reshape(2, tokens, local_heads, HEAD_SIZE)
    key_rows = lax.all_gather(keys.astype(BF16), "seq", axis=0, tiled=True)
    value_rows = lax.all_gather(values.astype(BF16), "seq", axis=0, tiled=True)
    key_rows = key_rows.reshape(-1, local_heads, HEAD_SIZE)
    value_rows = value_rows.reshape(-1, local_heads, HEAD_SIZE)
    scores = jnp.einsum("sthd,khd->shtk", both_sets, key_rows, preferred_element_type=F32)
    weights = jnp.exp(scores - jnp.max(scores, axis=-1, keepdims=True))
    mass = jnp.sum(weights, axis=-1)
    added = jnp.einsum(
        "shtk,khd->sthd", weights.astype(BF16), value_rows, preferred_element_type=F32
    )
    attn = (added / mass.transpose(0, 2, 1)[..., None]).astype(BF16).reshape(2, tokens, width)
    columns = output_matrix.shape[1]
    readout_part = columns_of(velocity_readout_weight, lax.axis_index("seq"), columns)
    mix_full = lax.psum(contract_final_axis(output_matrix, readout_part), "seq")
    lora_readout = contract_final_axis(adapter_output_up, velocity_readout_weight).astype(BF16)
    fake_mix = (mix_full + dot(adapter_output_down, lora_readout)).astype(BF16)
    real_sum, fake_sum = lax.psum(
        (dot(attn[0], mix_full.astype(BF16)), dot(attn[1], fake_mix)), ("group", "head")
    )
    base = contract_final_axis(hidden, velocity_readout_weight)
    noisy_wide = noisy.astype(F32)
    x0_real = noisy_wide - sigma * (base + real_sum)
    x0_fake = noisy_wide - sigma * (base + fake_sum)
    local_error = jnp.sum(jnp.abs(latents.astype(F32) - x0_real))
    weight = lax.psum(local_error, "seq") / (tokens * lax.axis_size("seq") * channels)
    return (x0_fake - x0_real) / weight


def solution(mesh):
    sizes = tuple(mesh.shape[name] for name in ("group", "seq", "head"))

    def local(*args):
        query_columns = args[6].shape[1]
        power = sizes[0] & (sizes[0] - 1) == 0
        paired = sizes[1] == 2 and sizes[2] == 4 and power
        if paired and (query_columns // HEAD_SIZE) % 2 == 0:
            return paired_local(sizes, *args)
        return gathered_local(*args)

    split = ("group", "head")
    in_specs = (
        P("seq", None),
        P("seq", None),
        P(),
        P("seq", None),
        P(),
        P(),
        P("seq", split),
        P("seq", split),
        P("seq", split),
        P(split, "seq"),
        P(),
        P("seq", None),
        P(None, split),
        P(split, None),
        P(),
    )
    return jax.shard_map(
        local, mesh=mesh, in_specs=in_specs, out_specs=P("seq", None), check_vma=False
    )
```

```python
import itertools

import jax
import jax.numpy as jnp
from jax import lax
from jax.experimental import pallas as pl
from jax.experimental.pallas import tpu as pltpu
from jax.sharding import PartitionSpec as P


HEAD_SIZE = 128
F32 = jnp.float32
BF16 = jnp.bfloat16


def contract_final_axis(left, right):
    return lax.dot_general(
        left, right, (((1,), (1,)), ((), ())), preferred_element_type=F32
    )


def dot(left, right):
    return jnp.dot(left, right, preferred_element_type=F32)


def noise_level(step):
    level = (step[0].astype(F32) + 1.0) / 1000.0
    return 5.0 * level / (1.0 + 4.0 * level)


def pairs(sizes, partner):
    def linear(coordinate):
        index = 0
        for value, size in zip(coordinate, sizes):
            index = index * size + value
        return index

    return [
        (linear(c), linear(partner(*c)))
        for c in itertools.product(*[range(n) for n in sizes])
    ]


def columns_of(x, index, count):
    return lax.dynamic_slice_in_dim(x, index * count, count, 1)


VMEM = pl.BlockSpec(memory_space=pltpu.VMEM)
HBM = pl.BlockSpec(memory_space=pltpu.HBM)


def run(kernel, outs, args, specs=None, scratch=(), flops=0, limit=8 << 20, moved=None):
    shapes = [jax.ShapeDtypeStruct(shape, kind) for shape, kind in outs]
    if moved is None:
        moved = sum(a.size * a.dtype.itemsize for a in (*args, *shapes))
    return pl.pallas_call(
        kernel,
        out_shape=shapes,
        in_specs=specs or [VMEM] * len(args),
        out_specs=[VMEM] * len(shapes),
        scratch_shapes=list(scratch),
        cost_estimate=pl.CostEstimate(flops=flops, bytes_accessed=moved, transcendentals=0),
        compiler_params=pltpu.CompilerParams(vmem_limit_bytes=limit),
    )(*args)


def aligned(index, count):
    return pl.ds(pl.multiple_of(index * count, count), count)


def fold(low, high):
    lane = lax.broadcasted_iota(jnp.int32, low.shape, 1)
    return jnp.where(lane < low.shape[1] // 2, low, high)


def swap_halves(x):
    return pltpu.roll(x, x.shape[1] // 2, 1)


def high_low(x):
    high = x.astype(BF16)
    return high, (x - high.astype(F32)).astype(BF16)


def slice_kernel(stream_hbm, message_ref, sem):
    quarter = message_ref.shape[1]
    target = (1 - lax.axis_index("seq")) * 2 + lax.axis_index("head") % 2
    copy = pltpu.make_async_copy(stream_hbm.at[:, aligned(target, quarter)], message_ref, sem)
    copy.start()
    copy.wait()


def first_kernel(
    step_any, latents_hbm, noise_hbm, stream_hbm, patch_hbm, readout_hbm, gain_hbm,
    normed_ref, rows_ref, base_ref, gain_ref,
    step_s, latents_v, noise_v, stream_v, patch_v, readout_v, gain_v, hidden_v, sems,
):
    parts, tokens, quarter = stream_v.shape
    channels = latents_v.shape[0]
    seq = lax.axis_index("seq")
    small = [
        pltpu.make_async_copy(latents_hbm, latents_v, sems.at[0]),
        pltpu.make_async_copy(noise_hbm, noise_v, sems.at[1]),
        pltpu.make_async_copy(step_any, step_s, sems.at[2]),
    ]
    gain_copy = pltpu.make_async_copy(gain_hbm, gain_v, sems.at[3])
    large = []
    for j in range(parts):
        span = pl.ds(j * quarter, quarter)
        large.append([
            pltpu.make_async_copy(source.at[:, span], target.at[j], sems.at[4 + 3 * j + i])
            for i, (source, target) in enumerate(
                ((stream_hbm, stream_v), (patch_hbm, patch_v), (readout_hbm, readout_v))
            )
        ])
    for copy in small:
        copy.start()
    for j in range(parts):
        for copy in large[j]:
            copy.start()
    gain_copy.start()
    for copy in small:
        copy.wait()
    level = (jnp.full((8, 128), step_s[0], jnp.int32).astype(F32) + 1.0) / 1000.0
    sigma = (5.0 * level / (1.0 + 4.0 * level))[:1, :1]
    latents = latents_v[...].astype(F32)
    noisy = ((1.0 - sigma) * latents + sigma * noise_v[...].astype(F32)).astype(BF16)
    base = (latents - noisy.astype(F32)) / sigma
    squares = jnp.zeros((tokens, 128), F32)
    for j in range(parts):
        for copy in large[j]:
            copy.wait()
        embedded = lax.dot_general(
            noisy, patch_v[j], (((0,), (0,)), ((), ())), preferred_element_type=F32
        )
        hidden = (stream_v[j].astype(F32) + embedded).astype(BF16)
        hidden_v[j] = hidden
        base += contract_final_axis(readout_v[j], hidden)
        wide = hidden.astype(F32)
        wide = wide * wide
        for i in range(quarter // 128):
            squares = squares + wide[:, i * 128 : (i + 1) * 128]
    mean = jnp.sum(squares, axis=1, keepdims=True) / (parts * quarter)
    inverse = lax.rsqrt(mean + 1e-06)
    rows_ref[:channels] = noisy.astype(F32)
    rows_ref[channels:] = jnp.broadcast_to(inverse, (tokens, tokens)).T[
        : rows_ref.shape[0] - channels
    ]
    once = (lax.axis_index("group") == 0) & (lax.axis_index("head") == 0)
    base_ref[...] = jnp.where(once, base, 0.0).T
    gain_copy.wait()
    for j in range(parts):

        @pl.when(seq == j // 2)
        def _(j=j):
            gain = gain_v[j * quarter : (j + 1) * quarter][None, :]
            start = (j % 2) * quarter
            gain_ref[j % 2 : j % 2 + 1] = gain
            normed_ref[:, start : start + quarter] = (
                hidden_v[j].astype(F32) * inverse * gain
            ).astype(BF16)


def pick(index, x):
    half = x.shape[1] // 2
    return jnp.where(index == 0, x[:, :half], x[:, half:])


def partial_outputs(parts, seq, sent_ref, kept_ref):
    q, k, v, lora = parts
    columns = q.shape[1] // 2
    blocks = [*high_low(pick(1 - seq, q)), *high_low(pick(1 - seq, k))]
    blocks += [pick(1 - seq, v).astype(BF16), *high_low(lora)]
    for i, block in enumerate(blocks):
        sent_ref[:, i * columns : (i + 1) * columns] = block
    for i, block in enumerate((pick(seq, q), pick(seq, k), pick(seq, v), lora)):
        kept_ref[:, i * columns : (i + 1) * columns] = block


def own_kernel(
    normed_ref, q_ref, k_ref, v_ref, down_ref, output_ref, readout_ref,
    sent_ref, kept_ref, mix_ref, mix_v,
):
    seq = lax.axis_index("seq")
    normed = normed_ref[...]
    parts = [dot(normed, w[...]) for w in (q_ref, k_ref, v_ref, down_ref)]
    partial_outputs(parts, seq, sent_ref, kept_ref)
    readout = readout_ref[:, aligned(seq, normed.shape[1])]
    mix_v[...] = contract_final_axis(output_ref[...], readout)
    rows, channels = mix_ref.shape
    theirs = mix_v[aligned(1 - seq, rows), :]
    high = theirs.astype(BF16).astype(F32)
    both = jnp.concatenate([high, theirs - high], axis=1)
    sent_ref[:, -2 * channels :] = both.astype(BF16)
    mix_ref[...] = mix_v[aligned(seq, rows), :]


def side_kernel(up_ref, readout_ref, readout_of_up_ref):
    readout_of_up_ref[...] = contract_final_axis(up_ref[...], readout_ref[...]).astype(BF16)


def other_parts(part, raw_ref, rows_ref, patch_ref, gain_ref, weights):
    tokens, quarter = raw_ref.shape
    channels = patch_ref.shape[0]
    quarters = lax.axis_index("seq") * 2 + part
    noisy = rows_ref[:channels].astype(BF16)
    inverse = jnp.broadcast_to(rows_ref[channels : channels + 1], (tokens, tokens)).T[:, :1]
    embedded = lax.dot_general(
        noisy, patch_ref[:, aligned(quarters, quarter)],
        (((0,), (0,)), ((), ())), preferred_element_type=F32,
    )
    hidden = (raw_ref[...].astype(F32) + embedded).astype(BF16).astype(F32)
    normed = (hidden * inverse * gain_ref[pl.ds(part, 1), :]).astype(BF16)
    return [dot(normed, w[aligned(part, quarter), :]) for w in weights]


def near_kernel(raw_ref, rows_ref, patch_ref, gain_ref, q_ref, k_ref, v_ref, down_ref, *outs):
    core = lax.axis_index("head") % 2
    weights = (q_ref, k_ref, v_ref, down_ref)
    parts = other_parts(core, raw_ref, rows_ref, patch_ref, gain_ref, weights)
    for out, part in zip(outs, parts):
        out[...] = part


def far_kernel(
    raw_ref, rows_ref, patch_ref, gain_ref, q_ref, k_ref, v_ref, down_ref,
    near_q_ref, near_k_ref, near_v_ref, near_down_ref, sent_ref, kept_ref,
):
    core = lax.axis_index("head") % 2
    weights = (q_ref, k_ref, v_ref, down_ref)
    parts = other_parts(1 - core, raw_ref, rows_ref, patch_ref, gain_ref, weights)
    near = (near_q_ref, near_k_ref, near_v_ref, near_down_ref)
    parts = [part + ref[...] for part, ref in zip(parts, near)]
    partial_outputs(parts, lax.axis_index("seq"), sent_ref, kept_ref)


def finish(kept_ref, got_ref, up):
    columns = up.shape[1]

    def got(i):
        return got_ref[:, i * columns : (i + 1) * columns].astype(F32)

    def kept(i):
        return kept_ref[:, i * columns : (i + 1) * columns]

    scale = HEAD_SIZE ** (-0.5)
    base = kept(0) + (got(0) + got(1))
    lora = (kept(3) + (got(5) + got(6))).astype(BF16)
    return (
        (base * scale).astype(BF16),
        ((base + dot(lora, up)) * scale).astype(BF16),
        (kept(1) + (got(2) + got(3))).astype(BF16),
        (kept(2) + got(4)).astype(BF16),
    )


def half_kernel(
    kept_ref, got_ref, up_ref, mix_ref, down_ref, readout_of_up_ref,
    set_ref, mixes_ref,
):
    seq = lax.axis_index("seq")
    rows, channels = mix_ref.shape
    up = up_ref[:, aligned(seq, rows)]
    for i, block in enumerate(finish(kept_ref, got_ref, up)):
        set_ref[i] = block
    got = got_ref[:, -2 * channels :].astype(F32)
    mix_full = mix_ref[...] + (got[:, :channels] + swap_halves(got)[:, :channels])
    low_rank = dot(down_ref[aligned(seq, rows), :], readout_of_up_ref[...])
    mix = mix_full.astype(BF16).astype(F32)
    fake = (mix_full + low_rank).astype(BF16).astype(F32)
    mixes_ref[0] = jnp.concatenate([mix, -mix], axis=1).astype(BF16)
    mixes_ref[1] = jnp.concatenate([jnp.zeros_like(fake), fake], axis=1).astype(BF16)


def attention_kernel(
    kept_ref, got_ref, up_ref, set_ref, mixes_ref, base_ref,
    sent_ref, stay_ref, sets_v, terms_v,
):
    seq = lax.axis_index("seq")
    core = lax.axis_index("head") % 2
    tokens, channels = base_ref.shape
    columns = set_ref.shape[2]
    up = up_ref[:, aligned(seq, columns)]
    for i, block in enumerate(finish(kept_ref, got_ref, up)):
        sets_v[i, :tokens] = block
        sets_v[i, tokens:] = set_ref[i]
    terms = jnp.zeros(terms_v.shape, F32)
    for start in range(0, columns, HEAD_SIZE):
        span = slice(start, start + HEAD_SIZE)
        keys, values = sets_v[2, :, span], sets_v[3, :, span]
        for kind in range(2):
            scores = contract_final_axis(sets_v[kind, :, span], keys)
            top = jnp.max(scores, axis=1, keepdims=True)
            probs = jnp.exp(scores - top)
            mass = jnp.sum(probs, axis=1, keepdims=True)
            attn = (dot(probs.astype(BF16), values) / mass).astype(BF16)
            terms = terms + dot(attn, mixes_ref[kind, span, :])
    terms_v[...] = terms
    terms_v[:tokens, :channels] = terms[:tokens, :channels] + base_ref[...]
    share = tokens // 2
    sent_ref[:share] = terms_v[aligned(1 - core, share), :]
    sent_ref[share:] = terms_v[aligned(3 - core, share), :]
    stay_ref[:share] = terms_v[aligned(core, share), :]
    stay_ref[share:] = terms_v[aligned(2 + core, share), :]


def pack_kernel(stay_ref, got_ref, same_ref, cross_ref):
    share = stay_ref.shape[0] // 2
    mine = stay_ref[:share] + got_ref[:share]
    theirs = stay_ref[share:] + got_ref[share:]
    half = share // 2
    same_ref[:share] = mine.astype(BF16)
    same_ref[share:] = fold(theirs[:half], swap_halves(theirs[half:])).astype(BF16)
    cross_ref[:share] = theirs.astype(BF16)
    cross_ref[share:] = fold(mine[:half], swap_halves(mine[half:])).astype(BF16)


def error_kernel(*refs):
    *parts, packet_ref = refs
    parts = [ref[...].astype(F32) for ref in parts]
    while len(parts) > 1:
        parts = [a + b for a, b in zip(parts[::2], parts[1::2])]
    total = parts[0]
    half = packet_ref.shape[0] - 8
    share = 2 * half
    own = jnp.abs(total[:half]) + jnp.abs(total[half:share])
    own = fold(own, jnp.zeros_like(own)) + jnp.abs(total[share:])
    packet_ref[:half] = fold(swap_halves(total[:half]), total[half:share])
    packet_ref[half:] = jnp.full((8, packet_ref.shape[1]), jnp.sum(own), F32)


def last_kernel(mine_ref, theirs_ref, out_ref, both_v):
    core = lax.axis_index("head") % 2
    channels, tokens = out_ref.shape
    share = tokens // 2
    half = share // 2
    weight = (mine_ref[half:] + theirs_ref[half:]) / (2 * tokens * channels)
    weight = weight[:1, :1]
    for ref, index in ((mine_ref, core), (theirs_ref, 1 - core)):
        packet = -ref[:half] / weight
        start = pl.multiple_of(index * share, share)
        both_v[pl.ds(start, half)] = packet
        both_v[pl.ds(start + half, half)] = swap_halves(packet)
    out_ref[...] = both_v[...].T[:channels]


def paired_local(
    sizes,
    latents,
    noise,
    step,
    stream,
    patch_embed_weight,
    prenorm_gain_vector,
    query_matrix,
    key_matrix,
    value_matrix,
    output_matrix,
    velocity_readout_weight,
    adapter_query_down,
    adapter_query_up,
    adapter_output_down,
    adapter_output_up,
):
    groups, _, heads = sizes
    tokens, channels = latents.shape
    half_width, local_columns = query_matrix.shape
    quarter = half_width // 2
    columns = local_columns // 2
    rank = adapter_query_down.shape[1]
    share = tokens // 2
    to_x = pairs((2,), lambda s: (s ^ 1,))
    to_core = pairs((heads,), lambda h: (h ^ 1,))
    to_y = pairs((heads,), lambda h: (h ^ 2,))
    to_xy = pairs((2, heads), lambda s, h: (s ^ 1, h ^ 2))
    weights = (query_matrix, key_matrix, value_matrix, adapter_query_down)
    partial_flops = 2 * tokens * half_width * (3 * local_columns + rank)

    in_hbm = pltpu.with_memory_space_constraint(stream, pltpu.HBM)
    (message,) = run(
        slice_kernel,
        [((tokens, quarter), BF16)],
        (in_hbm,),
        [HBM],
        [pltpu.SemaphoreType.DMA],
        moved=4 * tokens * quarter,
    )
    near = lax.ppermute(message, "seq", to_x)
    inputs = (
        latents.T, noise.T, stream, patch_embed_weight, velocity_readout_weight,
        prenorm_gain_vector,
    )
    normed, rows, base, gain = run(
        first_kernel,
        [
            ((tokens, half_width), BF16),
            ((channels + 8, tokens), F32),
            ((tokens, channels), F32),
            ((2, quarter), F32),
        ],
        [step, *(pltpu.with_memory_space_constraint(x, pltpu.HBM) for x in inputs)],
        [pl.BlockSpec(memory_space=pl.ANY)] + [HBM] * 6,
        [
            pltpu.SMEM((1,), jnp.int32),
            pltpu.VMEM((channels, tokens), BF16),
            pltpu.VMEM((channels, tokens), BF16),
            pltpu.VMEM((4, tokens, quarter), BF16),
            pltpu.VMEM((4, channels, quarter), BF16),
            pltpu.VMEM((4, channels, quarter), BF16),
            pltpu.VMEM((4 * quarter,), F32),
            pltpu.VMEM((4, tokens, quarter), BF16),
            pltpu.SemaphoreType.DMA((4 + 3 * 4,)),
        ],
    )
    other_rows = lax.ppermute(rows, "seq", to_x)
    own_sent, own_kept, mix_part = run(
        own_kernel,
        [
            ((tokens, 7 * columns + 2 * channels), BF16),
            ((tokens, 4 * columns), F32),
            ((columns, channels), F32),
        ],
        (normed, *weights, output_matrix, velocity_readout_weight),
        scratch=[pltpu.VMEM((local_columns, channels), F32)],
        flops=partial_flops,
    )
    own_got = lax.ppermute(own_sent, "seq", to_x)
    (readout_of_up,) = run(
        side_kernel,
        [((rank, channels), BF16)],
        (adapter_output_up, velocity_readout_weight),
        flops=4 * rank * half_width * channels,
    )
    far = lax.ppermute(near, "head", to_core)
    shared = (other_rows, patch_embed_weight, gain, *weights)
    near_parts = run(
        near_kernel,
        [((tokens, w.shape[1]), F32) for w in weights],
        (near, *shared),
        flops=partial_flops // 2,
    )
    other_sent, other_kept = run(
        far_kernel,
        [((tokens, 7 * columns), BF16), ((tokens, 4 * columns), F32)],
        (far, *shared, *near_parts),
        flops=partial_flops // 2,
    )
    other_got = lax.ppermute(other_sent, "seq", to_x)
    half_set, mixes = run(
        half_kernel,
        [((4, tokens, columns), BF16), ((2, columns, 2 * channels), BF16)],
        (
            other_kept, own_got, adapter_query_up, mix_part,
            adapter_output_down, readout_of_up,
        ),
    )
    sent, stay = run(
        attention_kernel,
        [((tokens, 2 * channels), F32)] * 2,
        (own_kept, other_got, adapter_query_up, half_set, mixes, base),
        scratch=[
            pltpu.VMEM((4, 2 * tokens, columns), BF16),
            pltpu.VMEM((2 * tokens, 2 * channels), F32),
        ],
    )

    got = lax.ppermute(sent, "head", to_core)
    packed = ((share + share // 2, 2 * channels), BF16)
    same, cross = run(pack_kernel, [packed, packed], (stay, got))
    from_x = lax.ppermute(cross, "seq", to_x)
    from_y = lax.ppermute(same, "head", to_y)
    from_xy = lax.ppermute(cross, ("seq", "head"), to_xy)
    total = (same.astype(F32) + from_y.astype(F32)) + (
        from_x.astype(F32) + from_xy.astype(F32)
    )
    total = total.astype(BF16)
    totals = [total] + [
        lax.ppermute(total, "group", pairs((groups,), lambda g, k=k: (g ^ k,)))
        for k in range(1, groups)
    ]
    (packet,) = run(error_kernel, [((share // 2 + 8, 2 * channels), F32)], totals)
    answer = lax.ppermute(packet, "head", to_core)
    (out,) = run(
        last_kernel,
        [((channels, tokens), F32)],
        (packet, answer),
        scratch=[pltpu.VMEM((tokens, 2 * channels), F32)],
    )
    return out.T


def gathered_local(
    latents,
    noise,
    step,
    stream,
    patch_embed_weight,
    prenorm_gain_vector,
    query_matrix,
    key_matrix,
    value_matrix,
    output_matrix,
    velocity_readout_weight,
    adapter_query_down,
    adapter_query_up,
    adapter_output_down,
    adapter_output_up,
):
    tokens = latents.shape[0]
    width = query_matrix.shape[1]
    local_heads = width // HEAD_SIZE
    channels = velocity_readout_weight.shape[0]
    sigma = noise_level(step)
    noisy = (
        (1.0 - sigma) * latents.astype(F32) + sigma * noise.astype(F32)
    ).astype(BF16)
    hidden = (stream.astype(F32) + dot(noisy, patch_embed_weight)).astype(BF16)
    hidden_wide = hidden.astype(F32)
    normed = (
        hidden_wide
        * lax.rsqrt(jnp.mean(hidden_wide * hidden_wide, axis=-1, keepdims=True) + 1e-06)
        * prenorm_gain_vector
    ).astype(BF16)
    base_query, keys, values, lora_hidden = (
        dot(normed, lax.all_gather(piece, "seq", axis=0, tiled=True))
        for piece in (query_matrix, key_matrix, value_matrix, adapter_query_down)
    )
    scale = HEAD_SIZE ** (-0.5)
    lora_delta = dot(lora_hidden.astype(BF16), adapter_query_up)
    queries = (base_query * scale).astype(BF16)
    fake_queries = ((base_query + lora_delta) * scale).astype(BF16)
    both_sets = jnp.stack([queries, fake_queries]).reshape(2, tokens, local_heads, HEAD_SIZE)
    key_rows = lax.all_gather(keys.astype(BF16), "seq", axis=0, tiled=True)
    value_rows = lax.all_gather(values.astype(BF16), "seq", axis=0, tiled=True)
    key_rows = key_rows.reshape(-1, local_heads, HEAD_SIZE)
    value_rows = value_rows.reshape(-1, local_heads, HEAD_SIZE)
    scores = jnp.einsum("sthd,khd->shtk", both_sets, key_rows, preferred_element_type=F32)
    weights = jnp.exp(scores - jnp.max(scores, axis=-1, keepdims=True))
    mass = jnp.sum(weights, axis=-1)
    added = jnp.einsum(
        "shtk,khd->sthd", weights.astype(BF16), value_rows, preferred_element_type=F32
    )
    attn = (added / mass.transpose(0, 2, 1)[..., None]).astype(BF16).reshape(2, tokens, width)
    columns = output_matrix.shape[1]
    readout_part = columns_of(velocity_readout_weight, lax.axis_index("seq"), columns)
    mix_full = lax.psum(contract_final_axis(output_matrix, readout_part), "seq")
    lora_readout = contract_final_axis(adapter_output_up, velocity_readout_weight).astype(BF16)
    fake_mix = (mix_full + dot(adapter_output_down, lora_readout)).astype(BF16)
    real_sum, fake_sum = lax.psum(
        (dot(attn[0], mix_full.astype(BF16)), dot(attn[1], fake_mix)), ("group", "head")
    )
    base = contract_final_axis(hidden, velocity_readout_weight)
    noisy_wide = noisy.astype(F32)
    x0_real = noisy_wide - sigma * (base + real_sum)
    x0_fake = noisy_wide - sigma * (base + fake_sum)
    local_error = jnp.sum(jnp.abs(latents.astype(F32) - x0_real))
    weight = lax.psum(local_error, "seq") / (tokens * lax.axis_size("seq") * channels)
    return (x0_fake - x0_real) / weight


def solution(mesh):
    sizes = tuple(mesh.shape[name] for name in ("group", "seq", "head"))

    def local(*args):
        query_columns = args[6].shape[1]
        power = sizes[0] & (sizes[0] - 1) == 0
        paired = sizes[1] == 2 and sizes[2] == 4 and power
        if paired and (query_columns // HEAD_SIZE) % 2 == 0:
            return paired_local(sizes, *args)
        return gathered_local(*args)

    split = ("group", "head")
    in_specs = (
        P("seq", None),
        P("seq", None),
        P(),
        P("seq", None),
        P(),
        P(),
        P("seq", split),
        P("seq", split),
        P("seq", split),
        P(split, "seq"),
        P(),
        P("seq", None),
        P(None, split),
        P(split, None),
        P(),
    )
    return jax.shard_map(
        local, mesh=mesh, in_specs=in_specs, out_specs=P("seq", None), check_vma=False
    )
```

```python
import itertools

import jax
import jax.numpy as jnp
from jax import lax
from jax.experimental import pallas as pl
from jax.experimental.pallas import tpu as pltpu
from jax.sharding import PartitionSpec as P


HEAD_SIZE = 128
F32 = jnp.float32
BF16 = jnp.bfloat16


def contract_final_axis(left, right):
    return lax.dot_general(
        left, right, (((1,), (1,)), ((), ())), preferred_element_type=F32
    )


def dot(left, right):
    return jnp.dot(left, right, preferred_element_type=F32)


def noise_level(step):
    level = (step[0].astype(F32) + 1.0) / 1000.0
    return 5.0 * level / (1.0 + 4.0 * level)


def pairs(sizes, partner):
    def linear(coordinate):
        index = 0
        for value, size in zip(coordinate, sizes):
            index = index * size + value
        return index

    return [
        (linear(c), linear(partner(*c)))
        for c in itertools.product(*[range(n) for n in sizes])
    ]


def columns_of(x, index, count):
    return lax.dynamic_slice_in_dim(x, index * count, count, 1)


VMEM = pl.BlockSpec(memory_space=pltpu.VMEM)
HBM = pl.BlockSpec(memory_space=pltpu.HBM)


def run(kernel, outs, args, specs=None, scratch=(), flops=0, limit=8 << 20, moved=None):
    shapes = [jax.ShapeDtypeStruct(shape, kind) for shape, kind in outs]
    if moved is None:
        moved = sum(a.size * a.dtype.itemsize for a in (*args, *shapes))
    return pl.pallas_call(
        kernel,
        out_shape=shapes,
        in_specs=specs or [VMEM] * len(args),
        out_specs=[VMEM] * len(shapes),
        scratch_shapes=list(scratch),
        cost_estimate=pl.CostEstimate(flops=flops, bytes_accessed=moved, transcendentals=0),
        compiler_params=pltpu.CompilerParams(vmem_limit_bytes=limit),
    )(*args)


def aligned(index, count):
    return pl.ds(pl.multiple_of(index * count, count), count)


def fold(low, high):
    lane = lax.broadcasted_iota(jnp.int32, low.shape, 1)
    return jnp.where(lane < low.shape[1] // 2, low, high)


def swap_halves(x):
    return pltpu.roll(x, x.shape[1] // 2, 1)


def high_low(x):
    high = x.astype(BF16)
    return high, (x - high.astype(F32)).astype(BF16)


def slice_kernel(stream_hbm, message_ref, sem):
    quarter = message_ref.shape[1]
    target = (1 - lax.axis_index("seq")) * 2 + lax.axis_index("head") % 2
    copy = pltpu.make_async_copy(stream_hbm.at[:, aligned(target, quarter)], message_ref, sem)
    copy.start()
    copy.wait()


def first_kernel(
    step_any, latents_hbm, noise_hbm, stream_hbm, patch_hbm, readout_hbm, gain_hbm,
    normed_ref, rows_ref, base_ref, gain_ref,
    step_s, latents_v, noise_v, stream_v, patch_v, readout_v, gain_v, hidden_v, sems,
):
    parts, tokens, quarter = stream_v.shape
    channels = latents_v.shape[0]
    seq = lax.axis_index("seq")
    small = [
        pltpu.make_async_copy(latents_hbm, latents_v, sems.at[0]),
        pltpu.make_async_copy(noise_hbm, noise_v, sems.at[1]),
        pltpu.make_async_copy(step_any, step_s, sems.at[2]),
    ]
    gain_copy = pltpu.make_async_copy(gain_hbm, gain_v, sems.at[3])
    large = []
    for j in range(parts):
        span = pl.ds(j * quarter, quarter)
        large.append([
            pltpu.make_async_copy(source.at[:, span], target.at[j], sems.at[4 + 3 * j + i])
            for i, (source, target) in enumerate(
                ((stream_hbm, stream_v), (patch_hbm, patch_v), (readout_hbm, readout_v))
            )
        ])
    for copy in small:
        copy.start()
    for j in range(parts):
        for copy in large[j]:
            copy.start()
    gain_copy.start()
    for copy in small:
        copy.wait()
    level = (jnp.full((8, 128), step_s[0], jnp.int32).astype(F32) + 1.0) / 1000.0
    sigma = (5.0 * level / (1.0 + 4.0 * level))[:1, :1]
    latents = latents_v[...].astype(F32)
    noisy = ((1.0 - sigma) * latents + sigma * noise_v[...].astype(F32)).astype(BF16)
    base = (latents - noisy.astype(F32)) / sigma
    squares = jnp.zeros((tokens, 128), F32)
    for j in range(parts):
        for copy in large[j]:
            copy.wait()
        embedded = lax.dot_general(
            noisy, patch_v[j], (((0,), (0,)), ((), ())), preferred_element_type=F32
        )
        hidden = (stream_v[j].astype(F32) + embedded).astype(BF16)
        hidden_v[j] = hidden
        base += contract_final_axis(readout_v[j], hidden)
        wide = hidden.astype(F32)
        wide = wide * wide
        for i in range(quarter // 128):
            squares = squares + wide[:, i * 128 : (i + 1) * 128]
    mean = jnp.sum(squares, axis=1, keepdims=True) / (parts * quarter)
    inverse = lax.rsqrt(mean + 1e-06)
    rows_ref[:channels] = noisy
    scale = jnp.broadcast_to(inverse, (tokens, tokens)).T[:8]
    first, _ = high_low(scale)
    second, third = high_low(scale - first.astype(F32))
    row = lax.broadcasted_iota(jnp.int32, (16, tokens), 0)
    terms = [jnp.concatenate([x.astype(F32)] * 2, axis=0) for x in (first, second, third)]
    terms = jnp.where(row == 0, terms[0], jnp.where(row == 1, terms[1], terms[2]))
    rows_ref[channels:] = terms.astype(BF16)
    once = (lax.axis_index("group") == 0) & (lax.axis_index("head") == 0)
    base_ref[...] = jnp.where(once, base, 0.0).T
    gain_copy.wait()
    for j in range(parts):

        @pl.when(seq == j // 2)
        def _(j=j):
            gain = gain_v[j * quarter : (j + 1) * quarter][None, :]
            start = (j % 2) * quarter
            gain_ref[j % 2 : j % 2 + 1] = gain
            normed_ref[:, start : start + quarter] = (
                hidden_v[j].astype(F32) * inverse * gain
            ).astype(BF16)


def pick(index, x):
    half = x.shape[1] // 2
    return jnp.where(index == 0, x[:, :half], x[:, half:])


def partial_outputs(parts, seq, sent_ref, kept_ref):
    q, k, v, lora = parts
    columns = q.shape[1] // 2
    blocks = [*high_low(pick(1 - seq, q)), *high_low(pick(1 - seq, k))]
    blocks += [pick(1 - seq, v).astype(BF16), *high_low(lora)]
    for i, block in enumerate(blocks):
        sent_ref[:, i * columns : (i + 1) * columns] = block
    for i, block in enumerate((pick(seq, q), pick(seq, k), pick(seq, v), lora)):
        kept_ref[:, i * columns : (i + 1) * columns] = block


def own_kernel(
    normed_ref, q_ref, k_ref, v_ref, down_hbm, output_hbm, readout_hbm,
    sent_ref, kept_ref, mix_ref,
    down_v, output_v, readout_v, mix_v, sems,
):
    seq = lax.axis_index("seq")
    copies = [
        pltpu.make_async_copy(down_hbm, down_v, sems.at[0]),
        pltpu.make_async_copy(output_hbm, output_v, sems.at[1]),
        pltpu.make_async_copy(
            readout_hbm.at[:, aligned(seq, readout_v.shape[1])], readout_v, sems.at[2]
        ),
    ]
    for copy in copies:
        copy.start()
    normed = normed_ref[...]
    parts = [dot(normed, w[...]) for w in (q_ref, k_ref, v_ref)]
    copies[0].wait()
    parts.append(dot(normed, down_v[...]))
    partial_outputs(parts, seq, sent_ref, kept_ref)
    for copy in copies[1:]:
        copy.wait()
    mix_v[...] = contract_final_axis(output_v[...], readout_v[...])
    rows, channels = mix_ref.shape
    theirs = mix_v[aligned(1 - seq, rows), :]
    high = theirs.astype(BF16).astype(F32)
    both = jnp.concatenate([high, theirs - high], axis=1)
    sent_ref[:, -2 * channels :] = both.astype(BF16)
    mix_ref[...] = mix_v[aligned(seq, rows), :]


def side_kernel(up_ref, readout_ref, readout_of_up_ref):
    readout_of_up_ref[...] = contract_final_axis(up_ref[...], readout_ref[...]).astype(BF16)


def other_parts(part, raw_ref, rows_ref, patch_ref, gain_ref, weights):
    tokens, quarter = raw_ref.shape
    channels = patch_ref.shape[0]
    quarters = lax.axis_index("seq") * 2 + part
    noisy = rows_ref[:channels]
    terms = rows_ref[channels:].astype(F32)
    scale = (terms[:1] + terms[1:2]) + terms[2:3]
    inverse = jnp.broadcast_to(scale, (tokens, tokens)).T[:, :1]
    embedded = lax.dot_general(
        noisy, patch_ref[:, aligned(quarters, quarter)],
        (((0,), (0,)), ((), ())), preferred_element_type=F32,
    )
    hidden = (raw_ref[...].astype(F32) + embedded).astype(BF16).astype(F32)
    normed = (hidden * inverse * gain_ref[pl.ds(part, 1), :]).astype(BF16)
    return [dot(normed, w[aligned(part, quarter), :]) for w in weights]


def near_kernel(raw_ref, rows_ref, patch_ref, gain_ref, q_ref, k_ref, v_ref, down_ref, *outs):
    core = lax.axis_index("head") % 2
    weights = (q_ref, k_ref, v_ref, down_ref)
    parts = other_parts(core, raw_ref, rows_ref, patch_ref, gain_ref, weights)
    for out, part in zip(outs, parts):
        out[...] = part


def far_kernel(
    raw_ref, rows_ref, patch_ref, gain_ref, q_ref, k_ref, v_ref, down_ref,
    near_q_ref, near_k_ref, near_v_ref, near_down_ref, sent_ref, kept_ref,
):
    core = lax.axis_index("head") % 2
    weights = (q_ref, k_ref, v_ref, down_ref)
    parts = other_parts(1 - core, raw_ref, rows_ref, patch_ref, gain_ref, weights)
    near = (near_q_ref, near_k_ref, near_v_ref, near_down_ref)
    parts = [part + ref[...] for part, ref in zip(parts, near)]
    partial_outputs(parts, lax.axis_index("seq"), sent_ref, kept_ref)


def finish(kept_ref, got_ref, up):
    columns = up.shape[1]

    def got(i):
        return got_ref[:, i * columns : (i + 1) * columns].astype(F32)

    def kept(i):
        return kept_ref[:, i * columns : (i + 1) * columns]

    scale = HEAD_SIZE ** (-0.5)
    base = kept(0) + (got(0) + got(1))
    lora = (kept(3) + (got(5) + got(6))).astype(BF16)
    return (
        (base * scale).astype(BF16),
        ((base + dot(lora, up)) * scale).astype(BF16),
        (kept(1) + (got(2) + got(3))).astype(BF16),
        (kept(2) + got(4)).astype(BF16),
    )


def half_kernel(
    kept_ref, got_ref, up_ref, mix_ref, down_ref, readout_of_up_ref,
    set_ref, mixes_ref,
):
    seq = lax.axis_index("seq")
    rows, channels = mix_ref.shape
    up = up_ref[:, aligned(seq, rows)]
    for i, block in enumerate(finish(kept_ref, got_ref, up)):
        set_ref[i] = block
    got = got_ref[:, -2 * channels :].astype(F32)
    mix_full = mix_ref[...] + (got[:, :channels] + swap_halves(got)[:, :channels])
    low_rank = dot(down_ref[aligned(seq, rows), :], readout_of_up_ref[...])
    mix = mix_full.astype(BF16).astype(F32)
    fake = (mix_full + low_rank).astype(BF16).astype(F32)
    mixes_ref[0] = jnp.concatenate([mix, -mix], axis=1).astype(BF16)
    mixes_ref[1] = jnp.concatenate([jnp.zeros_like(fake), fake], axis=1).astype(BF16)


def attention_kernel(
    kept_ref, got_ref, up_ref, set_ref, mixes_ref, base_ref,
    sent_ref, stay_ref, sets_v, terms_v,
):
    seq = lax.axis_index("seq")
    core = lax.axis_index("head") % 2
    tokens, channels = base_ref.shape
    columns = set_ref.shape[2]
    up = up_ref[:, aligned(seq, columns)]
    for i, block in enumerate(finish(kept_ref, got_ref, up)):
        sets_v[i, :tokens] = block
        sets_v[i, tokens:] = set_ref[i]
    terms = jnp.zeros(terms_v.shape, F32)
    for start in range(0, columns, HEAD_SIZE):
        span = slice(start, start + HEAD_SIZE)
        keys, values = sets_v[2, :, span], sets_v[3, :, span]
        for kind in range(2):
            scores = contract_final_axis(sets_v[kind, :, span], keys)
            top = jnp.max(scores, axis=1, keepdims=True)
            probs = jnp.exp(scores - top)
            mass = jnp.sum(probs, axis=1, keepdims=True)
            attn = (dot(probs.astype(BF16), values) / mass).astype(BF16)
            terms = terms + dot(attn, mixes_ref[kind, span, :])
    terms_v[...] = terms
    terms_v[:tokens, :channels] = terms[:tokens, :channels] + base_ref[...]
    share = tokens // 2
    sent_ref[:share] = terms_v[aligned(1 - core, share), :]
    sent_ref[share:] = terms_v[aligned(3 - core, share), :]
    stay_ref[:share] = terms_v[aligned(core, share), :]
    stay_ref[share:] = terms_v[aligned(2 + core, share), :]


def pack_kernel(stay_ref, got_ref, same_ref, cross_ref):
    share = stay_ref.shape[0] // 2
    mine = stay_ref[:share] + got_ref[:share]
    theirs = stay_ref[share:] + got_ref[share:]
    half = share // 2
    same_ref[:share] = mine.astype(BF16)
    same_ref[share:] = fold(theirs[:half], swap_halves(theirs[half:])).astype(BF16)
    cross_ref[:share] = theirs.astype(BF16)
    cross_ref[share:] = fold(mine[:half], swap_halves(mine[half:])).astype(BF16)


def error_kernel(*refs):
    *parts, packet_ref = refs
    parts = [ref[...].astype(F32) for ref in parts]
    while len(parts) > 1:
        parts = [a + b for a, b in zip(parts[::2], parts[1::2])]
    total = parts[0]
    half = packet_ref.shape[0] - 8
    share = 2 * half
    own = jnp.abs(total[:half]) + jnp.abs(total[half:share])
    own = fold(own, jnp.zeros_like(own)) + jnp.abs(total[share:])
    packet_ref[:half] = fold(swap_halves(total[:half]), total[half:share])
    packet_ref[half:] = jnp.full((8, packet_ref.shape[1]), jnp.sum(own), F32)


def last_kernel(mine_ref, theirs_ref, out_ref, both_v):
    core = lax.axis_index("head") % 2
    channels, tokens = out_ref.shape
    share = tokens // 2
    half = share // 2
    weight = (mine_ref[half:] + theirs_ref[half:]) / (2 * tokens * channels)
    weight = weight[:1, :1]
    for ref, index in ((mine_ref, core), (theirs_ref, 1 - core)):
        packet = -ref[:half] / weight
        start = pl.multiple_of(index * share, share)
        both_v[pl.ds(start, half)] = packet
        both_v[pl.ds(start + half, half)] = swap_halves(packet)
    out_ref[...] = both_v[...].T[:channels]


def paired_local(
    sizes,
    latents,
    noise,
    step,
    stream,
    patch_embed_weight,
    prenorm_gain_vector,
    query_matrix,
    key_matrix,
    value_matrix,
    output_matrix,
    velocity_readout_weight,
    adapter_query_down,
    adapter_query_up,
    adapter_output_down,
    adapter_output_up,
):
    groups, _, heads = sizes
    tokens, channels = latents.shape
    half_width, local_columns = query_matrix.shape
    quarter = half_width // 2
    columns = local_columns // 2
    rank = adapter_query_down.shape[1]
    share = tokens // 2
    to_x = pairs((2,), lambda s: (s ^ 1,))
    to_core = pairs((heads,), lambda h: (h ^ 1,))
    to_y = pairs((heads,), lambda h: (h ^ 2,))
    to_xy = pairs((2, heads), lambda s, h: (s ^ 1, h ^ 2))
    weights = (query_matrix, key_matrix, value_matrix, adapter_query_down)
    partial_flops = 2 * tokens * half_width * (3 * local_columns + rank)

    in_hbm = pltpu.with_memory_space_constraint(stream, pltpu.HBM)
    (message,) = run(
        slice_kernel,
        [((tokens, quarter), BF16)],
        (in_hbm,),
        [HBM],
        [pltpu.SemaphoreType.DMA],
        moved=4 * tokens * quarter,
    )
    near = lax.ppermute(message, "seq", to_x)
    inputs = (
        latents.T, noise.T, stream, patch_embed_weight, velocity_readout_weight,
        prenorm_gain_vector,
    )
    normed, rows, base, gain = run(
        first_kernel,
        [
            ((tokens, half_width), BF16),
            ((channels + 16, tokens), BF16),
            ((tokens, channels), F32),
            ((2, quarter), F32),
        ],
        [step, *(pltpu.with_memory_space_constraint(x, pltpu.HBM) for x in inputs)],
        [pl.BlockSpec(memory_space=pl.ANY)] + [HBM] * 6,
        [
            pltpu.SMEM((1,), jnp.int32),
            pltpu.VMEM((channels, tokens), BF16),
            pltpu.VMEM((channels, tokens), BF16),
            pltpu.VMEM((4, tokens, quarter), BF16),
            pltpu.VMEM((4, channels, quarter), BF16),
            pltpu.VMEM((4, channels, quarter), BF16),
            pltpu.VMEM((4 * quarter,), F32),
            pltpu.VMEM((4, tokens, quarter), BF16),
            pltpu.SemaphoreType.DMA((4 + 3 * 4,)),
        ],
    )
    other_rows = lax.ppermute(rows, "seq", to_x)
    own_sent, own_kept, mix_part = run(
        own_kernel,
        [
            ((tokens, 7 * columns + 2 * channels), BF16),
            ((tokens, 4 * columns), F32),
            ((columns, channels), F32),
        ],
        (
            normed, *weights[:3],
            *(
                pltpu.with_memory_space_constraint(x, pltpu.HBM)
                for x in (adapter_query_down, output_matrix, velocity_readout_weight)
            ),
        ),
        [VMEM] * 4 + [HBM] * 3,
        scratch=[
            pltpu.VMEM(adapter_query_down.shape, BF16),
            pltpu.VMEM(output_matrix.shape, BF16),
            pltpu.VMEM((channels, half_width), BF16),
            pltpu.VMEM((local_columns, channels), F32),
            pltpu.SemaphoreType.DMA((3,)),
        ],
        flops=partial_flops,
    )
    own_got = lax.ppermute(own_sent, "seq", to_x)
    (readout_of_up,) = run(
        side_kernel,
        [((rank, channels), BF16)],
        (adapter_output_up, velocity_readout_weight),
        flops=4 * rank * half_width * channels,
    )
    far = lax.ppermute(near, "head", to_core)
    shared = (other_rows, patch_embed_weight, gain, *weights)
    near_parts = run(
        near_kernel,
        [((tokens, w.shape[1]), F32) for w in weights],
        (near, *shared),
        flops=partial_flops // 2,
    )
    other_sent, other_kept = run(
        far_kernel,
        [((tokens, 7 * columns), BF16), ((tokens, 4 * columns), F32)],
        (far, *shared, *near_parts),
        flops=partial_flops // 2,
    )
    other_got = lax.ppermute(other_sent, "seq", to_x)
    half_set, mixes = run(
        half_kernel,
        [((4, tokens, columns), BF16), ((2, columns, 2 * channels), BF16)],
        (
            other_kept, own_got, adapter_query_up, mix_part,
            adapter_output_down, readout_of_up,
        ),
    )
    sent, stay = run(
        attention_kernel,
        [((tokens, 2 * channels), F32)] * 2,
        (own_kept, other_got, adapter_query_up, half_set, mixes, base),
        scratch=[
            pltpu.VMEM((4, 2 * tokens, columns), BF16),
            pltpu.VMEM((2 * tokens, 2 * channels), F32),
        ],
    )

    got = lax.ppermute(sent, "head", to_core)
    packed = ((share + share // 2, 2 * channels), BF16)
    same, cross = run(pack_kernel, [packed, packed], (stay, got))
    from_x = lax.ppermute(cross, "seq", to_x)
    from_y = lax.ppermute(same, "head", to_y)
    from_xy = lax.ppermute(cross, ("seq", "head"), to_xy)
    total = (same.astype(F32) + from_y.astype(F32)) + (
        from_x.astype(F32) + from_xy.astype(F32)
    )
    total = total.astype(BF16)
    totals = [total]
    for k in range(1, groups):
        to_group = pairs((groups,), lambda g, k=k: (g ^ k,))
        totals.append(lax.ppermute(total, "group", to_group))
    (packet,) = run(error_kernel, [((share // 2 + 8, 2 * channels), F32)], totals)
    answer = lax.ppermute(packet, "head", to_core)
    (out,) = run(
        last_kernel,
        [((channels, tokens), F32)],
        (packet, answer),
        scratch=[pltpu.VMEM((tokens, 2 * channels), F32)],
    )
    return out.T


def gathered_local(
    latents,
    noise,
    step,
    stream,
    patch_embed_weight,
    prenorm_gain_vector,
    query_matrix,
    key_matrix,
    value_matrix,
    output_matrix,
    velocity_readout_weight,
    adapter_query_down,
    adapter_query_up,
    adapter_output_down,
    adapter_output_up,
):
    tokens = latents.shape[0]
    width = query_matrix.shape[1]
    local_heads = width // HEAD_SIZE
    channels = velocity_readout_weight.shape[0]
    sigma = noise_level(step)
    noisy = (
        (1.0 - sigma) * latents.astype(F32) + sigma * noise.astype(F32)
    ).astype(BF16)
    hidden = (stream.astype(F32) + dot(noisy, patch_embed_weight)).astype(BF16)
    hidden_wide = hidden.astype(F32)
    normed = (
        hidden_wide
        * lax.rsqrt(jnp.mean(hidden_wide * hidden_wide, axis=-1, keepdims=True) + 1e-06)
        * prenorm_gain_vector
    ).astype(BF16)
    base_query, keys, values, lora_hidden = (
        dot(normed, lax.all_gather(piece, "seq", axis=0, tiled=True))
        for piece in (query_matrix, key_matrix, value_matrix, adapter_query_down)
    )
    scale = HEAD_SIZE ** (-0.5)
    lora_delta = dot(lora_hidden.astype(BF16), adapter_query_up)
    queries = (base_query * scale).astype(BF16)
    fake_queries = ((base_query + lora_delta) * scale).astype(BF16)
    both_sets = jnp.stack([queries, fake_queries]).reshape(2, tokens, local_heads, HEAD_SIZE)
    key_rows = lax.all_gather(keys.astype(BF16), "seq", axis=0, tiled=True)
    value_rows = lax.all_gather(values.astype(BF16), "seq", axis=0, tiled=True)
    key_rows = key_rows.reshape(-1, local_heads, HEAD_SIZE)
    value_rows = value_rows.reshape(-1, local_heads, HEAD_SIZE)
    scores = jnp.einsum("sthd,khd->shtk", both_sets, key_rows, preferred_element_type=F32)
    weights = jnp.exp(scores - jnp.max(scores, axis=-1, keepdims=True))
    mass = jnp.sum(weights, axis=-1)
    added = jnp.einsum(
        "shtk,khd->sthd", weights.astype(BF16), value_rows, preferred_element_type=F32
    )
    attn = (added / mass.transpose(0, 2, 1)[..., None]).astype(BF16).reshape(2, tokens, width)
    columns = output_matrix.shape[1]
    readout_part = columns_of(velocity_readout_weight, lax.axis_index("seq"), columns)
    mix_full = lax.psum(contract_final_axis(output_matrix, readout_part), "seq")
    lora_readout = contract_final_axis(adapter_output_up, velocity_readout_weight).astype(BF16)
    fake_mix = (mix_full + dot(adapter_output_down, lora_readout)).astype(BF16)
    real_sum, fake_sum = lax.psum(
        (dot(attn[0], mix_full.astype(BF16)), dot(attn[1], fake_mix)), ("group", "head")
    )
    base = contract_final_axis(hidden, velocity_readout_weight)
    noisy_wide = noisy.astype(F32)
    x0_real = noisy_wide - sigma * (base + real_sum)
    x0_fake = noisy_wide - sigma * (base + fake_sum)
    local_error = jnp.sum(jnp.abs(latents.astype(F32) - x0_real))
    weight = lax.psum(local_error, "seq") / (tokens * lax.axis_size("seq") * channels)
    return (x0_fake - x0_real) / weight


def solution(mesh):
    sizes = tuple(mesh.shape[name] for name in ("group", "seq", "head"))

    def local(*args):
        query_columns = args[6].shape[1]
        power = sizes[0] & (sizes[0] - 1) == 0
        paired = sizes[1] == 2 and sizes[2] == 4 and power
        if paired and (query_columns // HEAD_SIZE) % 2 == 0:
            return paired_local(sizes, *args)
        return gathered_local(*args)

    split = ("group", "head")
    in_specs = (
        P("seq", None),
        P("seq", None),
        P(),
        P("seq", None),
        P(),
        P(),
        P("seq", split),
        P("seq", split),
        P("seq", split),
        P(split, "seq"),
        P(),
        P("seq", None),
        P(None, split),
        P(split, None),
        P(),
    )
    return jax.shard_map(
        local, mesh=mesh, in_specs=in_specs, out_specs=P("seq", None), check_vma=False
    )
```

```python
import itertools

import jax
import jax.numpy as jnp
from jax import lax
from jax.experimental import pallas as pl
from jax.experimental.pallas import tpu as pltpu
from jax.sharding import PartitionSpec as P


HEAD_SIZE = 128
F32 = jnp.float32
BF16 = jnp.bfloat16


def contract_final_axis(left, right):
    return lax.dot_general(
        left, right, (((1,), (1,)), ((), ())), preferred_element_type=F32
    )


def dot(left, right):
    return jnp.dot(left, right, preferred_element_type=F32)


def noise_level(step):
    level = (step[0].astype(F32) + 1.0) / 1000.0
    return 5.0 * level / (1.0 + 4.0 * level)


def pairs(sizes, partner):
    def linear(coordinate):
        index = 0
        for value, size in zip(coordinate, sizes):
            index = index * size + value
        return index

    return [
        (linear(c), linear(partner(*c)))
        for c in itertools.product(*[range(n) for n in sizes])
    ]


def columns_of(x, index, count):
    return lax.dynamic_slice_in_dim(x, index * count, count, 1)


VMEM = pl.BlockSpec(memory_space=pltpu.VMEM)
HBM = pl.BlockSpec(memory_space=pltpu.HBM)


def run(kernel, outs, args, specs=None, scratch=(), flops=0, limit=8 << 20, moved=None):
    shapes = [jax.ShapeDtypeStruct(shape, kind) for shape, kind in outs]
    if moved is None:
        moved = sum(a.size * a.dtype.itemsize for a in (*args, *shapes))
    return pl.pallas_call(
        kernel,
        out_shape=shapes,
        in_specs=specs or [VMEM] * len(args),
        out_specs=[VMEM] * len(shapes),
        scratch_shapes=list(scratch),
        cost_estimate=pl.CostEstimate(flops=flops, bytes_accessed=moved, transcendentals=0),
        compiler_params=pltpu.CompilerParams(vmem_limit_bytes=limit),
    )(*args)


def aligned(index, count):
    return pl.ds(pl.multiple_of(index * count, count), count)


def fold(low, high):
    lane = lax.broadcasted_iota(jnp.int32, low.shape, 1)
    return jnp.where(lane < low.shape[1] // 2, low, high)


def swap_halves(x):
    return pltpu.roll(x, x.shape[1] // 2, 1)


def high_low(x):
    high = x.astype(BF16)
    return high, (x - high.astype(F32)).astype(BF16)


def slice_kernel(stream_hbm, message_ref, sems):
    tokens, quarter = message_ref.shape
    target = (1 - lax.axis_index("seq")) * 2 + lax.axis_index("head") % 2
    pieces = sems.shape[0]
    rows = tokens // pieces
    copies = [
        pltpu.make_async_copy(
            stream_hbm.at[pl.ds(i * rows, rows), aligned(target, quarter)],
            message_ref.at[pl.ds(i * rows, rows)],
            sems.at[i],
        )
        for i in range(pieces)
    ]
    for copy in copies:
        copy.start()
    for copy in copies:
        copy.wait()


def first_kernel(
    step_any, latents_hbm, noise_hbm, stream_hbm, patch_hbm, gain_hbm, value_hbm,
    normed_ref, rows_ref, gap_ref, hidden_ref, gain_ref, patch_ref, value_ref,
    step_s, latents_v, noise_v, stream_v, patch_v, gain_v, sems,
):
    parts, tokens, quarter = stream_v.shape
    channels = latents_v.shape[0]
    seq = lax.axis_index("seq")
    small = [
        pltpu.make_async_copy(latents_hbm, latents_v, sems.at[0]),
        pltpu.make_async_copy(noise_hbm, noise_v, sems.at[1]),
        pltpu.make_async_copy(step_any, step_s, sems.at[2]),
    ]
    gain_copy = pltpu.make_async_copy(gain_hbm, gain_v, sems.at[3])
    large = []
    for j in range(parts):
        span = pl.ds(j * quarter, quarter)
        large.append([
            pltpu.make_async_copy(source.at[:, span], target.at[j], sems.at[4 + 2 * j + i])
            for i, (source, target) in enumerate(
                ((stream_hbm, stream_v), (patch_hbm, patch_v))
            )
        ])
    for copy in small:
        copy.start()
    for j in range(parts):
        for copy in large[j]:
            copy.start()
    gain_copy.start()
    value_copy = pltpu.make_async_copy(value_hbm, value_ref, sems.at[sems.shape[0] - 1])
    value_copy.start()
    for copy in small:
        copy.wait()
    level = (jnp.full((8, 128), step_s[0], jnp.int32).astype(F32) + 1.0) / 1000.0
    sigma = (5.0 * level / (1.0 + 4.0 * level))[:1, :1]
    latents = latents_v[...].astype(F32)
    noisy = ((1.0 - sigma) * latents + sigma * noise_v[...].astype(F32)).astype(BF16)
    gap_ref[...] = (latents - noisy.astype(F32)) / sigma
    squares = jnp.zeros((tokens, 128), F32)
    for j in range(parts):
        for copy in large[j]:
            copy.wait()
        embedded = lax.dot_general(
            noisy, patch_v[j], (((0,), (0,)), ((), ())), preferred_element_type=F32
        )
        hidden = (stream_v[j].astype(F32) + embedded).astype(BF16)
        hidden_ref[j] = hidden
        wide = hidden.astype(F32)
        wide = wide * wide
        for i in range(quarter // 128):
            squares = squares + wide[:, i * 128 : (i + 1) * 128]
    mean = jnp.sum(squares, axis=1, keepdims=True) / (parts * quarter)
    inverse = lax.rsqrt(mean + 1e-06)
    rows_ref[:channels] = noisy
    scale = jnp.broadcast_to(inverse, (tokens, tokens)).T[:8]
    first, _ = high_low(scale)
    second, third = high_low(scale - first.astype(F32))
    row = lax.broadcasted_iota(jnp.int32, (16, tokens), 0)
    terms = [jnp.concatenate([x.astype(F32)] * 2, axis=0) for x in (first, second, third)]
    terms = jnp.where(row == 0, terms[0], jnp.where(row == 1, terms[1], terms[2]))
    rows_ref[channels:] = terms.astype(BF16)
    gain_copy.wait()
    for j in range(parts):

        @pl.when(seq == j // 2)
        def _(j=j):
            gain = gain_v[j * quarter : (j + 1) * quarter][None, :]
            start = (j % 2) * quarter
            gain_ref[j % 2 : j % 2 + 1] = gain
            patch_ref[j % 2] = patch_v[j]
            normed_ref[:, start : start + quarter] = (
                hidden_ref[j].astype(F32) * inverse * gain
            ).astype(BF16)

    value_copy.wait()


def pick(index, x):
    half = x.shape[1] // 2
    return jnp.where(index == 0, x[:, :half], x[:, half:])


def partial_outputs(parts, seq, lora_blocks, sent_ref, kept_ref):
    q, k, v, lora = parts
    columns = q.shape[1] // 2
    blocks = [*high_low(pick(1 - seq, q)), *high_low(pick(1 - seq, k))]
    blocks += [pick(1 - seq, v).astype(BF16), *lora_blocks]
    for i, block in enumerate(blocks):
        sent_ref[:, i * columns : (i + 1) * columns] = block
    for i, block in enumerate((pick(seq, q), pick(seq, k), pick(seq, v), lora)):
        kept_ref[:, i * columns : (i + 1) * columns] = block


def own_kernel(
    normed_ref, q_ref, k_ref, v_ref, down_hbm, output_hbm, readout_hbm,
    sent_ref, kept_ref, mix_ref, down_v,
    output_v, readout_v, mix_v, sems,
):
    seq = lax.axis_index("seq")
    copies = [
        pltpu.make_async_copy(down_hbm, down_v, sems.at[0]),
        pltpu.make_async_copy(output_hbm, output_v, sems.at[1]),
        pltpu.make_async_copy(
            readout_hbm.at[:, aligned(seq, readout_v.shape[1])], readout_v, sems.at[2]
        ),
    ]
    for copy in copies:
        copy.start()
    normed = normed_ref[...]
    parts = [dot(normed, w[...]) for w in (q_ref, k_ref, v_ref)]
    copies[0].wait()
    lora = dot(normed, down_v[...])
    share = lora.shape[0] // 2
    half = jnp.where(lax.axis_index("head") % 2 == 0, lora[:share], lora[share:])
    high, low = high_low(half)
    parts.append(lora)
    both = jnp.concatenate([high, low], axis=0)
    partial_outputs(parts, seq, [both], sent_ref, kept_ref)
    for copy in copies[1:]:
        copy.wait()
    mix_v[...] = contract_final_axis(output_v[...], readout_v[...])
    rows, channels = mix_ref.shape
    theirs = mix_v[aligned(1 - seq, rows), :]
    high = theirs.astype(BF16).astype(F32)
    both = jnp.concatenate([high, theirs - high], axis=1)
    sent_ref[:, -2 * channels :] = both.astype(BF16)
    mix_ref[...] = mix_v[aligned(seq, rows), :]


def side_kernel(hidden_ref, up_ref, readout_ref, gap_ref, readout_of_up_ref, base_ref):
    parts, _, quarter = hidden_ref.shape
    readout_of_up_ref[...] = contract_final_axis(up_ref[...], readout_ref[...]).astype(BF16)
    base = gap_ref[...]
    for j in range(parts):
        base += contract_final_axis(
            readout_ref[:, j * quarter : (j + 1) * quarter], hidden_ref[j]
        )
    once = (lax.axis_index("group") == 0) & (lax.axis_index("head") == 0)
    base_ref[...] = jnp.where(once, base, 0.0).T


def other_parts(part, raw_ref, rows_ref, patch_ref, gain_ref, weights):
    tokens, quarter = raw_ref.shape
    channels = patch_ref.shape[1]
    noisy = rows_ref[:channels]
    terms = rows_ref[channels:].astype(F32)
    scale = (terms[:1] + terms[1:2]) + terms[2:3]
    inverse = jnp.broadcast_to(scale, (tokens, tokens)).T[:, :1]
    embedded = lax.dot_general(
        noisy, patch_ref[part],
        (((0,), (0,)), ((), ())), preferred_element_type=F32,
    )
    hidden = (raw_ref[...].astype(F32) + embedded).astype(BF16).astype(F32)
    normed = (hidden * inverse * gain_ref[pl.ds(part, 1), :]).astype(BF16)
    return [dot(normed, w[aligned(part, quarter), :]) for w in weights]


def near_kernel(raw_ref, rows_ref, patch_ref, gain_ref, q_ref, k_ref, v_ref, down_ref, *outs):
    core = lax.axis_index("head") % 2
    weights = (q_ref, k_ref, v_ref, down_ref)
    parts = other_parts(core, raw_ref, rows_ref, patch_ref, gain_ref, weights)
    for out, part in zip(outs, parts):
        out[...] = part


def far_kernel(
    raw_ref, rows_ref, patch_ref, gain_ref, q_ref, k_ref, v_ref, down_ref,
    near_q_ref, near_k_ref, near_v_ref, near_down_ref, sent_ref, kept_ref,
):
    core = lax.axis_index("head") % 2
    weights = (q_ref, k_ref, v_ref, down_ref)
    parts = other_parts(1 - core, raw_ref, rows_ref, patch_ref, gain_ref, weights)
    near = (near_q_ref, near_k_ref, near_v_ref, near_down_ref)
    parts = [part + ref[...] for part, ref in zip(parts, near)]
    lora = high_low(parts[3])
    partial_outputs(parts, lax.axis_index("seq"), lora, sent_ref, kept_ref)


def finish(kept_ref, got_ref, up, lora):
    columns = up.shape[1]

    def got(i):
        return got_ref[:, i * columns : (i + 1) * columns].astype(F32)

    def kept(i):
        return kept_ref[:, i * columns : (i + 1) * columns]

    scale = HEAD_SIZE ** (-0.5)
    base = kept(0) + (got(0) + got(1))
    return (
        (base * scale).astype(BF16),
        ((base + dot(lora, up)) * scale).astype(BF16),
        (kept(1) + (got(2) + got(3))).astype(BF16),
        (kept(2) + got(4)).astype(BF16),
    )


def lora_kernel(kept_ref, got_ref, lora_ref):
    share, rank = lora_ref.shape
    got = got_ref[:, 5 * rank : 6 * rank].astype(F32)
    core = lax.axis_index("head") % 2
    kept = kept_ref[aligned(core, share), 3 * rank :]
    lora_ref[...] = (kept + (got[:share] + got[share:])).astype(BF16)


def half_kernel(
    kept_ref, got_ref, lora_ref, lora_far_ref, up_ref, mix_ref, down_ref, readout_of_up_ref,
    set_ref, mixes_ref,
):
    seq = lax.axis_index("seq")
    rows, channels = mix_ref.shape
    up = up_ref[:, aligned(seq, rows)]
    mine, far = lora_ref[...], lora_far_ref[...]
    first = lax.axis_index("head") % 2 == 0
    lora = jnp.concatenate([jnp.where(first, mine, far), jnp.where(first, far, mine)], axis=0)
    for i, block in enumerate(finish(kept_ref, got_ref, up, lora)):
        set_ref[i] = block
    got = got_ref[:, -2 * channels :].astype(F32)
    mix_full = mix_ref[...] + (got[:, :channels] + swap_halves(got)[:, :channels])
    low_rank = dot(down_ref[aligned(seq, rows), :], readout_of_up_ref[...])
    mix = mix_full.astype(BF16).astype(F32)
    fake = (mix_full + low_rank).astype(BF16).astype(F32)
    mixes_ref[0] = jnp.concatenate([mix, -mix], axis=1).astype(BF16)
    mixes_ref[1] = jnp.concatenate([jnp.zeros_like(fake), fake], axis=1).astype(BF16)


def attention_kernel(
    kept_ref, got_ref, up_ref, set_ref, mixes_ref, base_ref,
    sent_ref, stay_ref, sets_v, terms_v,
):
    seq = lax.axis_index("seq")
    core = lax.axis_index("head") % 2
    tokens, channels = base_ref.shape
    columns = set_ref.shape[2]
    up = up_ref[:, aligned(seq, columns)]
    rank = got_ref.shape[1] - 5 * columns
    got = got_ref[:, 5 * columns :].astype(F32)
    lora = kept_ref[:, 3 * columns :] + (got[:, : rank // 2] + got[:, rank // 2 :])
    for i, block in enumerate(finish(kept_ref, got_ref, up, lora.astype(BF16))):
        sets_v[i, :tokens] = block
        sets_v[i, tokens:] = set_ref[i]
    terms = jnp.zeros(terms_v.shape, F32)
    for start in range(0, columns, HEAD_SIZE):
        span = slice(start, start + HEAD_SIZE)
        keys, values = sets_v[2, :, span], sets_v[3, :, span]
        for kind in range(2):
            scores = contract_final_axis(sets_v[kind, :, span], keys)
            top = jnp.max(scores, axis=1, keepdims=True)
            probs = jnp.exp(scores - top)
            mass = jnp.sum(probs, axis=1, keepdims=True)
            attn = (dot(probs.astype(BF16), values) / mass).astype(BF16)
            terms = terms + dot(attn, mixes_ref[kind, span, :])
    terms_v[...] = terms
    terms_v[:tokens, :channels] = terms[:tokens, :channels] + base_ref[...]
    share = tokens // 2
    sent_ref[:share] = terms_v[aligned(1 - core, share), :]
    sent_ref[share:] = terms_v[aligned(3 - core, share), :]
    stay_ref[:share] = terms_v[aligned(core, share), :]
    stay_ref[share:] = terms_v[aligned(2 + core, share), :]


def pack_kernel(stay_ref, got_ref, same_ref, cross_ref):
    share = stay_ref.shape[0] // 2
    mine = stay_ref[:share] + got_ref[:share]
    theirs = stay_ref[share:] + got_ref[share:]
    half = share // 2
    same_ref[:share] = mine.astype(BF16)
    same_ref[share:] = fold(theirs[:half], swap_halves(theirs[half:])).astype(BF16)
    cross_ref[:share] = theirs.astype(BF16)
    cross_ref[share:] = fold(mine[:half], swap_halves(mine[half:])).astype(BF16)


def error_kernel(*refs):
    *parts, packet_ref = refs
    parts = [ref[...].astype(F32) for ref in parts]
    while len(parts) > 1:
        parts = [a + b for a, b in zip(parts[::2], parts[1::2])]
    total = parts[0]
    half = packet_ref.shape[0] - 8
    share = 2 * half
    own = jnp.abs(total[:half]) + jnp.abs(total[half:share])
    own = fold(own, jnp.zeros_like(own)) + jnp.abs(total[share:])
    packet_ref[:half] = fold(swap_halves(total[:half]), total[half:share])
    packet_ref[half:] = jnp.full((8, packet_ref.shape[1]), jnp.sum(own), F32)


def last_kernel(mine_ref, theirs_ref, out_ref, both_v):
    core = lax.axis_index("head") % 2
    channels, tokens = out_ref.shape
    share = tokens // 2
    half = share // 2
    weight = (mine_ref[half:] + theirs_ref[half:]) / (2 * tokens * channels)
    weight = weight[:1, :1]
    for ref, index in ((mine_ref, core), (theirs_ref, 1 - core)):
        packet = -ref[:half] / weight
        start = pl.multiple_of(index * share, share)
        both_v[pl.ds(start, half)] = packet
        both_v[pl.ds(start + half, half)] = swap_halves(packet)
    out_ref[...] = both_v[...].T[:channels]


def paired_local(
    sizes,
    latents,
    noise,
    step,
    stream,
    patch_embed_weight,
    prenorm_gain_vector,
    query_matrix,
    key_matrix,
    value_matrix,
    output_matrix,
    velocity_readout_weight,
    adapter_query_down,
    adapter_query_up,
    adapter_output_down,
    adapter_output_up,
):
    groups, _, heads = sizes
    tokens, channels = latents.shape
    half_width, local_columns = query_matrix.shape
    quarter = half_width // 2
    columns = local_columns // 2
    rank = adapter_query_down.shape[1]
    share = tokens // 2
    to_x = pairs((2,), lambda s: (s ^ 1,))
    to_core = pairs((heads,), lambda h: (h ^ 1,))
    to_y = pairs((heads,), lambda h: (h ^ 2,))
    to_xy = pairs((2, heads), lambda s, h: (s ^ 1, h ^ 2))
    partial_flops = 2 * tokens * half_width * (3 * local_columns + rank)

    in_hbm = pltpu.with_memory_space_constraint(stream, pltpu.HBM)
    (message,) = run(
        slice_kernel,
        [((tokens, quarter), BF16)],
        (in_hbm,),
        [HBM],
        [pltpu.SemaphoreType.DMA((4,))],
        moved=4 * tokens * quarter,
    )
    near = lax.ppermute(message, "seq", to_x)
    inputs = (
        latents.T, noise.T, stream, patch_embed_weight, prenorm_gain_vector, value_matrix,
    )
    normed, rows, gap, hidden, gain, patch, value = run(
        first_kernel,
        [
            ((tokens, half_width), BF16),
            ((channels + 16, tokens), BF16),
            ((channels, tokens), F32),
            ((4, tokens, quarter), BF16),
            ((2, quarter), F32),
            ((2, channels, quarter), BF16),
            (value_matrix.shape, BF16),
        ],
        [step, *(pltpu.with_memory_space_constraint(x, pltpu.HBM) for x in inputs)],
        [pl.BlockSpec(memory_space=pl.ANY)] + [HBM] * 6,
        [
            pltpu.SMEM((1,), jnp.int32),
            pltpu.VMEM((channels, tokens), BF16),
            pltpu.VMEM((channels, tokens), BF16),
            pltpu.VMEM((4, tokens, quarter), BF16),
            pltpu.VMEM((4, channels, quarter), BF16),
            pltpu.VMEM((4 * quarter,), F32),
            pltpu.SemaphoreType.DMA((5 + 2 * 4,)),
        ],
    )
    other_rows = lax.ppermute(rows, "seq", to_x)
    own_sent, own_kept, mix_part, down = run(
        own_kernel,
        [
            ((tokens, 6 * columns + 2 * channels), BF16),
            ((tokens, 4 * columns), F32),
            ((columns, channels), F32),
            (adapter_query_down.shape, BF16),
        ],
        (
            normed, query_matrix, key_matrix, value,
            *(
                pltpu.with_memory_space_constraint(x, pltpu.HBM)
                for x in (adapter_query_down, output_matrix, velocity_readout_weight)
            ),
        ),
        [VMEM] * 4 + [HBM] * 3,
        scratch=[
            pltpu.VMEM(output_matrix.shape, BF16),
            pltpu.VMEM((channels, half_width), BF16),
            pltpu.VMEM((local_columns, channels), F32),
            pltpu.SemaphoreType.DMA((3,)),
        ],
        flops=partial_flops,
    )
    own_got = lax.ppermute(own_sent, "seq", to_x)
    readout_of_up, base = run(
        side_kernel,
        [((rank, channels), BF16), ((tokens, channels), F32)],
        (hidden, adapter_output_up, velocity_readout_weight, gap),
        flops=8 * tokens * half_width * channels,
    )
    far = lax.ppermute(near, "head", to_core)
    weights = (query_matrix, key_matrix, value, down)
    shared = (other_rows, patch, gain, *weights)
    near_parts = run(
        near_kernel,
        [((tokens, w.shape[1]), F32) for w in weights],
        (near, *shared),
        flops=partial_flops // 2,
    )
    other_sent, other_kept = run(
        far_kernel,
        [((tokens, 7 * columns), BF16), ((tokens, 4 * columns), F32)],
        (far, *shared, *near_parts),
        flops=partial_flops // 2,
    )
    other_got = lax.ppermute(other_sent, "seq", to_x)
    (lora,) = run(lora_kernel, [((share, rank), BF16)], (other_kept, own_got))
    lora_far = lax.ppermute(lora, "head", to_core)
    half_set, mixes = run(
        half_kernel,
        [((4, tokens, columns), BF16), ((2, columns, 2 * channels), BF16)],
        (
            other_kept, own_got, lora, lora_far, adapter_query_up, mix_part,
            adapter_output_down, readout_of_up,
        ),
    )
    sent, stay = run(
        attention_kernel,
        [((tokens, 2 * channels), F32)] * 2,
        (own_kept, other_got, adapter_query_up, half_set, mixes, base),
        scratch=[
            pltpu.VMEM((4, 2 * tokens, columns), BF16),
            pltpu.VMEM((2 * tokens, 2 * channels), F32),
        ],
    )

    got = lax.ppermute(sent, "head", to_core)
    packed = ((share + share // 2, 2 * channels), BF16)
    same, cross = run(pack_kernel, [packed, packed], (stay, got))
    from_x = lax.ppermute(cross, "seq", to_x)
    from_y = lax.ppermute(same, "head", to_y)
    from_xy = lax.ppermute(cross, ("seq", "head"), to_xy)
    total = (same.astype(F32) + from_y.astype(F32)) + (
        from_x.astype(F32) + from_xy.astype(F32)
    )
    total = total.astype(BF16)
    totals = [total]
    for k in range(1, groups):
        to_group = pairs((groups,), lambda g, k=k: (g ^ k,))
        totals.append(lax.ppermute(total, "group", to_group))
    (packet,) = run(error_kernel, [((share // 2 + 8, 2 * channels), F32)], totals)
    answer = lax.ppermute(packet, "head", to_core)
    (out,) = run(
        last_kernel,
        [((channels, tokens), F32)],
        (packet, answer),
        scratch=[pltpu.VMEM((tokens, 2 * channels), F32)],
    )
    return out.T


def gathered_local(
    latents,
    noise,
    step,
    stream,
    patch_embed_weight,
    prenorm_gain_vector,
    query_matrix,
    key_matrix,
    value_matrix,
    output_matrix,
    velocity_readout_weight,
    adapter_query_down,
    adapter_query_up,
    adapter_output_down,
    adapter_output_up,
):
    tokens = latents.shape[0]
    width = query_matrix.shape[1]
    local_heads = width // HEAD_SIZE
    channels = velocity_readout_weight.shape[0]
    sigma = noise_level(step)
    noisy = (
        (1.0 - sigma) * latents.astype(F32) + sigma * noise.astype(F32)
    ).astype(BF16)
    hidden = (stream.astype(F32) + dot(noisy, patch_embed_weight)).astype(BF16)
    hidden_wide = hidden.astype(F32)
    normed = (
        hidden_wide
        * lax.rsqrt(jnp.mean(hidden_wide * hidden_wide, axis=-1, keepdims=True) + 1e-06)
        * prenorm_gain_vector
    ).astype(BF16)
    base_query, keys, values, lora_hidden = (
        dot(normed, lax.all_gather(piece, "seq", axis=0, tiled=True))
        for piece in (query_matrix, key_matrix, value_matrix, adapter_query_down)
    )
    scale = HEAD_SIZE ** (-0.5)
    lora_delta = dot(lora_hidden.astype(BF16), adapter_query_up)
    queries = (base_query * scale).astype(BF16)
    fake_queries = ((base_query + lora_delta) * scale).astype(BF16)
    both_sets = jnp.stack([queries, fake_queries]).reshape(2, tokens, local_heads, HEAD_SIZE)
    key_rows = lax.all_gather(keys.astype(BF16), "seq", axis=0, tiled=True)
    value_rows = lax.all_gather(values.astype(BF16), "seq", axis=0, tiled=True)
    key_rows = key_rows.reshape(-1, local_heads, HEAD_SIZE)
    value_rows = value_rows.reshape(-1, local_heads, HEAD_SIZE)
    scores = jnp.einsum("sthd,khd->shtk", both_sets, key_rows, preferred_element_type=F32)
    weights = jnp.exp(scores - jnp.max(scores, axis=-1, keepdims=True))
    mass = jnp.sum(weights, axis=-1)
    added = jnp.einsum(
        "shtk,khd->sthd", weights.astype(BF16), value_rows, preferred_element_type=F32
    )
    attn = (added / mass.transpose(0, 2, 1)[..., None]).astype(BF16).reshape(2, tokens, width)
    columns = output_matrix.shape[1]
    readout_part = columns_of(velocity_readout_weight, lax.axis_index("seq"), columns)
    mix_full = lax.psum(contract_final_axis(output_matrix, readout_part), "seq")
    lora_readout = contract_final_axis(adapter_output_up, velocity_readout_weight).astype(BF16)
    fake_mix = (mix_full + dot(adapter_output_down, lora_readout)).astype(BF16)
    real_sum, fake_sum = lax.psum(
        (dot(attn[0], mix_full.astype(BF16)), dot(attn[1], fake_mix)), ("group", "head")
    )
    base = contract_final_axis(hidden, velocity_readout_weight)
    noisy_wide = noisy.astype(F32)
    x0_real = noisy_wide - sigma * (base + real_sum)
    x0_fake = noisy_wide - sigma * (base + fake_sum)
    local_error = jnp.sum(jnp.abs(latents.astype(F32) - x0_real))
    weight = lax.psum(local_error, "seq") / (tokens * lax.axis_size("seq") * channels)
    return (x0_fake - x0_real) / weight


def solution(mesh):
    sizes = tuple(mesh.shape[name] for name in ("group", "seq", "head"))

    def local(*args):
        query_columns = args[6].shape[1]
        power = sizes[0] & (sizes[0] - 1) == 0
        paired = sizes[1] == 2 and sizes[2] == 4 and power
        if paired and (query_columns // HEAD_SIZE) % 2 == 0:
            return paired_local(sizes, *args)
        return gathered_local(*args)

    split = ("group", "head")
    in_specs = (
        P("seq", None),
        P("seq", None),
        P(),
        P("seq", None),
        P(),
        P(),
        P("seq", split),
        P("seq", split),
        P("seq", split),
        P(split, "seq"),
        P(),
        P("seq", None),
        P(None, split),
        P(split, None),
        P(),
    )
    return jax.shard_map(
        local, mesh=mesh, in_specs=in_specs, out_specs=P("seq", None), check_vma=False
    )
```

```python
import itertools

import jax
import jax.numpy as jnp
from jax import lax
from jax.experimental import pallas as pl
from jax.experimental.pallas import tpu as pltpu
from jax.sharding import PartitionSpec as P


HEAD_SIZE = 128
F32 = jnp.float32
BF16 = jnp.bfloat16


def contract_final_axis(left, right):
    return lax.dot_general(
        left, right, (((1,), (1,)), ((), ())), preferred_element_type=F32
    )


def dot(left, right):
    return jnp.dot(left, right, preferred_element_type=F32)


def noise_level(step):
    level = (step[0].astype(F32) + 1.0) / 1000.0
    return 5.0 * level / (1.0 + 4.0 * level)


def pairs(sizes, partner):
    def linear(coordinate):
        index = 0
        for value, size in zip(coordinate, sizes):
            index = index * size + value
        return index

    return [
        (linear(c), linear(partner(*c)))
        for c in itertools.product(*[range(n) for n in sizes])
    ]


def columns_of(x, index, count):
    return lax.dynamic_slice_in_dim(x, index * count, count, 1)


VMEM = pl.BlockSpec(memory_space=pltpu.VMEM)
HBM = pl.BlockSpec(memory_space=pltpu.HBM)


def run(kernel, outs, args, specs=None, scratch=(), flops=0, limit=8 << 20, moved=None):
    shapes = [jax.ShapeDtypeStruct(shape, kind) for shape, kind in outs]
    if moved is None:
        moved = sum(a.size * a.dtype.itemsize for a in (*args, *shapes))
    return pl.pallas_call(
        kernel,
        out_shape=shapes,
        in_specs=specs or [VMEM] * len(args),
        out_specs=[VMEM] * len(shapes),
        scratch_shapes=list(scratch),
        cost_estimate=pl.CostEstimate(flops=flops, bytes_accessed=moved, transcendentals=0),
        compiler_params=pltpu.CompilerParams(vmem_limit_bytes=limit),
    )(*args)


def aligned(index, count):
    return pl.ds(pl.multiple_of(index * count, count), count)


def fold(low, high):
    lane = lax.broadcasted_iota(jnp.int32, low.shape, 1)
    return jnp.where(lane < low.shape[1] // 2, low, high)


def swap_halves(x):
    return pltpu.roll(x, x.shape[1] // 2, 1)


def high_low(x):
    high = x.astype(BF16)
    return high, (x - high.astype(F32)).astype(BF16)


def first_kernel(
    step_any, latents_hbm, noise_hbm, stream_hbm, patch_hbm, gain_hbm, value_hbm,
    normed_ref, rows_ref, gap_ref, hidden_ref, gain_ref, patch_ref, value_ref,
    step_s, latents_v, noise_v, stream_v, patch_v, gain_v, sems,
):
    parts, tokens, quarter = stream_v.shape
    channels = latents_v.shape[0]
    seq = lax.axis_index("seq")
    small = [
        pltpu.make_async_copy(latents_hbm, latents_v, sems.at[0]),
        pltpu.make_async_copy(noise_hbm, noise_v, sems.at[1]),
        pltpu.make_async_copy(step_any, step_s, sems.at[2]),
    ]
    gain_copy = pltpu.make_async_copy(gain_hbm, gain_v, sems.at[3])
    large = []
    for j in range(parts):
        span = pl.ds(j * quarter, quarter)
        large.append([
            pltpu.make_async_copy(source.at[:, span], target.at[j], sems.at[4 + 2 * j + i])
            for i, (source, target) in enumerate(
                ((stream_hbm, stream_v), (patch_hbm, patch_v))
            )
        ])
    for copy in small:
        copy.start()
    for j in range(parts):
        for copy in large[j]:
            copy.start()
    gain_copy.start()
    value_copy = pltpu.make_async_copy(value_hbm, value_ref, sems.at[sems.shape[0] - 1])
    value_copy.start()
    for copy in small:
        copy.wait()
    level = (jnp.full((8, 128), step_s[0], jnp.int32).astype(F32) + 1.0) / 1000.0
    sigma = (5.0 * level / (1.0 + 4.0 * level))[:1, :1]
    latents = latents_v[...].astype(F32)
    noisy = ((1.0 - sigma) * latents + sigma * noise_v[...].astype(F32)).astype(BF16)
    gap_ref[...] = (latents - noisy.astype(F32)) / sigma
    squares = jnp.zeros((tokens, 128), F32)
    for j in range(parts):
        for copy in large[j]:
            copy.wait()
        embedded = lax.dot_general(
            noisy, patch_v[j], (((0,), (0,)), ((), ())), preferred_element_type=F32
        )
        hidden = (stream_v[j].astype(F32) + embedded).astype(BF16)
        hidden_ref[j] = hidden
        wide = hidden.astype(F32)
        wide = wide * wide
        for i in range(quarter // 128):
            squares = squares + wide[:, i * 128 : (i + 1) * 128]
    mean = jnp.sum(squares, axis=1, keepdims=True) / (parts * quarter)
    inverse = lax.rsqrt(mean + 1e-06)
    rows_ref[:channels] = noisy
    scale = jnp.broadcast_to(inverse, (tokens, tokens)).T[:8]
    first, _ = high_low(scale)
    second, third = high_low(scale - first.astype(F32))
    row = lax.broadcasted_iota(jnp.int32, (16, tokens), 0)
    terms = [jnp.concatenate([x.astype(F32)] * 2, axis=0) for x in (first, second, third)]
    terms = jnp.where(row == 0, terms[0], jnp.where(row == 1, terms[1], terms[2]))
    rows_ref[channels:] = terms.astype(BF16)
    gain_copy.wait()
    for j in range(parts):

        @pl.when(seq == j // 2)
        def _(j=j):
            gain = gain_v[j * quarter : (j + 1) * quarter][None, :]
            start = (j % 2) * quarter
            gain_ref[j % 2 : j % 2 + 1] = gain
            patch_ref[j % 2] = patch_v[j]
            normed_ref[:, start : start + quarter] = (
                hidden_ref[j].astype(F32) * inverse * gain
            ).astype(BF16)

    value_copy.wait()


def pick(index, x):
    half = x.shape[1] // 2
    return jnp.where(index == 0, x[:, :half], x[:, half:])


def partial_outputs(parts, seq, lora_blocks, sent_ref, kept_ref):
    q, k, v, lora = parts
    columns = q.shape[1] // 2
    blocks = [*high_low(pick(1 - seq, q)), *high_low(pick(1 - seq, k))]
    blocks += [pick(1 - seq, v).astype(BF16), *lora_blocks]
    for i, block in enumerate(blocks):
        sent_ref[:, i * columns : (i + 1) * columns] = block
    for i, block in enumerate((pick(seq, q), pick(seq, k), pick(seq, v), lora)):
        kept_ref[:, i * columns : (i + 1) * columns] = block


def half_rows(x):
    share = x.shape[0] // 2
    half = jnp.where(lax.axis_index("head") % 2 == 0, x[:share], x[share:])
    return jnp.concatenate(high_low(half), axis=0)


def own_kernel(
    normed_ref, q_ref, k_ref, v_ref, down_hbm, output_hbm, readout_hbm,
    sent_ref, kept_ref, mix_ref, down_v,
    output_v, readout_v, mix_v, sems,
):
    seq = lax.axis_index("seq")
    copies = [
        pltpu.make_async_copy(down_hbm, down_v, sems.at[0]),
        pltpu.make_async_copy(output_hbm, output_v, sems.at[1]),
        pltpu.make_async_copy(
            readout_hbm.at[:, aligned(seq, readout_v.shape[1])], readout_v, sems.at[2]
        ),
    ]
    for copy in copies:
        copy.start()
    normed = normed_ref[...]
    parts = [dot(normed, w[...]) for w in (q_ref, k_ref, v_ref)]
    copies[0].wait()
    lora = dot(normed, down_v[...])
    parts.append(lora)
    partial_outputs(parts, seq, [half_rows(lora)], sent_ref, kept_ref)
    for copy in copies[1:]:
        copy.wait()
    mix_v[...] = contract_final_axis(output_v[...], readout_v[...])
    rows, channels = mix_ref.shape
    theirs = mix_v[aligned(1 - seq, rows), :]
    high = theirs.astype(BF16).astype(F32)
    both = jnp.concatenate([high, theirs - high], axis=1)
    sent_ref[:, -2 * channels :] = both.astype(BF16)
    mix_ref[...] = mix_v[aligned(seq, rows), :]


def side_kernel(hidden_ref, up_ref, readout_ref, gap_ref, readout_of_up_ref, base_ref):
    parts, _, quarter = hidden_ref.shape
    readout_of_up_ref[...] = contract_final_axis(up_ref[...], readout_ref[...]).astype(BF16)
    base = gap_ref[...]
    for j in range(parts):
        base += contract_final_axis(
            readout_ref[:, j * quarter : (j + 1) * quarter], hidden_ref[j]
        )
    once = (lax.axis_index("group") == 0) & (lax.axis_index("head") == 0)
    base_ref[...] = jnp.where(once, base, 0.0).T


def other_parts(part, raw_ref, rows_ref, patch_ref, gain_ref, weights):
    tokens, quarter = raw_ref.shape
    channels = patch_ref.shape[1]
    noisy = rows_ref[:channels]
    terms = rows_ref[channels:].astype(F32)
    scale = (terms[:1] + terms[1:2]) + terms[2:3]
    inverse = jnp.broadcast_to(scale, (tokens, tokens)).T[:, :1]
    embedded = lax.dot_general(
        noisy, patch_ref[part],
        (((0,), (0,)), ((), ())), preferred_element_type=F32,
    )
    hidden = (raw_ref[...].astype(F32) + embedded).astype(BF16).astype(F32)
    normed = (hidden * inverse * gain_ref[pl.ds(part, 1), :]).astype(BF16)
    return [dot(normed, w[aligned(part, quarter), :]) for w in weights]


def near_kernel(raw_ref, rows_ref, patch_ref, gain_ref, q_ref, k_ref, v_ref, down_ref, *outs):
    core = lax.axis_index("head") % 2
    weights = (q_ref, k_ref, v_ref, down_ref)
    parts = other_parts(core, raw_ref, rows_ref, patch_ref, gain_ref, weights)
    for out, part in zip(outs, parts):
        out[...] = part


def far_kernel(
    raw_ref, rows_ref, patch_ref, gain_ref, q_ref, k_ref, v_ref, down_ref,
    near_q_ref, near_k_ref, near_v_ref, near_down_ref,
    small_ref, sent_ref, kept_ref,
):
    core = lax.axis_index("head") % 2
    weights = (q_ref, k_ref, v_ref, down_ref)
    parts = other_parts(1 - core, raw_ref, rows_ref, patch_ref, gain_ref, weights)
    near = (near_q_ref, near_k_ref, near_v_ref, near_down_ref)
    parts = [part + ref[...] for part, ref in zip(parts, near)]
    small_ref[...] = half_rows(parts[3])
    partial_outputs(parts, lax.axis_index("seq"), [], sent_ref, kept_ref)


def finish(kept_ref, got_ref, low_rank):
    columns = low_rank.shape[1]

    def got(i):
        return got_ref[:, i * columns : (i + 1) * columns].astype(F32)

    def kept(i):
        return kept_ref[:, i * columns : (i + 1) * columns]

    scale = HEAD_SIZE ** (-0.5)
    base = kept(0) + (got(0) + got(1))
    return (
        (base * scale).astype(BF16),
        ((base + low_rank) * scale).astype(BF16),
        (kept(1) + (got(2) + got(3))).astype(BF16),
        (kept(2) + got(4)).astype(BF16),
    )


def lora_kernel(own_kept_ref, small_got_ref, other_kept_ref, own_got_ref, lora_ref):
    rank = lora_ref.shape[1]
    share = lora_ref.shape[0] // 2
    core = lax.axis_index("head") % 2
    for i, (kept_ref, got) in enumerate((
        (own_kept_ref, small_got_ref[...]),
        (other_kept_ref, own_got_ref[:, 5 * rank : 6 * rank]),
    )):
        kept = kept_ref[aligned(core, share), kept_ref.shape[1] - rank :]
        got = got.astype(F32)
        lora_ref[i * share : (i + 1) * share] = (
            kept + (got[:share] + got[share:])
        ).astype(BF16)


def half_kernel(
    kept_ref, got_ref, lora_ref, lora_far_ref, up_ref, mix_ref, down_ref,
    readout_of_up_ref, set_ref, mixes_ref, low_rank_ref,
):
    seq = lax.axis_index("seq")
    rows, channels = mix_ref.shape
    up = up_ref[:, aligned(seq, rows)]
    mine, far = lora_ref[...], lora_far_ref[...]
    share = mine.shape[0] // 2
    first = lax.axis_index("head") % 2 == 0
    low, high = jnp.where(first, mine, far), jnp.where(first, far, mine)
    own = jnp.concatenate([low[:share], high[:share]], axis=0)
    other = jnp.concatenate([low[share:], high[share:]], axis=0)
    low_rank_ref[...] = dot(own, up)
    for i, block in enumerate(finish(kept_ref, got_ref, dot(other, up))):
        set_ref[i] = block
    got = got_ref[:, -2 * channels :].astype(F32)
    mix_full = mix_ref[...] + (got[:, :channels] + swap_halves(got)[:, :channels])
    low_rank = dot(down_ref[aligned(seq, rows), :], readout_of_up_ref[...])
    mix = mix_full.astype(BF16).astype(F32)
    fake = (mix_full + low_rank).astype(BF16).astype(F32)
    mixes_ref[0] = jnp.concatenate([mix, -mix], axis=1).astype(BF16)
    mixes_ref[1] = jnp.concatenate([jnp.zeros_like(fake), fake], axis=1).astype(BF16)


def attention_kernel(
    kept_ref, got_ref, low_rank_ref, set_ref, mixes_ref, base_ref,
    sent_ref, stay_ref, sets_v, terms_v,
):
    core = lax.axis_index("head") % 2
    tokens, channels = base_ref.shape
    columns = set_ref.shape[2]
    for i, block in enumerate(finish(kept_ref, got_ref, low_rank_ref[...])):
        sets_v[i, :tokens] = block
        sets_v[i, tokens:] = set_ref[i]
    terms = jnp.zeros(terms_v.shape, F32)
    for start in range(0, columns, HEAD_SIZE):
        span = slice(start, start + HEAD_SIZE)
        keys, values = sets_v[2, :, span], sets_v[3, :, span]
        for kind in range(2):
            scores = contract_final_axis(sets_v[kind, :, span], keys)
            top = jnp.max(scores, axis=1, keepdims=True)
            probs = jnp.exp(scores - top)
            mass = jnp.sum(probs, axis=1, keepdims=True)
            attn = (dot(probs.astype(BF16), values) / mass).astype(BF16)
            terms = terms + dot(attn, mixes_ref[kind, span, :])
    terms_v[...] = terms
    terms_v[:tokens, :channels] = terms[:tokens, :channels] + base_ref[...]
    share = tokens // 2
    sent_ref[:share] = terms_v[aligned(1 - core, share), :]
    sent_ref[share:] = terms_v[aligned(3 - core, share), :]
    stay_ref[:share] = terms_v[aligned(core, share), :]
    stay_ref[share:] = terms_v[aligned(2 + core, share), :]


def pack_kernel(stay_ref, got_ref, same_ref, cross_ref):
    share = stay_ref.shape[0] // 2
    mine = stay_ref[:share] + got_ref[:share]
    theirs = stay_ref[share:] + got_ref[share:]
    half = share // 2
    same_ref[:share] = mine.astype(BF16)
    same_ref[share:] = fold(theirs[:half], swap_halves(theirs[half:])).astype(BF16)
    cross_ref[:share] = theirs.astype(BF16)
    cross_ref[share:] = fold(mine[:half], swap_halves(mine[half:])).astype(BF16)


def error_kernel(*refs):
    *parts, packet_ref = refs
    parts = [ref[...].astype(F32) for ref in parts]
    while len(parts) > 1:
        parts = [a + b for a, b in zip(parts[::2], parts[1::2])]
    total = parts[0]
    half = packet_ref.shape[0] - 8
    share = 2 * half
    own = jnp.abs(total[:half]) + jnp.abs(total[half:share])
    own = fold(own, jnp.zeros_like(own)) + jnp.abs(total[share:])
    packet_ref[:half] = fold(swap_halves(total[:half]), total[half:share])
    packet_ref[half:] = jnp.full((8, packet_ref.shape[1]), jnp.sum(own), F32)


def last_kernel(mine_ref, theirs_ref, out_ref, both_v):
    core = lax.axis_index("head") % 2
    channels, tokens = out_ref.shape
    share = tokens // 2
    half = share // 2
    weight = (mine_ref[half:] + theirs_ref[half:]) / (2 * tokens * channels)
    weight = weight[:1, :1]
    for ref, index in ((mine_ref, core), (theirs_ref, 1 - core)):
        packet = -ref[:half] / weight
        start = pl.multiple_of(index * share, share)
        both_v[pl.ds(start, half)] = packet
        both_v[pl.ds(start + half, half)] = swap_halves(packet)
    out_ref[...] = both_v[...].T[:channels]


def paired_local(
    sizes,
    latents,
    noise,
    step,
    stream,
    patch_embed_weight,
    prenorm_gain_vector,
    query_matrix,
    key_matrix,
    value_matrix,
    output_matrix,
    velocity_readout_weight,
    adapter_query_down,
    adapter_query_up,
    adapter_output_down,
    adapter_output_up,
):
    groups, _, heads = sizes
    tokens, channels = latents.shape
    half_width, local_columns = query_matrix.shape
    quarter = half_width // 2
    columns = local_columns // 2
    rank = adapter_query_down.shape[1]
    share = tokens // 2
    to_x = pairs((2,), lambda s: (s ^ 1,))
    to_core = pairs((heads,), lambda h: (h ^ 1,))
    to_y = pairs((heads,), lambda h: (h ^ 2,))
    to_xy = pairs((2, heads), lambda s, h: (s ^ 1, h ^ 2))
    partial_flops = 2 * tokens * half_width * (3 * local_columns + rank)

    target = (1 - lax.axis_index("seq")) * 2 + lax.axis_index("head") % 2
    message = columns_of(stream, target, quarter)
    near = lax.ppermute(message, "seq", to_x)
    inputs = (
        latents.T, noise.T, stream, patch_embed_weight, prenorm_gain_vector, value_matrix,
    )
    normed, rows, gap, hidden, gain, patch, value = run(
        first_kernel,
        [
            ((tokens, half_width), BF16),
            ((channels + 16, tokens), BF16),
            ((channels, tokens), F32),
            ((4, tokens, quarter), BF16),
            ((2, quarter), F32),
            ((2, channels, quarter), BF16),
            (value_matrix.shape, BF16),
        ],
        [step, *(pltpu.with_memory_space_constraint(x, pltpu.HBM) for x in inputs)],
        [pl.BlockSpec(memory_space=pl.ANY)] + [HBM] * 6,
        [
            pltpu.SMEM((1,), jnp.int32),
            pltpu.VMEM((channels, tokens), BF16),
            pltpu.VMEM((channels, tokens), BF16),
            pltpu.VMEM((4, tokens, quarter), BF16),
            pltpu.VMEM((4, channels, quarter), BF16),
            pltpu.VMEM((4 * quarter,), F32),
            pltpu.SemaphoreType.DMA((5 + 2 * 4,)),
        ],
    )
    other_rows = lax.ppermute(rows, "seq", to_x)
    own_sent, own_kept, mix_part, down = run(
        own_kernel,
        [
            ((tokens, 6 * columns + 2 * channels), BF16),
            ((tokens, 4 * columns), F32),
            ((columns, channels), F32),
            (adapter_query_down.shape, BF16),
        ],
        (
            normed, query_matrix, key_matrix, value,
            *(
                pltpu.with_memory_space_constraint(x, pltpu.HBM)
                for x in (adapter_query_down, output_matrix, velocity_readout_weight)
            ),
        ),
        [VMEM] * 4 + [HBM] * 3,
        scratch=[
            pltpu.VMEM(output_matrix.shape, BF16),
            pltpu.VMEM((channels, half_width), BF16),
            pltpu.VMEM((local_columns, channels), F32),
            pltpu.SemaphoreType.DMA((3,)),
        ],
        flops=partial_flops,
    )
    own_got = lax.ppermute(own_sent, "seq", to_x)
    readout_of_up, base = run(
        side_kernel,
        [((rank, channels), BF16), ((tokens, channels), F32)],
        (hidden, adapter_output_up, velocity_readout_weight, gap),
        flops=8 * tokens * half_width * channels,
    )
    far = lax.ppermute(near, "head", to_core)
    weights = (query_matrix, key_matrix, value, down)
    shared = (other_rows, patch, gain, *weights)
    near_parts = run(
        near_kernel,
        [((tokens, w.shape[1]), F32) for w in weights],
        (near, *shared),
        flops=partial_flops // 2,
    )
    small_sent, other_sent, other_kept = run(
        far_kernel,
        [
            ((tokens, rank), BF16),
            ((tokens, 5 * columns), BF16),
            ((tokens, 4 * columns), F32),
        ],
        (far, *shared, *near_parts),
        flops=partial_flops // 2,
    )
    small_got = lax.ppermute(small_sent, "seq", to_x)
    other_got = lax.ppermute(other_sent, "seq", to_x)
    (lora,) = run(lora_kernel, [((tokens, rank), BF16)], (own_kept, small_got, other_kept, own_got))
    lora_far = lax.ppermute(lora, "head", to_core)
    half_set, mixes, low_rank = run(
        half_kernel,
        [
            ((4, tokens, columns), BF16),
            ((2, columns, 2 * channels), BF16),
            ((tokens, columns), F32),
        ],
        (
            other_kept, own_got, lora, lora_far, adapter_query_up, mix_part,
            adapter_output_down, readout_of_up,
        ),
    )
    sent, stay = run(
        attention_kernel,
        [((tokens, 2 * channels), F32)] * 2,
        (own_kept, other_got, low_rank, half_set, mixes, base),
        scratch=[
            pltpu.VMEM((4, 2 * tokens, columns), BF16),
            pltpu.VMEM((2 * tokens, 2 * channels), F32),
        ],
    )

    got = lax.ppermute(sent, "head", to_core)
    packed = ((share + share // 2, 2 * channels), BF16)
    same, cross = run(pack_kernel, [packed, packed], (stay, got))
    from_x = lax.ppermute(cross, "seq", to_x)
    from_y = lax.ppermute(same, "head", to_y)
    from_xy = lax.ppermute(cross, ("seq", "head"), to_xy)
    total = (same.astype(F32) + from_y.astype(F32)) + (
        from_x.astype(F32) + from_xy.astype(F32)
    )
    total = total.astype(BF16)
    totals = [total]
    for k in range(1, groups):
        to_group = pairs((groups,), lambda g, k=k: (g ^ k,))
        totals.append(lax.ppermute(total, "group", to_group))
    (packet,) = run(error_kernel, [((share // 2 + 8, 2 * channels), F32)], totals)
    answer = lax.ppermute(packet, "head", to_core)
    (out,) = run(
        last_kernel,
        [((channels, tokens), F32)],
        (packet, answer),
        scratch=[pltpu.VMEM((tokens, 2 * channels), F32)],
    )
    return out.T


def gathered_local(
    latents,
    noise,
    step,
    stream,
    patch_embed_weight,
    prenorm_gain_vector,
    query_matrix,
    key_matrix,
    value_matrix,
    output_matrix,
    velocity_readout_weight,
    adapter_query_down,
    adapter_query_up,
    adapter_output_down,
    adapter_output_up,
):
    tokens = latents.shape[0]
    width = query_matrix.shape[1]
    local_heads = width // HEAD_SIZE
    channels = velocity_readout_weight.shape[0]
    sigma = noise_level(step)
    noisy = (
        (1.0 - sigma) * latents.astype(F32) + sigma * noise.astype(F32)
    ).astype(BF16)
    hidden = (stream.astype(F32) + dot(noisy, patch_embed_weight)).astype(BF16)
    hidden_wide = hidden.astype(F32)
    normed = (
        hidden_wide
        * lax.rsqrt(jnp.mean(hidden_wide * hidden_wide, axis=-1, keepdims=True) + 1e-06)
        * prenorm_gain_vector
    ).astype(BF16)
    base_query, keys, values, lora_hidden = (
        dot(normed, lax.all_gather(piece, "seq", axis=0, tiled=True))
        for piece in (query_matrix, key_matrix, value_matrix, adapter_query_down)
    )
    scale = HEAD_SIZE ** (-0.5)
    lora_delta = dot(lora_hidden.astype(BF16), adapter_query_up)
    queries = (base_query * scale).astype(BF16)
    fake_queries = ((base_query + lora_delta) * scale).astype(BF16)
    both_sets = jnp.stack([queries, fake_queries]).reshape(2, tokens, local_heads, HEAD_SIZE)
    key_rows = lax.all_gather(keys.astype(BF16), "seq", axis=0, tiled=True)
    value_rows = lax.all_gather(values.astype(BF16), "seq", axis=0, tiled=True)
    key_rows = key_rows.reshape(-1, local_heads, HEAD_SIZE)
    value_rows = value_rows.reshape(-1, local_heads, HEAD_SIZE)
    scores = jnp.einsum("sthd,khd->shtk", both_sets, key_rows, preferred_element_type=F32)
    weights = jnp.exp(scores - jnp.max(scores, axis=-1, keepdims=True))
    mass = jnp.sum(weights, axis=-1)
    added = jnp.einsum(
        "shtk,khd->sthd", weights.astype(BF16), value_rows, preferred_element_type=F32
    )
    attn = (added / mass.transpose(0, 2, 1)[..., None]).astype(BF16).reshape(2, tokens, width)
    columns = output_matrix.shape[1]
    readout_part = columns_of(velocity_readout_weight, lax.axis_index("seq"), columns)
    mix_full = lax.psum(contract_final_axis(output_matrix, readout_part), "seq")
    lora_readout = contract_final_axis(adapter_output_up, velocity_readout_weight).astype(BF16)
    fake_mix = (mix_full + dot(adapter_output_down, lora_readout)).astype(BF16)
    real_sum, fake_sum = lax.psum(
        (dot(attn[0], mix_full.astype(BF16)), dot(attn[1], fake_mix)), ("group", "head")
    )
    base = contract_final_axis(hidden, velocity_readout_weight)
    noisy_wide = noisy.astype(F32)
    x0_real = noisy_wide - sigma * (base + real_sum)
    x0_fake = noisy_wide - sigma * (base + fake_sum)
    local_error = jnp.sum(jnp.abs(latents.astype(F32) - x0_real))
    weight = lax.psum(local_error, "seq") / (tokens * lax.axis_size("seq") * channels)
    return (x0_fake - x0_real) / weight


def solution(mesh):
    sizes = tuple(mesh.shape[name] for name in ("group", "seq", "head"))

    def local(*args):
        query_columns = args[6].shape[1]
        power = sizes[0] & (sizes[0] - 1) == 0
        paired = sizes[1] == 2 and sizes[2] == 4 and power
        paired = paired and args[0].shape[0] == query_columns // 2
        if paired and (query_columns // HEAD_SIZE) % 2 == 0:
            return paired_local(sizes, *args)
        return gathered_local(*args)

    split = ("group", "head")
    in_specs = (
        P("seq", None),
        P("seq", None),
        P(),
        P("seq", None),
        P(),
        P(),
        P("seq", split),
        P("seq", split),
        P("seq", split),
        P(split, "seq"),
        P(),
        P("seq", None),
        P(None, split),
        P(split, None),
        P(),
    )
    return jax.shard_map(
        local, mesh=mesh, in_specs=in_specs, out_specs=P("seq", None), check_vma=False
    )
```

```python
import itertools

import jax
import jax.numpy as jnp
from jax import lax
from jax.experimental import pallas as pl
from jax.experimental.pallas import tpu as pltpu
from jax.sharding import PartitionSpec as P


HEAD_SIZE = 128
F32 = jnp.float32
BF16 = jnp.bfloat16


def contract_final_axis(left, right):
    return lax.dot_general(
        left, right, (((1,), (1,)), ((), ())), preferred_element_type=F32
    )


def dot(left, right):
    return jnp.dot(left, right, preferred_element_type=F32)


def noise_level(step):
    level = (step[0].astype(F32) + 1.0) / 1000.0
    return 5.0 * level / (1.0 + 4.0 * level)


def pairs(sizes, partner):
    def linear(coordinate):
        index = 0
        for value, size in zip(coordinate, sizes):
            index = index * size + value
        return index

    return [
        (linear(c), linear(partner(*c)))
        for c in itertools.product(*[range(n) for n in sizes])
    ]


def columns_of(x, index, count):
    return lax.dynamic_slice_in_dim(x, index * count, count, 1)


VMEM = pl.BlockSpec(memory_space=pltpu.VMEM)
HBM = pl.BlockSpec(memory_space=pltpu.HBM)


def run(kernel, outs, args, specs=None, scratch=(), flops=0, limit=8 << 20, moved=None):
    shapes = [jax.ShapeDtypeStruct(shape, kind) for shape, kind in outs]
    if moved is None:
        moved = sum(a.size * a.dtype.itemsize for a in (*args, *shapes))
    return pl.pallas_call(
        kernel,
        out_shape=shapes,
        in_specs=specs or [VMEM] * len(args),
        out_specs=[VMEM] * len(shapes),
        scratch_shapes=list(scratch),
        cost_estimate=pl.CostEstimate(flops=flops, bytes_accessed=moved, transcendentals=0),
        compiler_params=pltpu.CompilerParams(vmem_limit_bytes=limit),
    )(*args)


def aligned(index, count):
    return pl.ds(pl.multiple_of(index * count, count), count)


def fold(low, high):
    lane = lax.broadcasted_iota(jnp.int32, low.shape, 1)
    return jnp.where(lane < low.shape[1] // 2, low, high)


def swap_halves(x):
    return pltpu.roll(x, x.shape[1] // 2, 1)


def high_low(x):
    high = x.astype(BF16)
    return high, (x - high.astype(F32)).astype(BF16)


def first_kernel(
    step_any, latents_hbm, noise_hbm, stream_hbm, patch_hbm, gain_hbm, value_hbm,
    normed_ref, rows_ref, gap_ref, hidden_ref, gain_ref, patch_ref, value_ref,
    step_s, latents_v, noise_v, stream_v, patch_v, gain_v, sems,
):
    parts, tokens, quarter = stream_v.shape
    channels = latents_v.shape[0]
    seq = lax.axis_index("seq")
    small = [
        pltpu.make_async_copy(latents_hbm, latents_v, sems.at[0]),
        pltpu.make_async_copy(noise_hbm, noise_v, sems.at[1]),
        pltpu.make_async_copy(step_any, step_s, sems.at[2]),
    ]
    gain_copy = pltpu.make_async_copy(gain_hbm, gain_v, sems.at[3])
    large = []
    for j in range(parts):
        span = pl.ds(j * quarter, quarter)
        large.append([
            pltpu.make_async_copy(source.at[:, span], target.at[j], sems.at[4 + 2 * j + i])
            for i, (source, target) in enumerate(
                ((stream_hbm, stream_v), (patch_hbm, patch_v))
            )
        ])
    for copy in small:
        copy.start()
    for j in range(parts):
        for copy in large[j]:
            copy.start()
    gain_copy.start()
    value_copy = pltpu.make_async_copy(value_hbm, value_ref, sems.at[sems.shape[0] - 1])
    value_copy.start()
    for copy in small:
        copy.wait()
    level = (jnp.full((8, 128), step_s[0], jnp.int32).astype(F32) + 1.0) / 1000.0
    sigma = (5.0 * level / (1.0 + 4.0 * level))[:1, :1]
    latents = latents_v[...].astype(F32)
    noisy = ((1.0 - sigma) * latents + sigma * noise_v[...].astype(F32)).astype(BF16)
    gap_ref[...] = (latents - noisy.astype(F32)) / sigma
    squares = jnp.zeros((tokens, 128), F32)
    for j in range(parts):
        for copy in large[j]:
            copy.wait()
        embedded = lax.dot_general(
            noisy, patch_v[j], (((0,), (0,)), ((), ())), preferred_element_type=F32
        )
        hidden = (stream_v[j].astype(F32) + embedded).astype(BF16)
        hidden_ref[j] = hidden
        wide = hidden.astype(F32)
        wide = wide * wide
        for i in range(quarter // 128):
            squares = squares + wide[:, i * 128 : (i + 1) * 128]
    mean = jnp.sum(squares, axis=1, keepdims=True) / (parts * quarter)
    inverse = lax.rsqrt(mean + 1e-06)
    rows_ref[:channels] = noisy
    scale = jnp.broadcast_to(inverse, (tokens, tokens)).T[:8]
    first, _ = high_low(scale)
    second, third = high_low(scale - first.astype(F32))
    row = lax.broadcasted_iota(jnp.int32, (16, tokens), 0)
    terms = [jnp.concatenate([x.astype(F32)] * 2, axis=0) for x in (first, second, third)]
    terms = jnp.where(row == 0, terms[0], jnp.where(row == 1, terms[1], terms[2]))
    rows_ref[channels:] = terms.astype(BF16)
    gain_copy.wait()
    for j in range(parts):

        @pl.when(seq == j // 2)
        def _(j=j):
            gain = gain_v[j * quarter : (j + 1) * quarter][None, :]
            start = (j % 2) * quarter
            gain_ref[j % 2 : j % 2 + 1] = gain
            patch_ref[j % 2] = patch_v[j]
            normed_ref[:, start : start + quarter] = (
                hidden_ref[j].astype(F32) * inverse * gain
            ).astype(BF16)

    value_copy.wait()


def pick(index, x):
    half = x.shape[1] // 2
    return jnp.where(index == 0, x[:, :half], x[:, half:])


def partial_outputs(parts, seq, lora_blocks, sent_ref, kept_ref):
    q, k, v, lora = parts
    columns = q.shape[1] // 2
    blocks = [*high_low(pick(1 - seq, q)), *high_low(pick(1 - seq, k))]
    blocks += [pick(1 - seq, v).astype(BF16), *lora_blocks]
    for i, block in enumerate(blocks):
        sent_ref[:, i * columns : (i + 1) * columns] = block
    for i, block in enumerate((pick(seq, q), pick(seq, k), pick(seq, v), lora)):
        kept_ref[:, i * columns : (i + 1) * columns] = block


def half_rows(x):
    share = x.shape[0] // 2
    half = jnp.where(lax.axis_index("head") % 2 == 0, x[:share], x[share:])
    return jnp.concatenate(high_low(half), axis=0)


def own_kernel(
    normed_ref, q_ref, k_ref, v_ref, down_hbm, output_hbm, readout_hbm,
    sent_ref, kept_ref, mix_ref, down_v,
    output_v, readout_v, mix_v, sems,
):
    seq = lax.axis_index("seq")
    copies = [
        pltpu.make_async_copy(down_hbm, down_v, sems.at[0]),
        pltpu.make_async_copy(output_hbm, output_v, sems.at[1]),
        pltpu.make_async_copy(
            readout_hbm.at[:, aligned(seq, readout_v.shape[1])], readout_v, sems.at[2]
        ),
    ]
    for copy in copies:
        copy.start()
    normed = normed_ref[...]
    parts = [dot(normed, w[...]) for w in (q_ref, k_ref, v_ref)]
    copies[0].wait()
    lora = dot(normed, down_v[...])
    parts.append(lora)
    partial_outputs(parts, seq, [half_rows(lora)], sent_ref, kept_ref)
    for copy in copies[1:]:
        copy.wait()
    mix_v[...] = contract_final_axis(output_v[...], readout_v[...])
    rows, channels = mix_ref.shape
    theirs = mix_v[aligned(1 - seq, rows), :]
    high = theirs.astype(BF16).astype(F32)
    both = jnp.concatenate([high, theirs - high], axis=1)
    sent_ref[:, -2 * channels :] = both.astype(BF16)
    mix_ref[...] = mix_v[aligned(seq, rows), :]


def side_kernel(hidden_ref, up_ref, readout_ref, gap_ref, readout_of_up_ref, base_ref):
    parts, _, quarter = hidden_ref.shape
    readout_of_up_ref[...] = contract_final_axis(up_ref[...], readout_ref[...]).astype(BF16)
    base = gap_ref[...]
    for j in range(parts):
        base += contract_final_axis(
            readout_ref[:, j * quarter : (j + 1) * quarter], hidden_ref[j]
        )
    once = (lax.axis_index("group") == 0) & (lax.axis_index("head") == 0)
    base_ref[...] = jnp.where(once, base, 0.0).T


def other_parts(part, raw_ref, rows_ref, patch_ref, gain_ref, weights):
    tokens, quarter = raw_ref.shape
    channels = patch_ref.shape[1]
    noisy = rows_ref[:channels]
    terms = rows_ref[channels:].astype(F32)
    scale = (terms[:1] + terms[1:2]) + terms[2:3]
    inverse = jnp.broadcast_to(scale, (tokens, tokens)).T[:, :1]
    embedded = lax.dot_general(
        noisy, patch_ref[part],
        (((0,), (0,)), ((), ())), preferred_element_type=F32,
    )
    hidden = (raw_ref[...].astype(F32) + embedded).astype(BF16).astype(F32)
    normed = (hidden * inverse * gain_ref[pl.ds(part, 1), :]).astype(BF16)
    return [dot(normed, w[aligned(part, quarter), :]) for w in weights]


def near_kernel(raw_ref, rows_ref, patch_ref, gain_ref, q_ref, k_ref, v_ref, down_ref, *outs):
    core = lax.axis_index("head") % 2
    weights = (q_ref, k_ref, v_ref, down_ref)
    parts = other_parts(core, raw_ref, rows_ref, patch_ref, gain_ref, weights)
    for out, part in zip(outs, parts):
        out[...] = part


def far_kernel(
    raw_ref, rows_ref, patch_ref, gain_ref, q_ref, k_ref, v_ref, down_ref,
    near_q_ref, near_k_ref, near_v_ref, near_down_ref,
    small_ref, sent_ref, kept_ref,
):
    core = lax.axis_index("head") % 2
    weights = (q_ref, k_ref, v_ref, down_ref)
    parts = other_parts(1 - core, raw_ref, rows_ref, patch_ref, gain_ref, weights)
    near = (near_q_ref, near_k_ref, near_v_ref, near_down_ref)
    parts = [part + ref[...] for part, ref in zip(parts, near)]
    small_ref[...] = half_rows(parts[3])
    partial_outputs(parts, lax.axis_index("seq"), [], sent_ref, kept_ref)


def finish(kept_ref, got_ref, low_rank):
    columns = low_rank.shape[1]

    def got(i):
        return got_ref[:, i * columns : (i + 1) * columns].astype(F32)

    def kept(i):
        return kept_ref[:, i * columns : (i + 1) * columns]

    scale = HEAD_SIZE ** (-0.5)
    base = kept(0) + (got(0) + got(1))
    return (
        (base * scale).astype(BF16),
        ((base + low_rank) * scale).astype(BF16),
        (kept(1) + (got(2) + got(3))).astype(BF16),
        (kept(2) + got(4)).astype(BF16),
    )


def lora_kernel(own_kept_ref, small_got_ref, other_kept_ref, own_got_ref, lora_ref):
    rank = lora_ref.shape[1]
    share = lora_ref.shape[0] // 2
    core = lax.axis_index("head") % 2
    for i, (kept_ref, got) in enumerate((
        (own_kept_ref, small_got_ref[...]),
        (other_kept_ref, own_got_ref[:, 5 * rank : 6 * rank]),
    )):
        kept = kept_ref[aligned(core, share), kept_ref.shape[1] - rank :]
        got = got.astype(F32)
        lora_ref[i * share : (i + 1) * share] = (
            kept + (got[:share] + got[share:])
        ).astype(BF16)


def half_kernel(
    kept_ref, got_ref, lora_ref, lora_far_ref, up_ref, mix_ref, down_ref,
    readout_of_up_ref, set_ref, mixes_ref, low_rank_ref,
):
    seq = lax.axis_index("seq")
    rows, channels = mix_ref.shape
    up = up_ref[:, aligned(seq, rows)]
    mine, far = lora_ref[...], lora_far_ref[...]
    share = mine.shape[0] // 2
    first = lax.axis_index("head") % 2 == 0
    low, high = jnp.where(first, mine, far), jnp.where(first, far, mine)
    own = jnp.concatenate([low[:share], high[:share]], axis=0)
    other = jnp.concatenate([low[share:], high[share:]], axis=0)
    low_rank_ref[...] = dot(own, up)
    for i, block in enumerate(finish(kept_ref, got_ref, dot(other, up))):
        set_ref[i] = block
    got = got_ref[:, -2 * channels :].astype(F32)
    mix_full = mix_ref[...] + (got[:, :channels] + swap_halves(got)[:, :channels])
    low_rank = dot(down_ref[aligned(seq, rows), :], readout_of_up_ref[...])
    mix = mix_full.astype(BF16).astype(F32)
    fake = (mix_full + low_rank).astype(BF16).astype(F32)
    mixes_ref[0] = jnp.concatenate([mix, -mix], axis=1).astype(BF16)
    mixes_ref[1] = jnp.concatenate([jnp.zeros_like(fake), fake], axis=1).astype(BF16)


def attention_kernel(
    kept_ref, got_ref, low_rank_ref, set_ref, mixes_ref, base_ref,
    sent_ref, stay_ref, sets_v, terms_v,
):
    core = lax.axis_index("head") % 2
    tokens, channels = base_ref.shape
    columns = set_ref.shape[2]
    for i, block in enumerate(finish(kept_ref, got_ref, low_rank_ref[...])):
        sets_v[i, :tokens] = block
        sets_v[i, tokens:] = set_ref[i]
    terms = jnp.zeros(terms_v.shape, F32)
    rows = 2 * tokens
    for start in range(0, columns, HEAD_SIZE):
        span = slice(start, start + HEAD_SIZE)
        queries = jnp.concatenate([sets_v[0, :, span], sets_v[1, :, span]], axis=0)
        scores = contract_final_axis(queries, sets_v[2, :, span])
        probs = jnp.exp(scores - jnp.max(scores, axis=1, keepdims=True))
        mass = jnp.sum(probs, axis=1, keepdims=True)
        attn = (dot(probs.astype(BF16), sets_v[3, :, span]) * (1.0 / mass)).astype(BF16)
        attn = jnp.concatenate([attn[:rows], attn[rows:]], axis=1)
        mixes = jnp.concatenate([mixes_ref[0, span, :], mixes_ref[1, span, :]], axis=0)
        terms = terms + dot(attn, mixes)
    terms_v[...] = terms
    terms_v[:tokens, :channels] = terms[:tokens, :channels] + base_ref[...]
    share = tokens // 2
    sent_ref[:share] = terms_v[aligned(1 - core, share), :]
    sent_ref[share:] = terms_v[aligned(3 - core, share), :]
    stay_ref[:share] = terms_v[aligned(core, share), :]
    stay_ref[share:] = terms_v[aligned(2 + core, share), :]


def pack_kernel(stay_ref, got_ref, same_ref, cross_ref):
    share = stay_ref.shape[0] // 2
    mine = stay_ref[:share] + got_ref[:share]
    theirs = stay_ref[share:] + got_ref[share:]
    half = share // 2
    same_ref[:share] = mine.astype(BF16)
    same_ref[share:] = fold(theirs[:half], swap_halves(theirs[half:])).astype(BF16)
    cross_ref[:share] = theirs.astype(BF16)
    cross_ref[share:] = fold(mine[:half], swap_halves(mine[half:])).astype(BF16)


def error_kernel(*refs):
    *parts, packet_ref = refs
    parts = [ref[...].astype(F32) for ref in parts]
    while len(parts) > 1:
        parts = [a + b for a, b in zip(parts[::2], parts[1::2])]
    total = parts[0]
    half = packet_ref.shape[0] - 8
    share = 2 * half
    own = jnp.abs(total[:half]) + jnp.abs(total[half:share])
    own = fold(own, jnp.zeros_like(own)) + jnp.abs(total[share:])
    packet_ref[:half] = fold(swap_halves(total[:half]), total[half:share])
    packet_ref[half:] = jnp.full((8, packet_ref.shape[1]), jnp.sum(own), F32)


def last_kernel(mine_ref, theirs_ref, out_ref, both_v):
    core = lax.axis_index("head") % 2
    channels, tokens = out_ref.shape
    share = tokens // 2
    half = share // 2
    weight = (mine_ref[half:] + theirs_ref[half:]) / (2 * tokens * channels)
    weight = weight[:1, :1]
    for ref, index in ((mine_ref, core), (theirs_ref, 1 - core)):
        packet = -ref[:half] / weight
        start = pl.multiple_of(index * share, share)
        both_v[pl.ds(start, half)] = packet
        both_v[pl.ds(start + half, half)] = swap_halves(packet)
    out_ref[...] = both_v[...].T[:channels]


def paired_local(
    sizes,
    latents,
    noise,
    step,
    stream,
    patch_embed_weight,
    prenorm_gain_vector,
    query_matrix,
    key_matrix,
    value_matrix,
    output_matrix,
    velocity_readout_weight,
    adapter_query_down,
    adapter_query_up,
    adapter_output_down,
    adapter_output_up,
):
    groups, _, heads = sizes
    tokens, channels = latents.shape
    half_width, local_columns = query_matrix.shape
    quarter = half_width // 2
    columns = local_columns // 2
    rank = adapter_query_down.shape[1]
    share = tokens // 2
    to_x = pairs((2,), lambda s: (s ^ 1,))
    to_core = pairs((heads,), lambda h: (h ^ 1,))
    to_y = pairs((heads,), lambda h: (h ^ 2,))
    to_xy = pairs((2, heads), lambda s, h: (s ^ 1, h ^ 2))
    partial_flops = 2 * tokens * half_width * (3 * local_columns + rank)

    target = (1 - lax.axis_index("seq")) * 2 + lax.axis_index("head") % 2
    message = columns_of(stream, target, quarter)
    near = lax.ppermute(message, "seq", to_x)
    inputs = (
        latents.T, noise.T, stream, patch_embed_weight, prenorm_gain_vector, value_matrix,
    )
    normed, rows, gap, hidden, gain, patch, value = run(
        first_kernel,
        [
            ((tokens, half_width), BF16),
            ((channels + 16, tokens), BF16),
            ((channels, tokens), F32),
            ((4, tokens, quarter), BF16),
            ((2, quarter), F32),
            ((2, channels, quarter), BF16),
            (value_matrix.shape, BF16),
        ],
        [step, *(pltpu.with_memory_space_constraint(x, pltpu.HBM) for x in inputs)],
        [pl.BlockSpec(memory_space=pl.ANY)] + [HBM] * 6,
        [
            pltpu.SMEM((1,), jnp.int32),
            pltpu.VMEM((channels, tokens), BF16),
            pltpu.VMEM((channels, tokens), BF16),
            pltpu.VMEM((4, tokens, quarter), BF16),
            pltpu.VMEM((4, channels, quarter), BF16),
            pltpu.VMEM((4 * quarter,), F32),
            pltpu.SemaphoreType.DMA((5 + 2 * 4,)),
        ],
    )
    other_rows = lax.ppermute(rows, "seq", to_x)
    own_sent, own_kept, mix_part, down = run(
        own_kernel,
        [
            ((tokens, 6 * columns + 2 * channels), BF16),
            ((tokens, 4 * columns), F32),
            ((columns, channels), F32),
            (adapter_query_down.shape, BF16),
        ],
        (
            normed, query_matrix, key_matrix, value,
            *(
                pltpu.with_memory_space_constraint(x, pltpu.HBM)
                for x in (adapter_query_down, output_matrix, velocity_readout_weight)
            ),
        ),
        [VMEM] * 4 + [HBM] * 3,
        scratch=[
            pltpu.VMEM(output_matrix.shape, BF16),
            pltpu.VMEM((channels, half_width), BF16),
            pltpu.VMEM((local_columns, channels), F32),
            pltpu.SemaphoreType.DMA((3,)),
        ],
        flops=partial_flops,
    )
    own_got = lax.ppermute(own_sent, "seq", to_x)
    readout_of_up, base = run(
        side_kernel,
        [((rank, channels), BF16), ((tokens, channels), F32)],
        (hidden, adapter_output_up, velocity_readout_weight, gap),
        flops=8 * tokens * half_width * channels,
    )
    far = lax.ppermute(near, "head", to_core)
    weights = (query_matrix, key_matrix, value, down)
    shared = (other_rows, patch, gain, *weights)
    near_parts = run(
        near_kernel,
        [((tokens, w.shape[1]), F32) for w in weights],
        (near, *shared),
        flops=partial_flops // 2,
    )
    small_sent, other_sent, other_kept = run(
        far_kernel,
        [
            ((tokens, rank), BF16),
            ((tokens, 5 * columns), BF16),
            ((tokens, 4 * columns), F32),
        ],
        (far, *shared, *near_parts),
        flops=partial_flops // 2,
    )
    small_got = lax.ppermute(small_sent, "seq", to_x)
    other_got = lax.ppermute(other_sent, "seq", to_x)
    (lora,) = run(lora_kernel, [((tokens, rank), BF16)], (own_kept, small_got, other_kept, own_got))
    lora_far = lax.ppermute(lora, "head", to_core)
    half_set, mixes, low_rank = run(
        half_kernel,
        [
            ((4, tokens, columns), BF16),
            ((2, columns, 2 * channels), BF16),
            ((tokens, columns), F32),
        ],
        (
            other_kept, own_got, lora, lora_far, adapter_query_up, mix_part,
            adapter_output_down, readout_of_up,
        ),
    )
    sent, stay = run(
        attention_kernel,
        [((tokens, 2 * channels), F32)] * 2,
        (own_kept, other_got, low_rank, half_set, mixes, base),
        scratch=[
            pltpu.VMEM((4, 2 * tokens, columns), BF16),
            pltpu.VMEM((2 * tokens, 2 * channels), F32),
        ],
    )

    got = lax.ppermute(sent, "head", to_core)
    packed = ((share + share // 2, 2 * channels), BF16)
    same, cross = run(pack_kernel, [packed, packed], (stay, got))
    from_x = lax.ppermute(cross, "seq", to_x)
    from_y = lax.ppermute(same, "head", to_y)
    from_xy = lax.ppermute(cross, ("seq", "head"), to_xy)
    total = (same.astype(F32) + from_y.astype(F32)) + (
        from_x.astype(F32) + from_xy.astype(F32)
    )
    total = total.astype(BF16)
    totals = [total]
    for k in range(1, groups):
        to_group = pairs((groups,), lambda g, k=k: (g ^ k,))
        totals.append(lax.ppermute(total, "group", to_group))
    (packet,) = run(error_kernel, [((share // 2 + 8, 2 * channels), F32)], totals)
    answer = lax.ppermute(packet, "head", to_core)
    (out,) = run(
        last_kernel,
        [((channels, tokens), F32)],
        (packet, answer),
        scratch=[pltpu.VMEM((tokens, 2 * channels), F32)],
    )
    return out.T


def gathered_local(
    latents,
    noise,
    step,
    stream,
    patch_embed_weight,
    prenorm_gain_vector,
    query_matrix,
    key_matrix,
    value_matrix,
    output_matrix,
    velocity_readout_weight,
    adapter_query_down,
    adapter_query_up,
    adapter_output_down,
    adapter_output_up,
):
    tokens = latents.shape[0]
    width = query_matrix.shape[1]
    local_heads = width // HEAD_SIZE
    channels = velocity_readout_weight.shape[0]
    sigma = noise_level(step)
    noisy = (
        (1.0 - sigma) * latents.astype(F32) + sigma * noise.astype(F32)
    ).astype(BF16)
    hidden = (stream.astype(F32) + dot(noisy, patch_embed_weight)).astype(BF16)
    hidden_wide = hidden.astype(F32)
    normed = (
        hidden_wide
        * lax.rsqrt(jnp.mean(hidden_wide * hidden_wide, axis=-1, keepdims=True) + 1e-06)
        * prenorm_gain_vector
    ).astype(BF16)
    base_query, keys, values, lora_hidden = (
        dot(normed, lax.all_gather(piece, "seq", axis=0, tiled=True))
        for piece in (query_matrix, key_matrix, value_matrix, adapter_query_down)
    )
    scale = HEAD_SIZE ** (-0.5)
    lora_delta = dot(lora_hidden.astype(BF16), adapter_query_up)
    queries = (base_query * scale).astype(BF16)
    fake_queries = ((base_query + lora_delta) * scale).astype(BF16)
    both_sets = jnp.stack([queries, fake_queries]).reshape(2, tokens, local_heads, HEAD_SIZE)
    key_rows = lax.all_gather(keys.astype(BF16), "seq", axis=0, tiled=True)
    value_rows = lax.all_gather(values.astype(BF16), "seq", axis=0, tiled=True)
    key_rows = key_rows.reshape(-1, local_heads, HEAD_SIZE)
    value_rows = value_rows.reshape(-1, local_heads, HEAD_SIZE)
    scores = jnp.einsum("sthd,khd->shtk", both_sets, key_rows, preferred_element_type=F32)
    weights = jnp.exp(scores - jnp.max(scores, axis=-1, keepdims=True))
    mass = jnp.sum(weights, axis=-1)
    added = jnp.einsum(
        "shtk,khd->sthd", weights.astype(BF16), value_rows, preferred_element_type=F32
    )
    attn = (added / mass.transpose(0, 2, 1)[..., None]).astype(BF16).reshape(2, tokens, width)
    columns = output_matrix.shape[1]
    readout_part = columns_of(velocity_readout_weight, lax.axis_index("seq"), columns)
    mix_full = lax.psum(contract_final_axis(output_matrix, readout_part), "seq")
    lora_readout = contract_final_axis(adapter_output_up, velocity_readout_weight).astype(BF16)
    fake_mix = (mix_full + dot(adapter_output_down, lora_readout)).astype(BF16)
    real_sum, fake_sum = lax.psum(
        (dot(attn[0], mix_full.astype(BF16)), dot(attn[1], fake_mix)), ("group", "head")
    )
    base = contract_final_axis(hidden, velocity_readout_weight)
    noisy_wide = noisy.astype(F32)
    x0_real = noisy_wide - sigma * (base + real_sum)
    x0_fake = noisy_wide - sigma * (base + fake_sum)
    local_error = jnp.sum(jnp.abs(latents.astype(F32) - x0_real))
    weight = lax.psum(local_error, "seq") / (tokens * lax.axis_size("seq") * channels)
    return (x0_fake - x0_real) / weight


def solution(mesh):
    sizes = tuple(mesh.shape[name] for name in ("group", "seq", "head"))

    def local(*args):
        query_columns = args[6].shape[1]
        power = sizes[0] & (sizes[0] - 1) == 0
        paired = sizes[1] == 2 and sizes[2] == 4 and power
        paired = paired and args[0].shape[0] == query_columns // 2
        if paired and (query_columns // HEAD_SIZE) % 2 == 0:
            return paired_local(sizes, *args)
        return gathered_local(*args)

    split = ("group", "head")
    in_specs = (
        P("seq", None),
        P("seq", None),
        P(),
        P("seq", None),
        P(),
        P(),
        P("seq", split),
        P("seq", split),
        P("seq", split),
        P(split, "seq"),
        P(),
        P("seq", None),
        P(None, split),
        P(split, None),
        P(),
    )
    return jax.shard_map(
        local, mesh=mesh, in_specs=in_specs, out_specs=P("seq", None), check_vma=False
    )
```

```python
import itertools

import jax
import jax.numpy as jnp
from jax import lax
from jax.experimental import pallas as pl
from jax.experimental.pallas import tpu as pltpu
from jax.sharding import PartitionSpec as P


HEAD_SIZE = 128
F32 = jnp.float32
BF16 = jnp.bfloat16


def contract_final_axis(left, right):
    return lax.dot_general(
        left, right, (((1,), (1,)), ((), ())), preferred_element_type=F32
    )


def dot(left, right):
    return jnp.dot(left, right, preferred_element_type=F32)


def noise_level(step):
    level = (step[0].astype(F32) + 1.0) / 1000.0
    return 5.0 * level / (1.0 + 4.0 * level)


def pairs(sizes, partner):
    def linear(coordinate):
        index = 0
        for value, size in zip(coordinate, sizes):
            index = index * size + value
        return index

    return [
        (linear(c), linear(partner(*c)))
        for c in itertools.product(*[range(n) for n in sizes])
    ]


def columns_of(x, index, count):
    return lax.dynamic_slice_in_dim(x, index * count, count, 1)


VMEM = pl.BlockSpec(memory_space=pltpu.VMEM)
HBM = pl.BlockSpec(memory_space=pltpu.HBM)


def run(kernel, outs, args, specs=None, scratch=(), flops=0, limit=8 << 20, moved=None):
    shapes = [jax.ShapeDtypeStruct(shape, kind) for shape, kind in outs]
    if moved is None:
        moved = sum(a.size * a.dtype.itemsize for a in (*args, *shapes))
    return pl.pallas_call(
        kernel,
        out_shape=shapes,
        in_specs=specs or [VMEM] * len(args),
        out_specs=[VMEM] * len(shapes),
        scratch_shapes=list(scratch),
        cost_estimate=pl.CostEstimate(flops=flops, bytes_accessed=moved, transcendentals=0),
        compiler_params=pltpu.CompilerParams(vmem_limit_bytes=limit),
    )(*args)


def aligned(index, count):
    return pl.ds(pl.multiple_of(index * count, count), count)


def fold(low, high):
    lane = lax.broadcasted_iota(jnp.int32, low.shape, 1)
    return jnp.where(lane < low.shape[1] // 2, low, high)


def swap_halves(x):
    return pltpu.roll(x, x.shape[1] // 2, 1)


def high_low(x):
    high = x.astype(BF16)
    return high, (x - high.astype(F32)).astype(BF16)


def first_kernel(
    step_any, latents_hbm, noise_hbm, stream_hbm, patch_hbm, gain_hbm, value_hbm,
    normed_ref, rows_ref, gap_ref, hidden_ref, gain_ref, patch_ref, value_ref,
    step_s, latents_v, noise_v, stream_v, patch_v, gain_v, sems,
):
    parts, tokens, quarter = stream_v.shape
    channels = latents_v.shape[0]
    seq = lax.axis_index("seq")
    small = [
        pltpu.make_async_copy(latents_hbm, latents_v, sems.at[0]),
        pltpu.make_async_copy(noise_hbm, noise_v, sems.at[1]),
        pltpu.make_async_copy(step_any, step_s, sems.at[2]),
    ]
    gain_copy = pltpu.make_async_copy(gain_hbm, gain_v, sems.at[3])
    large = []
    for j in range(parts):
        span = pl.ds(j * quarter, quarter)
        large.append([
            pltpu.make_async_copy(source.at[:, span], target.at[j], sems.at[4 + 2 * j + i])
            for i, (source, target) in enumerate(
                ((stream_hbm, stream_v), (patch_hbm, patch_v))
            )
        ])
    for copy in small:
        copy.start()
    for j in range(parts):
        for copy in large[j]:
            copy.start()
    gain_copy.start()
    value_copy = pltpu.make_async_copy(value_hbm, value_ref, sems.at[sems.shape[0] - 1])
    value_copy.start()
    for copy in small:
        copy.wait()
    level = (jnp.full((8, 128), step_s[0], jnp.int32).astype(F32) + 1.0) / 1000.0
    sigma = (5.0 * level / (1.0 + 4.0 * level))[:1, :1]
    latents = latents_v[...].astype(F32)
    noisy = ((1.0 - sigma) * latents + sigma * noise_v[...].astype(F32)).astype(BF16)
    gap_ref[...] = (latents - noisy.astype(F32)) / sigma
    squares = jnp.zeros((tokens, 128), F32)
    for j in range(parts):
        for copy in large[j]:
            copy.wait()
        embedded = lax.dot_general(
            noisy, patch_v[j], (((0,), (0,)), ((), ())), preferred_element_type=F32
        )
        hidden = (stream_v[j].astype(F32) + embedded).astype(BF16)
        hidden_ref[j] = hidden
        wide = hidden.astype(F32)
        wide = wide * wide
        for i in range(quarter // 128):
            squares = squares + wide[:, i * 128 : (i + 1) * 128]
    mean = jnp.sum(squares, axis=1, keepdims=True) / (parts * quarter)
    inverse = lax.rsqrt(mean + 1e-06)
    rows_ref[:channels] = noisy
    scale = jnp.broadcast_to(inverse, (tokens, tokens)).T[:8]
    first, _ = high_low(scale)
    second, third = high_low(scale - first.astype(F32))
    row = lax.broadcasted_iota(jnp.int32, (16, tokens), 0)
    terms = [jnp.concatenate([x.astype(F32)] * 2, axis=0) for x in (first, second, third)]
    terms = jnp.where(row == 0, terms[0], jnp.where(row == 1, terms[1], terms[2]))
    rows_ref[channels:] = terms.astype(BF16)
    gain_copy.wait()
    for j in range(parts):

        @pl.when(seq == j // 2)
        def _(j=j):
            gain = gain_v[j * quarter : (j + 1) * quarter][None, :]
            start = (j % 2) * quarter
            gain_ref[j % 2 : j % 2 + 1] = gain
            patch_ref[j % 2] = patch_v[j]
            normed_ref[:, start : start + quarter] = (
                hidden_ref[j].astype(F32) * inverse * gain
            ).astype(BF16)

    value_copy.wait()


def pick(index, x):
    half = x.shape[1] // 2
    return jnp.where(index == 0, x[:, :half], x[:, half:])


def partial_outputs(parts, seq, query_terms, lora_blocks, sent_ref, kept_ref):
    q, k, v, lora = parts
    columns = q.shape[1] // 2
    blocks = [*high_low(pick(1 - seq, q))[:query_terms], *high_low(pick(1 - seq, k))]
    blocks += [pick(1 - seq, v).astype(BF16), *lora_blocks]
    for i, block in enumerate(blocks):
        sent_ref[:, i * columns : (i + 1) * columns] = block
    for i, block in enumerate((pick(seq, q), pick(seq, k), pick(seq, v), lora)):
        kept_ref[:, i * columns : (i + 1) * columns] = block


def half_rows(x):
    share = x.shape[0] // 2
    half = jnp.where(lax.axis_index("head") % 2 == 0, x[:share], x[share:])
    return jnp.concatenate(high_low(half), axis=0)


def own_kernel(
    normed_ref, q_ref, k_ref, v_ref, down_hbm, output_hbm, readout_hbm,
    sent_ref, kept_ref, mix_ref, down_v,
    output_v, readout_v, mix_v, sems,
):
    seq = lax.axis_index("seq")
    copies = [
        pltpu.make_async_copy(down_hbm, down_v, sems.at[0]),
        pltpu.make_async_copy(output_hbm, output_v, sems.at[1]),
        pltpu.make_async_copy(
            readout_hbm.at[:, aligned(seq, readout_v.shape[1])], readout_v, sems.at[2]
        ),
    ]
    for copy in copies:
        copy.start()
    normed = normed_ref[...]
    parts = [dot(normed, w[...]) for w in (q_ref, k_ref, v_ref)]
    copies[0].wait()
    lora = dot(normed, down_v[...])
    parts.append(lora)
    partial_outputs(parts, seq, 2, [half_rows(lora)], sent_ref, kept_ref)
    for copy in copies[1:]:
        copy.wait()
    mix_v[...] = contract_final_axis(output_v[...], readout_v[...])
    rows, channels = mix_ref.shape
    theirs = mix_v[aligned(1 - seq, rows), :]
    high = theirs.astype(BF16).astype(F32)
    both = jnp.concatenate([high, theirs - high], axis=1)
    sent_ref[:, -2 * channels :] = both.astype(BF16)
    mix_ref[...] = mix_v[aligned(seq, rows), :]


def side_kernel(hidden_ref, up_ref, readout_ref, gap_ref, readout_of_up_ref, base_ref):
    parts, _, quarter = hidden_ref.shape
    readout_of_up_ref[...] = contract_final_axis(up_ref[...], readout_ref[...]).astype(BF16)
    base = gap_ref[...]
    for j in range(parts):
        base += contract_final_axis(
            readout_ref[:, j * quarter : (j + 1) * quarter], hidden_ref[j]
        )
    once = (lax.axis_index("group") == 0) & (lax.axis_index("head") == 0)
    base_ref[...] = jnp.where(once, base, 0.0).T


def other_parts(part, raw_ref, rows_ref, patch_ref, gain_ref, weights):
    tokens, quarter = raw_ref.shape
    channels = patch_ref.shape[1]
    noisy = rows_ref[:channels]
    terms = rows_ref[channels:].astype(F32)
    scale = (terms[:1] + terms[1:2]) + terms[2:3]
    inverse = jnp.broadcast_to(scale, (tokens, tokens)).T[:, :1]
    embedded = lax.dot_general(
        noisy, patch_ref[part],
        (((0,), (0,)), ((), ())), preferred_element_type=F32,
    )
    hidden = (raw_ref[...].astype(F32) + embedded).astype(BF16).astype(F32)
    normed = (hidden * inverse * gain_ref[pl.ds(part, 1), :]).astype(BF16)
    return [dot(normed, w[aligned(part, quarter), :]) for w in weights]


def near_kernel(raw_ref, rows_ref, patch_ref, gain_ref, q_ref, k_ref, v_ref, down_ref, *outs):
    core = lax.axis_index("head") % 2
    weights = (q_ref, k_ref, v_ref, down_ref)
    parts = other_parts(core, raw_ref, rows_ref, patch_ref, gain_ref, weights)
    for out, part in zip(outs, parts):
        out[...] = part


def far_kernel(
    raw_ref, rows_ref, patch_ref, gain_ref, q_ref, k_ref, v_ref, down_ref,
    near_q_ref, near_k_ref, near_v_ref, near_down_ref,
    small_ref, sent_ref, kept_ref,
):
    core = lax.axis_index("head") % 2
    weights = (q_ref, k_ref, v_ref, down_ref)
    parts = other_parts(1 - core, raw_ref, rows_ref, patch_ref, gain_ref, weights)
    near = (near_q_ref, near_k_ref, near_v_ref, near_down_ref)
    parts = [part + ref[...] for part, ref in zip(parts, near)]
    small_ref[...] = half_rows(parts[3])
    partial_outputs(parts, lax.axis_index("seq"), 1, [], sent_ref, kept_ref)


def finish(kept_ref, got_ref, query_terms, low_rank):
    columns = low_rank.shape[1]

    def got(i):
        return got_ref[:, i * columns : (i + 1) * columns].astype(F32)

    def kept(i):
        return kept_ref[:, i * columns : (i + 1) * columns]

    scale = HEAD_SIZE ** (-0.5)
    n = query_terms
    base = kept(0) + sum(got(i) for i in reversed(range(n)))
    return (
        (base * scale).astype(BF16),
        ((base + low_rank) * scale).astype(BF16),
        (kept(1) + (got(n) + got(n + 1))).astype(BF16),
        (kept(2) + got(n + 2)).astype(BF16),
    )


def lora_kernel(own_kept_ref, small_got_ref, other_kept_ref, own_got_ref, lora_ref):
    rank = lora_ref.shape[1]
    share = lora_ref.shape[0] // 2
    core = lax.axis_index("head") % 2
    for i, (kept_ref, got) in enumerate((
        (own_kept_ref, small_got_ref[...]),
        (other_kept_ref, own_got_ref[:, 5 * rank : 6 * rank]),
    )):
        kept = kept_ref[aligned(core, share), kept_ref.shape[1] - rank :]
        got = got.astype(F32)
        lora_ref[i * share : (i + 1) * share] = (
            kept + (got[:share] + got[share:])
        ).astype(BF16)


def half_kernel(
    kept_ref, got_ref, lora_ref, lora_far_ref, up_ref, mix_ref, down_ref,
    readout_of_up_ref, set_ref, mixes_ref, low_rank_ref,
):
    seq = lax.axis_index("seq")
    rows, channels = mix_ref.shape
    up = up_ref[:, aligned(seq, rows)]
    mine, far = lora_ref[...], lora_far_ref[...]
    share = mine.shape[0] // 2
    first = lax.axis_index("head") % 2 == 0
    low, high = jnp.where(first, mine, far), jnp.where(first, far, mine)
    own = jnp.concatenate([low[:share], high[:share]], axis=0)
    other = jnp.concatenate([low[share:], high[share:]], axis=0)
    low_rank_ref[...] = dot(own, up)
    for i, block in enumerate(finish(kept_ref, got_ref, 2, dot(other, up))):
        set_ref[i] = block
    got = got_ref[:, -2 * channels :].astype(F32)
    mix_full = mix_ref[...] + (got[:, :channels] + swap_halves(got)[:, :channels])
    low_rank = dot(down_ref[aligned(seq, rows), :], readout_of_up_ref[...])
    mix = mix_full.astype(BF16).astype(F32)
    fake = (mix_full + low_rank).astype(BF16).astype(F32)
    mixes_ref[0] = jnp.concatenate([mix, -mix], axis=1).astype(BF16)
    mixes_ref[1] = jnp.concatenate([jnp.zeros_like(fake), fake], axis=1).astype(BF16)


def attention_kernel(
    kept_ref, got_ref, low_rank_ref, set_ref, mixes_ref, base_ref,
    sent_ref, stay_ref, sets_v, terms_v,
):
    core = lax.axis_index("head") % 2
    tokens, channels = base_ref.shape
    columns = set_ref.shape[2]
    for i, block in enumerate(finish(kept_ref, got_ref, 1, low_rank_ref[...])):
        sets_v[i, :tokens] = block
        sets_v[i, tokens:] = set_ref[i]
    terms = jnp.zeros(terms_v.shape, F32)
    rows = 2 * tokens
    for start in range(0, columns, HEAD_SIZE):
        span = slice(start, start + HEAD_SIZE)
        queries = jnp.concatenate([sets_v[0, :, span], sets_v[1, :, span]], axis=0)
        scores = contract_final_axis(queries, sets_v[2, :, span])
        probs = jnp.exp(scores - jnp.max(scores, axis=1, keepdims=True))
        mass = jnp.sum(probs, axis=1, keepdims=True)
        attn = (dot(probs.astype(BF16), sets_v[3, :, span]) * (1.0 / mass)).astype(BF16)
        attn = jnp.concatenate([attn[:rows], attn[rows:]], axis=1)
        mixes = jnp.concatenate([mixes_ref[0, span, :], mixes_ref[1, span, :]], axis=0)
        terms = terms + dot(attn, mixes)
    terms_v[...] = terms
    terms_v[:tokens, :channels] = terms[:tokens, :channels] + base_ref[...]
    share = tokens // 2
    sent_ref[:share] = terms_v[aligned(1 - core, share), :]
    sent_ref[share:] = terms_v[aligned(3 - core, share), :]
    stay_ref[:share] = terms_v[aligned(core, share), :]
    stay_ref[share:] = terms_v[aligned(2 + core, share), :]


def pack_kernel(stay_ref, got_ref, same_ref, cross_ref):
    share = stay_ref.shape[0] // 2
    mine = stay_ref[:share] + got_ref[:share]
    theirs = stay_ref[share:] + got_ref[share:]
    half = share // 2
    same_ref[:share] = mine.astype(BF16)
    same_ref[share:] = fold(theirs[:half], swap_halves(theirs[half:])).astype(BF16)
    cross_ref[:share] = theirs.astype(BF16)
    cross_ref[share:] = fold(mine[:half], swap_halves(mine[half:])).astype(BF16)


def error_kernel(*refs):
    *parts, packet_ref = refs
    parts = [ref[...].astype(F32) for ref in parts]
    while len(parts) > 1:
        parts = [a + b for a, b in zip(parts[::2], parts[1::2])]
    total = parts[0]
    half = packet_ref.shape[0] - 8
    share = 2 * half
    own = jnp.abs(total[:half]) + jnp.abs(total[half:share])
    own = fold(own, jnp.zeros_like(own)) + jnp.abs(total[share:])
    packet_ref[:half] = fold(swap_halves(total[:half]), total[half:share])
    packet_ref[half:] = jnp.full((8, packet_ref.shape[1]), jnp.sum(own), F32)


def last_kernel(mine_ref, theirs_ref, out_ref, both_v):
    core = lax.axis_index("head") % 2
    channels, tokens = out_ref.shape
    share = tokens // 2
    half = share // 2
    weight = (mine_ref[half:] + theirs_ref[half:]) / (2 * tokens * channels)
    weight = weight[:1, :1]
    for ref, index in ((mine_ref, core), (theirs_ref, 1 - core)):
        packet = -ref[:half] / weight
        start = pl.multiple_of(index * share, share)
        both_v[pl.ds(start, half)] = packet
        both_v[pl.ds(start + half, half)] = swap_halves(packet)
    out_ref[...] = both_v[...].T[:channels]


def paired_local(
    sizes,
    latents,
    noise,
    step,
    stream,
    patch_embed_weight,
    prenorm_gain_vector,
    query_matrix,
    key_matrix,
    value_matrix,
    output_matrix,
    velocity_readout_weight,
    adapter_query_down,
    adapter_query_up,
    adapter_output_down,
    adapter_output_up,
):
    groups, _, heads = sizes
    tokens, channels = latents.shape
    half_width, local_columns = query_matrix.shape
    quarter = half_width // 2
    columns = local_columns // 2
    rank = adapter_query_down.shape[1]
    share = tokens // 2
    to_x = pairs((2,), lambda s: (s ^ 1,))
    to_core = pairs((heads,), lambda h: (h ^ 1,))
    to_y = pairs((heads,), lambda h: (h ^ 2,))
    to_xy = pairs((2, heads), lambda s, h: (s ^ 1, h ^ 2))
    partial_flops = 2 * tokens * half_width * (3 * local_columns + rank)

    target = (1 - lax.axis_index("seq")) * 2 + lax.axis_index("head") % 2
    message = columns_of(stream, target, quarter)
    near = lax.ppermute(message, "seq", to_x)
    inputs = (
        latents.T, noise.T, stream, patch_embed_weight, prenorm_gain_vector, value_matrix,
    )
    normed, rows, gap, hidden, gain, patch, value = run(
        first_kernel,
        [
            ((tokens, half_width), BF16),
            ((channels + 16, tokens), BF16),
            ((channels, tokens), F32),
            ((4, tokens, quarter), BF16),
            ((2, quarter), F32),
            ((2, channels, quarter), BF16),
            (value_matrix.shape, BF16),
        ],
        [step, *(pltpu.with_memory_space_constraint(x, pltpu.HBM) for x in inputs)],
        [pl.BlockSpec(memory_space=pl.ANY)] + [HBM] * 6,
        [
            pltpu.SMEM((1,), jnp.int32),
            pltpu.VMEM((channels, tokens), BF16),
            pltpu.VMEM((channels, tokens), BF16),
            pltpu.VMEM((4, tokens, quarter), BF16),
            pltpu.VMEM((4, channels, quarter), BF16),
            pltpu.VMEM((4 * quarter,), F32),
            pltpu.SemaphoreType.DMA((5 + 2 * 4,)),
        ],
    )
    other_rows = lax.ppermute(rows, "seq", to_x)
    own_sent, own_kept, mix_part, down = run(
        own_kernel,
        [
            ((tokens, 6 * columns + 2 * channels), BF16),
            ((tokens, 4 * columns), F32),
            ((columns, channels), F32),
            (adapter_query_down.shape, BF16),
        ],
        (
            normed, query_matrix, key_matrix, value,
            *(
                pltpu.with_memory_space_constraint(x, pltpu.HBM)
                for x in (adapter_query_down, output_matrix, velocity_readout_weight)
            ),
        ),
        [VMEM] * 4 + [HBM] * 3,
        scratch=[
            pltpu.VMEM(output_matrix.shape, BF16),
            pltpu.VMEM((channels, half_width), BF16),
            pltpu.VMEM((local_columns, channels), F32),
            pltpu.SemaphoreType.DMA((3,)),
        ],
        flops=partial_flops,
    )
    own_got = lax.ppermute(own_sent, "seq", to_x)
    readout_of_up, base = run(
        side_kernel,
        [((rank, channels), BF16), ((tokens, channels), F32)],
        (hidden, adapter_output_up, velocity_readout_weight, gap),
        flops=8 * tokens * half_width * channels,
    )
    far = lax.ppermute(near, "head", to_core)
    weights = (query_matrix, key_matrix, value, down)
    shared = (other_rows, patch, gain, *weights)
    near_parts = run(
        near_kernel,
        [((tokens, w.shape[1]), F32) for w in weights],
        (near, *shared),
        flops=partial_flops // 2,
    )
    small_sent, other_sent, other_kept = run(
        far_kernel,
        [
            ((tokens, rank), BF16),
            ((tokens, 4 * columns), BF16),
            ((tokens, 4 * columns), F32),
        ],
        (far, *shared, *near_parts),
        flops=partial_flops // 2,
    )
    small_got = lax.ppermute(small_sent, "seq", to_x)
    other_got = lax.ppermute(other_sent, "seq", to_x)
    (lora,) = run(lora_kernel, [((tokens, rank), BF16)], (own_kept, small_got, other_kept, own_got))
    lora_far = lax.ppermute(lora, "head", to_core)
    half_set, mixes, low_rank = run(
        half_kernel,
        [
            ((4, tokens, columns), BF16),
            ((2, columns, 2 * channels), BF16),
            ((tokens, columns), F32),
        ],
        (
            other_kept, own_got, lora, lora_far, adapter_query_up, mix_part,
            adapter_output_down, readout_of_up,
        ),
    )
    sent, stay = run(
        attention_kernel,
        [((tokens, 2 * channels), F32)] * 2,
        (own_kept, other_got, low_rank, half_set, mixes, base),
        scratch=[
            pltpu.VMEM((4, 2 * tokens, columns), BF16),
            pltpu.VMEM((2 * tokens, 2 * channels), F32),
        ],
    )

    got = lax.ppermute(sent, "head", to_core)
    packed = ((share + share // 2, 2 * channels), BF16)
    same, cross = run(pack_kernel, [packed, packed], (stay, got))
    from_x = lax.ppermute(cross, "seq", to_x)
    from_y = lax.ppermute(same, "head", to_y)
    from_xy = lax.ppermute(cross, ("seq", "head"), to_xy)
    total = (same.astype(F32) + from_y.astype(F32)) + (
        from_x.astype(F32) + from_xy.astype(F32)
    )
    total = total.astype(BF16)
    totals = [total]
    for k in range(1, groups):
        to_group = pairs((groups,), lambda g, k=k: (g ^ k,))
        totals.append(lax.ppermute(total, "group", to_group))
    (packet,) = run(error_kernel, [((share // 2 + 8, 2 * channels), F32)], totals)
    answer = lax.ppermute(packet, "head", to_core)
    (out,) = run(
        last_kernel,
        [((channels, tokens), F32)],
        (packet, answer),
        scratch=[pltpu.VMEM((tokens, 2 * channels), F32)],
    )
    return out.T


def gathered_local(
    latents,
    noise,
    step,
    stream,
    patch_embed_weight,
    prenorm_gain_vector,
    query_matrix,
    key_matrix,
    value_matrix,
    output_matrix,
    velocity_readout_weight,
    adapter_query_down,
    adapter_query_up,
    adapter_output_down,
    adapter_output_up,
):
    tokens = latents.shape[0]
    width = query_matrix.shape[1]
    local_heads = width // HEAD_SIZE
    channels = velocity_readout_weight.shape[0]
    sigma = noise_level(step)
    noisy = (
        (1.0 - sigma) * latents.astype(F32) + sigma * noise.astype(F32)
    ).astype(BF16)
    hidden = (stream.astype(F32) + dot(noisy, patch_embed_weight)).astype(BF16)
    hidden_wide = hidden.astype(F32)
    normed = (
        hidden_wide
        * lax.rsqrt(jnp.mean(hidden_wide * hidden_wide, axis=-1, keepdims=True) + 1e-06)
        * prenorm_gain_vector
    ).astype(BF16)
    base_query, keys, values, lora_hidden = (
        dot(normed, lax.all_gather(piece, "seq", axis=0, tiled=True))
        for piece in (query_matrix, key_matrix, value_matrix, adapter_query_down)
    )
    scale = HEAD_SIZE ** (-0.5)
    lora_delta = dot(lora_hidden.astype(BF16), adapter_query_up)
    queries = (base_query * scale).astype(BF16)
    fake_queries = ((base_query + lora_delta) * scale).astype(BF16)
    both_sets = jnp.stack([queries, fake_queries]).reshape(2, tokens, local_heads, HEAD_SIZE)
    key_rows = lax.all_gather(keys.astype(BF16), "seq", axis=0, tiled=True)
    value_rows = lax.all_gather(values.astype(BF16), "seq", axis=0, tiled=True)
    key_rows = key_rows.reshape(-1, local_heads, HEAD_SIZE)
    value_rows = value_rows.reshape(-1, local_heads, HEAD_SIZE)
    scores = jnp.einsum("sthd,khd->shtk", both_sets, key_rows, preferred_element_type=F32)
    weights = jnp.exp(scores - jnp.max(scores, axis=-1, keepdims=True))
    mass = jnp.sum(weights, axis=-1)
    added = jnp.einsum(
        "shtk,khd->sthd", weights.astype(BF16), value_rows, preferred_element_type=F32
    )
    attn = (added / mass.transpose(0, 2, 1)[..., None]).astype(BF16).reshape(2, tokens, width)
    columns = output_matrix.shape[1]
    readout_part = columns_of(velocity_readout_weight, lax.axis_index("seq"), columns)
    mix_full = lax.psum(contract_final_axis(output_matrix, readout_part), "seq")
    lora_readout = contract_final_axis(adapter_output_up, velocity_readout_weight).astype(BF16)
    fake_mix = (mix_full + dot(adapter_output_down, lora_readout)).astype(BF16)
    real_sum, fake_sum = lax.psum(
        (dot(attn[0], mix_full.astype(BF16)), dot(attn[1], fake_mix)), ("group", "head")
    )
    base = contract_final_axis(hidden, velocity_readout_weight)
    noisy_wide = noisy.astype(F32)
    x0_real = noisy_wide - sigma * (base + real_sum)
    x0_fake = noisy_wide - sigma * (base + fake_sum)
    local_error = jnp.sum(jnp.abs(latents.astype(F32) - x0_real))
    weight = lax.psum(local_error, "seq") / (tokens * lax.axis_size("seq") * channels)
    return (x0_fake - x0_real) / weight


def solution(mesh):
    sizes = tuple(mesh.shape[name] for name in ("group", "seq", "head"))

    def local(*args):
        query_columns = args[6].shape[1]
        power = sizes[0] & (sizes[0] - 1) == 0
        paired = sizes[1] == 2 and sizes[2] == 4 and power
        paired = paired and args[0].shape[0] == query_columns // 2
        if paired and (query_columns // HEAD_SIZE) % 2 == 0:
            return paired_local(sizes, *args)
        return gathered_local(*args)

    split = ("group", "head")
    in_specs = (
        P("seq", None),
        P("seq", None),
        P(),
        P("seq", None),
        P(),
        P(),
        P("seq", split),
        P("seq", split),
        P("seq", split),
        P(split, "seq"),
        P(),
        P("seq", None),
        P(None, split),
        P(split, None),
        P(),
    )
    return jax.shard_map(
        local, mesh=mesh, in_specs=in_specs, out_specs=P("seq", None), check_vma=False
    )
```

```python
import itertools

import jax
import jax.numpy as jnp
from jax import lax
from jax.experimental import pallas as pl
from jax.experimental.pallas import tpu as pltpu
from jax.sharding import PartitionSpec as P


HEAD_SIZE = 128
F32 = jnp.float32
BF16 = jnp.bfloat16


def contract_final_axis(left, right):
    return lax.dot_general(
        left, right, (((1,), (1,)), ((), ())), preferred_element_type=F32
    )


def dot(left, right):
    return jnp.dot(left, right, preferred_element_type=F32)


def noise_level(step):
    level = (step[0].astype(F32) + 1.0) / 1000.0
    return 5.0 * level / (1.0 + 4.0 * level)


def pairs(sizes, partner):
    def linear(coordinate):
        index = 0
        for value, size in zip(coordinate, sizes):
            index = index * size + value
        return index

    return [
        (linear(c), linear(partner(*c)))
        for c in itertools.product(*[range(n) for n in sizes])
    ]


def columns_of(x, index, count):
    return lax.dynamic_slice_in_dim(x, index * count, count, 1)


VMEM = pl.BlockSpec(memory_space=pltpu.VMEM)
HBM = pl.BlockSpec(memory_space=pltpu.HBM)


def run(kernel, outs, args, specs=None, scratch=(), flops=0, limit=8 << 20, moved=None):
    shapes = [jax.ShapeDtypeStruct(shape, kind) for shape, kind in outs]
    if moved is None:
        moved = sum(a.size * a.dtype.itemsize for a in (*args, *shapes))
    return pl.pallas_call(
        kernel,
        out_shape=shapes,
        in_specs=specs or [VMEM] * len(args),
        out_specs=[VMEM] * len(shapes),
        scratch_shapes=list(scratch),
        cost_estimate=pl.CostEstimate(flops=flops, bytes_accessed=moved, transcendentals=0),
        compiler_params=pltpu.CompilerParams(vmem_limit_bytes=limit),
    )(*args)


def aligned(index, count):
    return pl.ds(pl.multiple_of(index * count, count), count)


def fold(low, high):
    lane = lax.broadcasted_iota(jnp.int32, low.shape, 1)
    return jnp.where(lane < low.shape[1] // 2, low, high)


def swap_halves(x):
    return pltpu.roll(x, x.shape[1] // 2, 1)


def high_low(x):
    high = x.astype(BF16)
    return high, (x - high.astype(F32)).astype(BF16)


def first_kernel(
    step_any, latents_hbm, noise_hbm, stream_hbm, patch_hbm, gain_hbm, value_hbm,
    normed_ref, rows_ref, gap_ref, hidden_ref, gain_ref, patch_ref, value_ref,
    step_s, latents_v, noise_v, stream_v, patch_v, gain_v, sems,
):
    parts, tokens, quarter = stream_v.shape
    channels = latents_v.shape[0]
    seq = lax.axis_index("seq")
    small = [
        pltpu.make_async_copy(latents_hbm, latents_v, sems.at[0]),
        pltpu.make_async_copy(noise_hbm, noise_v, sems.at[1]),
        pltpu.make_async_copy(step_any, step_s, sems.at[2]),
    ]
    gain_copy = pltpu.make_async_copy(gain_hbm, gain_v, sems.at[3])
    large = []
    for j in range(parts):
        span = pl.ds(j * quarter, quarter)
        large.append([
            pltpu.make_async_copy(source.at[:, span], target.at[j], sems.at[4 + 2 * j + i])
            for i, (source, target) in enumerate(
                ((stream_hbm, stream_v), (patch_hbm, patch_v))
            )
        ])
    for copy in small:
        copy.start()
    for j in range(parts):
        for copy in large[j]:
            copy.start()
    gain_copy.start()
    value_copy = pltpu.make_async_copy(value_hbm, value_ref, sems.at[sems.shape[0] - 1])
    value_copy.start()
    for copy in small:
        copy.wait()
    level = (jnp.full((8, 128), step_s[0], jnp.int32).astype(F32) + 1.0) / 1000.0
    sigma = (5.0 * level / (1.0 + 4.0 * level))[:1, :1]
    latents = latents_v[...].astype(F32)
    noisy = ((1.0 - sigma) * latents + sigma * noise_v[...].astype(F32)).astype(BF16)
    gap_ref[...] = (latents - noisy.astype(F32)) / sigma
    squares = jnp.zeros((tokens, 128), F32)
    for j in range(parts):
        for copy in large[j]:
            copy.wait()
        embedded = lax.dot_general(
            noisy, patch_v[j], (((0,), (0,)), ((), ())), preferred_element_type=F32
        )
        hidden = (stream_v[j].astype(F32) + embedded).astype(BF16)
        hidden_ref[j] = hidden
        wide = hidden.astype(F32)
        wide = wide * wide
        for i in range(quarter // 128):
            squares = squares + wide[:, i * 128 : (i + 1) * 128]
    mean = jnp.sum(squares, axis=1, keepdims=True) / (parts * quarter)
    inverse = lax.rsqrt(mean + 1e-06)
    rows_ref[:channels] = noisy
    scale = jnp.broadcast_to(inverse, (tokens, tokens)).T[:8]
    first, _ = high_low(scale)
    second, third = high_low(scale - first.astype(F32))
    row = lax.broadcasted_iota(jnp.int32, (16, tokens), 0)
    terms = [jnp.concatenate([x.astype(F32)] * 2, axis=0) for x in (first, second, third)]
    terms = jnp.where(row == 0, terms[0], jnp.where(row == 1, terms[1], terms[2]))
    rows_ref[channels:] = terms.astype(BF16)
    gain_copy.wait()
    for j in range(parts):

        @pl.when(seq == j // 2)
        def _(j=j):
            gain = gain_v[j * quarter : (j + 1) * quarter][None, :]
            start = (j % 2) * quarter
            gain_ref[j % 2 : j % 2 + 1] = gain
            patch_ref[j % 2] = patch_v[j]
            normed_ref[:, start : start + quarter] = (
                hidden_ref[j].astype(F32) * inverse * gain
            ).astype(BF16)

    value_copy.wait()


def pick(index, x):
    half = x.shape[1] // 2
    return jnp.where(index == 0, x[:, :half], x[:, half:])


def partial_outputs(parts, seq, terms, lora_blocks, sent_ref, kept_ref):
    q, k, v, lora = parts
    columns = q.shape[1] // 2
    blocks = [*high_low(pick(1 - seq, q))[:terms], *high_low(pick(1 - seq, k))[:terms]]
    blocks += [pick(1 - seq, v).astype(BF16), *lora_blocks]
    for i, block in enumerate(blocks):
        sent_ref[:, i * columns : (i + 1) * columns] = block
    for i, block in enumerate((pick(seq, q), pick(seq, k), pick(seq, v), lora)):
        kept_ref[:, i * columns : (i + 1) * columns] = block


def half_rows(x):
    share = x.shape[0] // 2
    half = jnp.where(lax.axis_index("head") % 2 == 0, x[:share], x[share:])
    return jnp.concatenate(high_low(half), axis=0)


def own_kernel(
    normed_ref, q_ref, k_ref, v_ref, down_hbm, output_hbm, readout_hbm,
    sent_ref, kept_ref, mix_ref, down_v,
    output_v, readout_v, mix_v, sems,
):
    seq = lax.axis_index("seq")
    copies = [
        pltpu.make_async_copy(down_hbm, down_v, sems.at[0]),
        pltpu.make_async_copy(output_hbm, output_v, sems.at[1]),
        pltpu.make_async_copy(
            readout_hbm.at[:, aligned(seq, readout_v.shape[1])], readout_v, sems.at[2]
        ),
    ]
    for copy in copies:
        copy.start()
    normed = normed_ref[...]
    parts = [dot(normed, w[...]) for w in (q_ref, k_ref, v_ref)]
    copies[0].wait()
    lora = dot(normed, down_v[...])
    parts.append(lora)
    partial_outputs(parts, seq, 2, [half_rows(lora)], sent_ref, kept_ref)
    for copy in copies[1:]:
        copy.wait()
    mix_v[...] = contract_final_axis(output_v[...], readout_v[...])
    rows, channels = mix_ref.shape
    theirs = mix_v[aligned(1 - seq, rows), :]
    high = theirs.astype(BF16).astype(F32)
    both = jnp.concatenate([high, theirs - high], axis=1)
    sent_ref[:, -2 * channels :] = both.astype(BF16)
    mix_ref[...] = mix_v[aligned(seq, rows), :]


def side_kernel(hidden_ref, up_ref, readout_ref, gap_ref, readout_of_up_ref, base_ref):
    parts, _, quarter = hidden_ref.shape
    readout_of_up_ref[...] = contract_final_axis(up_ref[...], readout_ref[...]).astype(BF16)
    base = gap_ref[...]
    for j in range(parts):
        base += contract_final_axis(
            readout_ref[:, j * quarter : (j + 1) * quarter], hidden_ref[j]
        )
    once = (lax.axis_index("group") == 0) & (lax.axis_index("head") == 0)
    base_ref[...] = jnp.where(once, base, 0.0).T


def other_parts(part, raw_ref, rows_ref, patch_ref, gain_ref, weights):
    tokens, quarter = raw_ref.shape
    channels = patch_ref.shape[1]
    noisy = rows_ref[:channels]
    terms = rows_ref[channels:].astype(F32)
    scale = (terms[:1] + terms[1:2]) + terms[2:3]
    inverse = jnp.broadcast_to(scale, (tokens, tokens)).T[:, :1]
    embedded = lax.dot_general(
        noisy, patch_ref[part],
        (((0,), (0,)), ((), ())), preferred_element_type=F32,
    )
    hidden = (raw_ref[...].astype(F32) + embedded).astype(BF16).astype(F32)
    normed = (hidden * inverse * gain_ref[pl.ds(part, 1), :]).astype(BF16)
    return [dot(normed, w[aligned(part, quarter), :]) for w in weights]


def near_kernel(raw_ref, rows_ref, patch_ref, gain_ref, q_ref, k_ref, v_ref, down_ref, *outs):
    core = lax.axis_index("head") % 2
    weights = (q_ref, k_ref, v_ref, down_ref)
    parts = other_parts(core, raw_ref, rows_ref, patch_ref, gain_ref, weights)
    for out, part in zip(outs, parts):
        out[...] = part


def far_kernel(
    raw_ref, rows_ref, patch_ref, gain_ref, q_ref, k_ref, v_ref, down_ref,
    near_q_ref, near_k_ref, near_v_ref, near_down_ref,
    small_ref, sent_ref, kept_ref,
):
    core = lax.axis_index("head") % 2
    weights = (q_ref, k_ref, v_ref, down_ref)
    parts = other_parts(1 - core, raw_ref, rows_ref, patch_ref, gain_ref, weights)
    near = (near_q_ref, near_k_ref, near_v_ref, near_down_ref)
    parts = [part + ref[...] for part, ref in zip(parts, near)]
    small_ref[...] = half_rows(parts[3])
    partial_outputs(parts, lax.axis_index("seq"), 1, [], sent_ref, kept_ref)


def finish(kept_ref, got_ref, terms, low_rank):
    columns = low_rank.shape[1]

    def got(i):
        return got_ref[:, i * columns : (i + 1) * columns].astype(F32)

    def kept(i):
        return kept_ref[:, i * columns : (i + 1) * columns]

    scale = HEAD_SIZE ** (-0.5)

    def got_sum(start):
        return sum(got(start + i) for i in reversed(range(terms)))

    base = kept(0) + got_sum(0)
    return (
        (base * scale).astype(BF16),
        ((base + low_rank) * scale).astype(BF16),
        (kept(1) + got_sum(terms)).astype(BF16),
        (kept(2) + got(2 * terms)).astype(BF16),
    )


def lora_kernel(own_kept_ref, small_got_ref, other_kept_ref, own_got_ref, lora_ref):
    rank = lora_ref.shape[1]
    share = lora_ref.shape[0] // 2
    core = lax.axis_index("head") % 2
    for i, (kept_ref, got) in enumerate((
        (own_kept_ref, small_got_ref[...]),
        (other_kept_ref, own_got_ref[:, 5 * rank : 6 * rank]),
    )):
        kept = kept_ref[aligned(core, share), kept_ref.shape[1] - rank :]
        got = got.astype(F32)
        lora_ref[i * share : (i + 1) * share] = (
            kept + (got[:share] + got[share:])
        ).astype(BF16)


def half_kernel(
    kept_ref, got_ref, lora_ref, lora_far_ref, up_ref, mix_ref, down_ref,
    readout_of_up_ref, set_ref, mixes_ref, low_rank_ref,
):
    seq = lax.axis_index("seq")
    rows, channels = mix_ref.shape
    up = up_ref[:, aligned(seq, rows)]
    mine, far = lora_ref[...], lora_far_ref[...]
    share = mine.shape[0] // 2
    first = lax.axis_index("head") % 2 == 0
    low, high = jnp.where(first, mine, far), jnp.where(first, far, mine)
    own = jnp.concatenate([low[:share], high[:share]], axis=0)
    other = jnp.concatenate([low[share:], high[share:]], axis=0)
    low_rank_ref[...] = dot(own, up)
    for i, block in enumerate(finish(kept_ref, got_ref, 2, dot(other, up))):
        set_ref[i] = block
    got = got_ref[:, -2 * channels :].astype(F32)
    mix_full = mix_ref[...] + (got[:, :channels] + swap_halves(got)[:, :channels])
    low_rank = dot(down_ref[aligned(seq, rows), :], readout_of_up_ref[...])
    mix = mix_full.astype(BF16).astype(F32)
    fake = (mix_full + low_rank).astype(BF16).astype(F32)
    mixes_ref[0] = jnp.concatenate([mix, -mix], axis=1).astype(BF16)
    mixes_ref[1] = jnp.concatenate([jnp.zeros_like(fake), fake], axis=1).astype(BF16)


def attention_kernel(
    kept_ref, got_ref, low_rank_ref, set_ref, mixes_ref, base_ref,
    sent_ref, stay_ref, sets_v, terms_v,
):
    core = lax.axis_index("head") % 2
    tokens, channels = base_ref.shape
    columns = set_ref.shape[2]
    for i, block in enumerate(finish(kept_ref, got_ref, 1, low_rank_ref[...])):
        sets_v[i, :tokens] = block
        sets_v[i, tokens:] = set_ref[i]
    terms = jnp.zeros(terms_v.shape, F32)
    rows = 2 * tokens
    for start in range(0, columns, HEAD_SIZE):
        span = slice(start, start + HEAD_SIZE)
        queries = jnp.concatenate([sets_v[0, :, span], sets_v[1, :, span]], axis=0)
        scores = contract_final_axis(queries, sets_v[2, :, span])
        probs = jnp.exp(scores - jnp.max(scores, axis=1, keepdims=True))
        mass = jnp.sum(probs, axis=1, keepdims=True)
        attn = (dot(probs.astype(BF16), sets_v[3, :, span]) * (1.0 / mass)).astype(BF16)
        attn = jnp.concatenate([attn[:rows], attn[rows:]], axis=1)
        mixes = jnp.concatenate([mixes_ref[0, span, :], mixes_ref[1, span, :]], axis=0)
        terms = terms + dot(attn, mixes)
    terms_v[...] = terms
    terms_v[:tokens, :channels] = terms[:tokens, :channels] + base_ref[...]
    share = tokens // 2
    sent_ref[:share] = terms_v[aligned(1 - core, share), :]
    sent_ref[share:] = terms_v[aligned(3 - core, share), :]
    stay_ref[:share] = terms_v[aligned(core, share), :]
    stay_ref[share:] = terms_v[aligned(2 + core, share), :]


def pack_kernel(stay_ref, got_ref, same_ref, cross_ref):
    share = stay_ref.shape[0] // 2
    mine = stay_ref[:share] + got_ref[:share]
    theirs = stay_ref[share:] + got_ref[share:]
    half = share // 2
    same_ref[:share] = mine.astype(BF16)
    same_ref[share:] = fold(theirs[:half], swap_halves(theirs[half:])).astype(BF16)
    cross_ref[:share] = theirs.astype(BF16)
    cross_ref[share:] = fold(mine[:half], swap_halves(mine[half:])).astype(BF16)


def error_kernel(*refs):
    *parts, packet_ref = refs
    parts = [ref[...].astype(F32) for ref in parts]
    while len(parts) > 1:
        parts = [a + b for a, b in zip(parts[::2], parts[1::2])]
    total = parts[0]
    half = packet_ref.shape[0] - 8
    share = 2 * half
    own = jnp.abs(total[:half]) + jnp.abs(total[half:share])
    own = fold(own, jnp.zeros_like(own)) + jnp.abs(total[share:])
    packet_ref[:half] = fold(swap_halves(total[:half]), total[half:share])
    packet_ref[half:] = jnp.full((8, packet_ref.shape[1]), jnp.sum(own), F32)


def last_kernel(mine_ref, theirs_ref, out_ref, both_v):
    core = lax.axis_index("head") % 2
    channels, tokens = out_ref.shape
    share = tokens // 2
    half = share // 2
    weight = (mine_ref[half:] + theirs_ref[half:]) / (2 * tokens * channels)
    weight = weight[:1, :1]
    for ref, index in ((mine_ref, core), (theirs_ref, 1 - core)):
        packet = -ref[:half] / weight
        start = pl.multiple_of(index * share, share)
        both_v[pl.ds(start, half)] = packet
        both_v[pl.ds(start + half, half)] = swap_halves(packet)
    out_ref[...] = both_v[...].T[:channels]


def paired_local(
    sizes,
    latents,
    noise,
    step,
    stream,
    patch_embed_weight,
    prenorm_gain_vector,
    query_matrix,
    key_matrix,
    value_matrix,
    output_matrix,
    velocity_readout_weight,
    adapter_query_down,
    adapter_query_up,
    adapter_output_down,
    adapter_output_up,
):
    groups, _, heads = sizes
    tokens, channels = latents.shape
    half_width, local_columns = query_matrix.shape
    quarter = half_width // 2
    columns = local_columns // 2
    rank = adapter_query_down.shape[1]
    share = tokens // 2
    to_x = pairs((2,), lambda s: (s ^ 1,))
    to_core = pairs((heads,), lambda h: (h ^ 1,))
    to_y = pairs((heads,), lambda h: (h ^ 2,))
    to_xy = pairs((2, heads), lambda s, h: (s ^ 1, h ^ 2))
    partial_flops = 2 * tokens * half_width * (3 * local_columns + rank)

    target = (1 - lax.axis_index("seq")) * 2 + lax.axis_index("head") % 2
    message = columns_of(stream, target, quarter)
    near = lax.ppermute(message, "seq", to_x)
    inputs = (
        latents.T, noise.T, stream, patch_embed_weight, prenorm_gain_vector, value_matrix,
    )
    normed, rows, gap, hidden, gain, patch, value = run(
        first_kernel,
        [
            ((tokens, half_width), BF16),
            ((channels + 16, tokens), BF16),
            ((channels, tokens), F32),
            ((4, tokens, quarter), BF16),
            ((2, quarter), F32),
            ((2, channels, quarter), BF16),
            (value_matrix.shape, BF16),
        ],
        [step, *(pltpu.with_memory_space_constraint(x, pltpu.HBM) for x in inputs)],
        [pl.BlockSpec(memory_space=pl.ANY)] + [HBM] * 6,
        [
            pltpu.SMEM((1,), jnp.int32),
            pltpu.VMEM((channels, tokens), BF16),
            pltpu.VMEM((channels, tokens), BF16),
            pltpu.VMEM((4, tokens, quarter), BF16),
            pltpu.VMEM((4, channels, quarter), BF16),
            pltpu.VMEM((4 * quarter,), F32),
            pltpu.SemaphoreType.DMA((5 + 2 * 4,)),
        ],
    )
    other_rows = lax.ppermute(rows, "seq", to_x)
    own_sent, own_kept, mix_part, down = run(
        own_kernel,
        [
            ((tokens, 6 * columns + 2 * channels), BF16),
            ((tokens, 4 * columns), F32),
            ((columns, channels), F32),
            (adapter_query_down.shape, BF16),
        ],
        (
            normed, query_matrix, key_matrix, value,
            *(
                pltpu.with_memory_space_constraint(x, pltpu.HBM)
                for x in (adapter_query_down, output_matrix, velocity_readout_weight)
            ),
        ),
        [VMEM] * 4 + [HBM] * 3,
        scratch=[
            pltpu.VMEM(output_matrix.shape, BF16),
            pltpu.VMEM((channels, half_width), BF16),
            pltpu.VMEM((local_columns, channels), F32),
            pltpu.SemaphoreType.DMA((3,)),
        ],
        flops=partial_flops,
    )
    own_got = lax.ppermute(own_sent, "seq", to_x)
    readout_of_up, base = run(
        side_kernel,
        [((rank, channels), BF16), ((tokens, channels), F32)],
        (hidden, adapter_output_up, velocity_readout_weight, gap),
        flops=8 * tokens * half_width * channels,
    )
    far = lax.ppermute(near, "head", to_core)
    weights = (query_matrix, key_matrix, value, down)
    shared = (other_rows, patch, gain, *weights)
    near_parts = run(
        near_kernel,
        [((tokens, w.shape[1]), F32) for w in weights],
        (near, *shared),
        flops=partial_flops // 2,
    )
    small_sent, other_sent, other_kept = run(
        far_kernel,
        [
            ((tokens, rank), BF16),
            ((tokens, 3 * columns), BF16),
            ((tokens, 4 * columns), F32),
        ],
        (far, *shared, *near_parts),
        flops=partial_flops // 2,
    )
    small_got = lax.ppermute(small_sent, "seq", to_x)
    other_got = lax.ppermute(other_sent, "seq", to_x)
    (lora,) = run(lora_kernel, [((tokens, rank), BF16)], (own_kept, small_got, other_kept, own_got))
    lora_far = lax.ppermute(lora, "head", to_core)
    half_set, mixes, low_rank = run(
        half_kernel,
        [
            ((4, tokens, columns), BF16),
            ((2, columns, 2 * channels), BF16),
            ((tokens, columns), F32),
        ],
        (
            other_kept, own_got, lora, lora_far, adapter_query_up, mix_part,
            adapter_output_down, readout_of_up,
        ),
    )
    sent, stay = run(
        attention_kernel,
        [((tokens, 2 * channels), F32)] * 2,
        (own_kept, other_got, low_rank, half_set, mixes, base),
        scratch=[
            pltpu.VMEM((4, 2 * tokens, columns), BF16),
            pltpu.VMEM((2 * tokens, 2 * channels), F32),
        ],
    )

    got = lax.ppermute(sent, "head", to_core)
    packed = ((share + share // 2, 2 * channels), BF16)
    same, cross = run(pack_kernel, [packed, packed], (stay, got))
    from_x = lax.ppermute(cross, "seq", to_x)
    from_y = lax.ppermute(same, "head", to_y)
    from_xy = lax.ppermute(cross, ("seq", "head"), to_xy)
    total = (same.astype(F32) + from_y.astype(F32)) + (
        from_x.astype(F32) + from_xy.astype(F32)
    )
    total = total.astype(BF16)
    totals = [total]
    for k in range(1, groups):
        to_group = pairs((groups,), lambda g, k=k: (g ^ k,))
        totals.append(lax.ppermute(total, "group", to_group))
    (packet,) = run(error_kernel, [((share // 2 + 8, 2 * channels), F32)], totals)
    answer = lax.ppermute(packet, "head", to_core)
    (out,) = run(
        last_kernel,
        [((channels, tokens), F32)],
        (packet, answer),
        scratch=[pltpu.VMEM((tokens, 2 * channels), F32)],
    )
    return out.T


def gathered_local(
    latents,
    noise,
    step,
    stream,
    patch_embed_weight,
    prenorm_gain_vector,
    query_matrix,
    key_matrix,
    value_matrix,
    output_matrix,
    velocity_readout_weight,
    adapter_query_down,
    adapter_query_up,
    adapter_output_down,
    adapter_output_up,
):
    tokens = latents.shape[0]
    width = query_matrix.shape[1]
    local_heads = width // HEAD_SIZE
    channels = velocity_readout_weight.shape[0]
    sigma = noise_level(step)
    noisy = (
        (1.0 - sigma) * latents.astype(F32) + sigma * noise.astype(F32)
    ).astype(BF16)
    hidden = (stream.astype(F32) + dot(noisy, patch_embed_weight)).astype(BF16)
    hidden_wide = hidden.astype(F32)
    normed = (
        hidden_wide
        * lax.rsqrt(jnp.mean(hidden_wide * hidden_wide, axis=-1, keepdims=True) + 1e-06)
        * prenorm_gain_vector
    ).astype(BF16)
    base_query, keys, values, lora_hidden = (
        dot(normed, lax.all_gather(piece, "seq", axis=0, tiled=True))
        for piece in (query_matrix, key_matrix, value_matrix, adapter_query_down)
    )
    scale = HEAD_SIZE ** (-0.5)
    lora_delta = dot(lora_hidden.astype(BF16), adapter_query_up)
    queries = (base_query * scale).astype(BF16)
    fake_queries = ((base_query + lora_delta) * scale).astype(BF16)
    both_sets = jnp.stack([queries, fake_queries]).reshape(2, tokens, local_heads, HEAD_SIZE)
    key_rows = lax.all_gather(keys.astype(BF16), "seq", axis=0, tiled=True)
    value_rows = lax.all_gather(values.astype(BF16), "seq", axis=0, tiled=True)
    key_rows = key_rows.reshape(-1, local_heads, HEAD_SIZE)
    value_rows = value_rows.reshape(-1, local_heads, HEAD_SIZE)
    scores = jnp.einsum("sthd,khd->shtk", both_sets, key_rows, preferred_element_type=F32)
    weights = jnp.exp(scores - jnp.max(scores, axis=-1, keepdims=True))
    mass = jnp.sum(weights, axis=-1)
    added = jnp.einsum(
        "shtk,khd->sthd", weights.astype(BF16), value_rows, preferred_element_type=F32
    )
    attn = (added / mass.transpose(0, 2, 1)[..., None]).astype(BF16).reshape(2, tokens, width)
    columns = output_matrix.shape[1]
    readout_part = columns_of(velocity_readout_weight, lax.axis_index("seq"), columns)
    mix_full = lax.psum(contract_final_axis(output_matrix, readout_part), "seq")
    lora_readout = contract_final_axis(adapter_output_up, velocity_readout_weight).astype(BF16)
    fake_mix = (mix_full + dot(adapter_output_down, lora_readout)).astype(BF16)
    real_sum, fake_sum = lax.psum(
        (dot(attn[0], mix_full.astype(BF16)), dot(attn[1], fake_mix)), ("group", "head")
    )
    base = contract_final_axis(hidden, velocity_readout_weight)
    noisy_wide = noisy.astype(F32)
    x0_real = noisy_wide - sigma * (base + real_sum)
    x0_fake = noisy_wide - sigma * (base + fake_sum)
    local_error = jnp.sum(jnp.abs(latents.astype(F32) - x0_real))
    weight = lax.psum(local_error, "seq") / (tokens * lax.axis_size("seq") * channels)
    return (x0_fake - x0_real) / weight


def solution(mesh):
    sizes = tuple(mesh.shape[name] for name in ("group", "seq", "head"))

    def local(*args):
        query_columns = args[6].shape[1]
        power = sizes[0] & (sizes[0] - 1) == 0
        paired = sizes[1] == 2 and sizes[2] == 4 and power
        paired = paired and args[0].shape[0] == query_columns // 2
        if paired and (query_columns // HEAD_SIZE) % 2 == 0:
            return paired_local(sizes, *args)
        return gathered_local(*args)

    split = ("group", "head")
    in_specs = (
        P("seq", None),
        P("seq", None),
        P(),
        P("seq", None),
        P(),
        P(),
        P("seq", split),
        P("seq", split),
        P("seq", split),
        P(split, "seq"),
        P(),
        P("seq", None),
        P(None, split),
        P(split, None),
        P(),
    )
    return jax.shard_map(
        local, mesh=mesh, in_specs=in_specs, out_specs=P("seq", None), check_vma=False
    )
```

```python
import itertools

import jax
import jax.numpy as jnp
from jax import lax
from jax.experimental import pallas as pl
from jax.experimental.pallas import tpu as pltpu
from jax.sharding import PartitionSpec as P


HEAD_SIZE = 128
F32 = jnp.float32
BF16 = jnp.bfloat16


def contract_final_axis(left, right):
    return lax.dot_general(
        left, right, (((1,), (1,)), ((), ())), preferred_element_type=F32
    )


def dot(left, right):
    return jnp.dot(left, right, preferred_element_type=F32)


def noise_level(step):
    level = (step[0].astype(F32) + 1.0) / 1000.0
    return 5.0 * level / (1.0 + 4.0 * level)


def pairs(sizes, partner):
    def linear(coordinate):
        index = 0
        for value, size in zip(coordinate, sizes):
            index = index * size + value
        return index

    return [
        (linear(c), linear(partner(*c)))
        for c in itertools.product(*[range(n) for n in sizes])
    ]


def columns_of(x, index, count):
    return lax.dynamic_slice_in_dim(x, index * count, count, 1)


VMEM = pl.BlockSpec(memory_space=pltpu.VMEM)
HBM = pl.BlockSpec(memory_space=pltpu.HBM)


def run(kernel, outs, args, specs=None, scratch=(), flops=0, limit=8 << 20, moved=None):
    shapes = [jax.ShapeDtypeStruct(shape, kind) for shape, kind in outs]
    if moved is None:
        moved = sum(a.size * a.dtype.itemsize for a in (*args, *shapes))
    return pl.pallas_call(
        kernel,
        out_shape=shapes,
        in_specs=specs or [VMEM] * len(args),
        out_specs=[VMEM] * len(shapes),
        scratch_shapes=list(scratch),
        cost_estimate=pl.CostEstimate(flops=flops, bytes_accessed=moved, transcendentals=0),
        compiler_params=pltpu.CompilerParams(vmem_limit_bytes=limit),
    )(*args)


def aligned(index, count):
    return pl.ds(pl.multiple_of(index * count, count), count)


def fold(low, high):
    lane = lax.broadcasted_iota(jnp.int32, low.shape, 1)
    return jnp.where(lane < low.shape[1] // 2, low, high)


def swap_halves(x):
    return pltpu.roll(x, x.shape[1] // 2, 1)


def high_low(x):
    high = x.astype(BF16)
    return high, (x - high.astype(F32)).astype(BF16)


def pass_kernel(message_ref, *refs):
    pass


def first_kernel(
    step_any, latents_hbm, noise_hbm, stream_hbm, patch_hbm, gain_hbm,
    normed_ref, rows_ref, gap_ref, hidden_ref, gain_ref, patch_ref,
    step_s, latents_v, noise_v, stream_v, patch_v, gain_v, sems,
):
    parts, tokens, quarter = stream_v.shape
    channels = latents_v.shape[0]
    seq = lax.axis_index("seq")
    small = [
        pltpu.make_async_copy(latents_hbm, latents_v, sems.at[0]),
        pltpu.make_async_copy(noise_hbm, noise_v, sems.at[1]),
        pltpu.make_async_copy(step_any, step_s, sems.at[2]),
    ]
    gain_copy = pltpu.make_async_copy(gain_hbm, gain_v, sems.at[3])
    large = []
    for j in range(parts):
        span = pl.ds(j * quarter, quarter)
        large.append([
            pltpu.make_async_copy(source.at[:, span], target.at[j], sems.at[4 + 2 * j + i])
            for i, (source, target) in enumerate(
                ((stream_hbm, stream_v), (patch_hbm, patch_v))
            )
        ])
    for copy in small:
        copy.start()
    for j in range(parts):
        for copy in large[j]:
            copy.start()
    gain_copy.start()
    for copy in small:
        copy.wait()
    level = (jnp.full((8, 128), step_s[0], jnp.int32).astype(F32) + 1.0) / 1000.0
    sigma = (5.0 * level / (1.0 + 4.0 * level))[:1, :1]
    latents = latents_v[...].astype(F32)
    noisy = ((1.0 - sigma) * latents + sigma * noise_v[...].astype(F32)).astype(BF16)
    gap_ref[...] = (latents - noisy.astype(F32)) / sigma
    squares = jnp.zeros((tokens, 128), F32)
    for j in range(parts):
        for copy in large[j]:
            copy.wait()
        embedded = lax.dot_general(
            noisy, patch_v[j], (((0,), (0,)), ((), ())), preferred_element_type=F32
        )
        hidden = (stream_v[j].astype(F32) + embedded).astype(BF16)
        hidden_ref[j] = hidden
        wide = hidden.astype(F32)
        wide = wide * wide
        for i in range(quarter // 128):
            squares = squares + wide[:, i * 128 : (i + 1) * 128]
    mean = jnp.sum(squares, axis=1, keepdims=True) / (parts * quarter)
    inverse = lax.rsqrt(mean + 1e-06)
    rows_ref[:channels] = noisy
    scale = jnp.broadcast_to(inverse, (tokens, tokens)).T[:8]
    first, _ = high_low(scale)
    second, third = high_low(scale - first.astype(F32))
    row = lax.broadcasted_iota(jnp.int32, (16, tokens), 0)
    terms = [jnp.concatenate([x.astype(F32)] * 2, axis=0) for x in (first, second, third)]
    terms = jnp.where(row == 0, terms[0], jnp.where(row == 1, terms[1], terms[2]))
    rows_ref[channels:] = terms.astype(BF16)
    gain_copy.wait()
    for j in range(parts):

        @pl.when(seq == j // 2)
        def _(j=j):
            gain = gain_v[j * quarter : (j + 1) * quarter][None, :]
            start = (j % 2) * quarter
            gain_ref[j % 2 : j % 2 + 1] = gain
            patch_ref[j % 2] = patch_v[j]
            normed_ref[:, start : start + quarter] = (
                hidden_ref[j].astype(F32) * inverse * gain
            ).astype(BF16)


def pick(index, x):
    half = x.shape[1] // 2
    return jnp.where(index == 0, x[:, :half], x[:, half:])


def partial_outputs(parts, seq, terms, lora_blocks, sent_ref, kept_ref):
    q, k, v, lora = parts
    columns = q.shape[1] // 2
    blocks = [*high_low(pick(1 - seq, q))[:terms], *high_low(pick(1 - seq, k))[:terms]]
    blocks += [pick(1 - seq, v).astype(BF16), *lora_blocks]
    for i, block in enumerate(blocks):
        sent_ref[:, i * columns : (i + 1) * columns] = block
    for i, block in enumerate((pick(seq, q), pick(seq, k), pick(seq, v), lora)):
        kept_ref[:, i * columns : (i + 1) * columns] = block


def half_rows(x):
    share = x.shape[0] // 2
    half = jnp.where(lax.axis_index("head") % 2 == 0, x[:share], x[share:])
    return jnp.concatenate(high_low(half), axis=0)


def own_kernel(
    normed_ref, q_ref, k_ref, v_ref, down_hbm, output_v, readout_hbm,
    sent_ref, kept_ref, mix_ref, down_v,
    readout_v, mix_v, sems,
):
    seq = lax.axis_index("seq")
    copies = [
        pltpu.make_async_copy(down_hbm, down_v, sems.at[0]),
        pltpu.make_async_copy(
            readout_hbm.at[:, aligned(seq, readout_v.shape[1])], readout_v, sems.at[2]
        ),
    ]
    for copy in copies:
        copy.start()
    normed = normed_ref[...]
    parts = [dot(normed, w[...]) for w in (q_ref, k_ref, v_ref)]
    copies[0].wait()
    lora = dot(normed, down_v[...])
    parts.append(lora)
    partial_outputs(parts, seq, 2, [half_rows(lora)], sent_ref, kept_ref)
    for copy in copies[1:]:
        copy.wait()
    mix_v[...] = contract_final_axis(output_v[...], readout_v[...])
    rows, channels = mix_ref.shape
    theirs = mix_v[aligned(1 - seq, rows), :]
    high = theirs.astype(BF16).astype(F32)
    both = jnp.concatenate([high, theirs - high], axis=1)
    sent_ref[:, -2 * channels :] = both.astype(BF16)
    mix_ref[...] = mix_v[aligned(seq, rows), :]


def side_kernel(hidden_ref, up_ref, readout_ref, gap_ref, readout_of_up_ref, base_ref):
    parts, _, quarter = hidden_ref.shape
    readout_of_up_ref[...] = contract_final_axis(up_ref[...], readout_ref[...]).astype(BF16)
    base = gap_ref[...]
    for j in range(parts):
        base += contract_final_axis(
            readout_ref[:, j * quarter : (j + 1) * quarter], hidden_ref[j]
        )
    once = (lax.axis_index("group") == 0) & (lax.axis_index("head") == 0)
    base_ref[...] = jnp.where(once, base, 0.0).T


def other_parts(part, raw_ref, rows_ref, patch_ref, gain_ref, weights):
    tokens, quarter = raw_ref.shape
    channels = patch_ref.shape[1]
    noisy = rows_ref[:channels]
    terms = rows_ref[channels:].astype(F32)
    scale = (terms[:1] + terms[1:2]) + terms[2:3]
    inverse = jnp.broadcast_to(scale, (tokens, tokens)).T[:, :1]
    embedded = lax.dot_general(
        noisy, patch_ref[part],
        (((0,), (0,)), ((), ())), preferred_element_type=F32,
    )
    hidden = (raw_ref[...].astype(F32) + embedded).astype(BF16).astype(F32)
    normed = (hidden * inverse * gain_ref[pl.ds(part, 1), :]).astype(BF16)
    return [dot(normed, w[aligned(part, quarter), :]) for w in weights]


def near_kernel(raw_ref, rows_ref, patch_ref, gain_ref, q_ref, k_ref, v_ref, down_ref, *outs):
    core = lax.axis_index("head") % 2
    weights = (q_ref, k_ref, v_ref, down_ref)
    parts = other_parts(core, raw_ref, rows_ref, patch_ref, gain_ref, weights)
    for out, part in zip(outs, parts):
        out[...] = part


def far_kernel(
    raw_ref, rows_ref, patch_ref, gain_ref, q_ref, k_ref, v_ref, down_ref,
    near_q_ref, near_k_ref, near_v_ref, near_down_ref,
    small_ref, sent_ref, kept_ref,
):
    core = lax.axis_index("head") % 2
    weights = (q_ref, k_ref, v_ref, down_ref)
    parts = other_parts(1 - core, raw_ref, rows_ref, patch_ref, gain_ref, weights)
    near = (near_q_ref, near_k_ref, near_v_ref, near_down_ref)
    parts = [part + ref[...] for part, ref in zip(parts, near)]
    small_ref[...] = half_rows(parts[3])
    partial_outputs(parts, lax.axis_index("seq"), 1, [], sent_ref, kept_ref)


def finish(kept_ref, got_ref, terms, low_rank):
    columns = low_rank.shape[1]

    def got(i):
        return got_ref[:, i * columns : (i + 1) * columns].astype(F32)

    def kept(i):
        return kept_ref[:, i * columns : (i + 1) * columns]

    scale = HEAD_SIZE ** (-0.5)

    def got_sum(start):
        return sum(got(start + i) for i in reversed(range(terms)))

    base = kept(0) + got_sum(0)
    return (
        (base * scale).astype(BF16),
        ((base + low_rank) * scale).astype(BF16),
        (kept(1) + got_sum(terms)).astype(BF16),
        (kept(2) + got(2 * terms)).astype(BF16),
    )


def lora_kernel(own_kept_ref, small_got_ref, other_kept_ref, own_got_ref, lora_ref):
    rank = lora_ref.shape[1]
    share = lora_ref.shape[0] // 2
    core = lax.axis_index("head") % 2
    for i, (kept_ref, got) in enumerate((
        (own_kept_ref, small_got_ref[...]),
        (other_kept_ref, own_got_ref[:, 5 * rank : 6 * rank]),
    )):
        kept = kept_ref[aligned(core, share), kept_ref.shape[1] - rank :]
        got = got.astype(F32)
        lora_ref[i * share : (i + 1) * share] = (
            kept + (got[:share] + got[share:])
        ).astype(BF16)


def half_kernel(
    kept_ref, got_ref, lora_ref, lora_far_ref, up_ref, mix_ref, down_ref,
    readout_of_up_ref, set_ref, mixes_ref, low_rank_ref,
):
    seq = lax.axis_index("seq")
    rows, channels = mix_ref.shape
    up = up_ref[:, aligned(seq, rows)]
    mine, far = lora_ref[...], lora_far_ref[...]
    share = mine.shape[0] // 2
    first = lax.axis_index("head") % 2 == 0
    low, high = jnp.where(first, mine, far), jnp.where(first, far, mine)
    own = jnp.concatenate([low[:share], high[:share]], axis=0)
    other = jnp.concatenate([low[share:], high[share:]], axis=0)
    low_rank_ref[...] = dot(own, up)
    for i, block in enumerate(finish(kept_ref, got_ref, 2, dot(other, up))):
        set_ref[i] = block
    got = got_ref[:, -2 * channels :].astype(F32)
    mix_full = mix_ref[...] + (got[:, :channels] + swap_halves(got)[:, :channels])
    low_rank = dot(down_ref[aligned(seq, rows), :], readout_of_up_ref[...])
    mix = mix_full.astype(BF16).astype(F32)
    fake = (mix_full + low_rank).astype(BF16).astype(F32)
    mixes_ref[0] = jnp.concatenate([mix, -mix], axis=1).astype(BF16)
    mixes_ref[1] = jnp.concatenate([jnp.zeros_like(fake), fake], axis=1).astype(BF16)


def attention_kernel(
    kept_ref, got_ref, low_rank_ref, set_ref, mixes_ref, base_ref,
    sent_ref, stay_ref, sets_v, terms_v,
):
    core = lax.axis_index("head") % 2
    tokens, channels = base_ref.shape
    columns = set_ref.shape[2]
    for i, block in enumerate(finish(kept_ref, got_ref, 1, low_rank_ref[...])):
        sets_v[i, :tokens] = block
        sets_v[i, tokens:] = set_ref[i]
    terms = jnp.zeros(terms_v.shape, F32)
    rows = 2 * tokens
    for start in range(0, columns, HEAD_SIZE):
        span = slice(start, start + HEAD_SIZE)
        queries = jnp.concatenate([sets_v[0, :, span], sets_v[1, :, span]], axis=0)
        scores = contract_final_axis(queries, sets_v[2, :, span])
        probs = jnp.exp(scores - jnp.max(scores, axis=1, keepdims=True))
        mass = jnp.sum(probs, axis=1, keepdims=True)
        attn = (dot(probs.astype(BF16), sets_v[3, :, span]) * (1.0 / mass)).astype(BF16)
        attn = jnp.concatenate([attn[:rows], attn[rows:]], axis=1)
        mixes = jnp.concatenate([mixes_ref[0, span, :], mixes_ref[1, span, :]], axis=0)
        terms = terms + dot(attn, mixes)
    terms_v[...] = terms
    terms_v[:tokens, :channels] = terms[:tokens, :channels] + base_ref[...]
    share = tokens // 2
    sent_ref[:share] = terms_v[aligned(1 - core, share), :]
    sent_ref[share:] = terms_v[aligned(3 - core, share), :]
    stay_ref[:share] = terms_v[aligned(core, share), :]
    stay_ref[share:] = terms_v[aligned(2 + core, share), :]


def pack_kernel(stay_ref, got_ref, same_ref, cross_ref):
    share = stay_ref.shape[0] // 2
    mine = stay_ref[:share] + got_ref[:share]
    theirs = stay_ref[share:] + got_ref[share:]
    half = share // 2
    same_ref[:share] = mine.astype(BF16)
    same_ref[share:] = fold(theirs[:half], swap_halves(theirs[half:])).astype(BF16)
    cross_ref[:share] = theirs.astype(BF16)
    cross_ref[share:] = fold(mine[:half], swap_halves(mine[half:])).astype(BF16)


def error_kernel(*refs):
    *parts, packet_ref = refs
    parts = [ref[...].astype(F32) for ref in parts]
    while len(parts) > 1:
        parts = [a + b for a, b in zip(parts[::2], parts[1::2])]
    total = parts[0]
    half = packet_ref.shape[0] - 8
    share = 2 * half
    own = jnp.abs(total[:half]) + jnp.abs(total[half:share])
    own = fold(own, jnp.zeros_like(own)) + jnp.abs(total[share:])
    packet_ref[:half] = fold(swap_halves(total[:half]), total[half:share])
    packet_ref[half:] = jnp.full((8, packet_ref.shape[1]), jnp.sum(own), F32)


def last_kernel(mine_ref, theirs_ref, out_ref, both_v):
    core = lax.axis_index("head") % 2
    channels, tokens = out_ref.shape
    share = tokens // 2
    half = share // 2
    weight = (mine_ref[half:] + theirs_ref[half:]) / (2 * tokens * channels)
    weight = weight[:1, :1]
    for ref, index in ((mine_ref, core), (theirs_ref, 1 - core)):
        packet = -ref[:half] / weight
        start = pl.multiple_of(index * share, share)
        both_v[pl.ds(start, half)] = packet
        both_v[pl.ds(start + half, half)] = swap_halves(packet)
    out_ref[...] = both_v[...].T[:channels]


def paired_local(
    sizes,
    latents,
    noise,
    step,
    stream,
    patch_embed_weight,
    prenorm_gain_vector,
    query_matrix,
    key_matrix,
    value_matrix,
    output_matrix,
    velocity_readout_weight,
    adapter_query_down,
    adapter_query_up,
    adapter_output_down,
    adapter_output_up,
):
    groups, _, heads = sizes
    tokens, channels = latents.shape
    half_width, local_columns = query_matrix.shape
    quarter = half_width // 2
    columns = local_columns // 2
    rank = adapter_query_down.shape[1]
    share = tokens // 2
    to_x = pairs((2,), lambda s: (s ^ 1,))
    to_core = pairs((heads,), lambda h: (h ^ 1,))
    to_y = pairs((heads,), lambda h: (h ^ 2,))
    to_xy = pairs((2, heads), lambda s, h: (s ^ 1, h ^ 2))
    partial_flops = 2 * tokens * half_width * (3 * local_columns + rank)

    target = (1 - lax.axis_index("seq")) * 2 + lax.axis_index("head") % 2
    message = columns_of(stream, target, quarter)
    for _ in range(2):
        message = pl.pallas_call(
            pass_kernel,
            out_shape=jax.ShapeDtypeStruct(message.shape, BF16),
            in_specs=[VMEM] + [HBM] * 4,
            out_specs=VMEM,
            input_output_aliases={0: 0},
            compiler_params=pltpu.CompilerParams(vmem_limit_bytes=1 << 20),
        )(message, *(
            pltpu.with_memory_space_constraint(x, pltpu.HBM)
            for x in (query_matrix, key_matrix, value_matrix, output_matrix)
        ))
    near = lax.ppermute(message, "seq", to_x)
    inputs = (
        latents.T, noise.T, stream, patch_embed_weight, prenorm_gain_vector,
    )
    normed, rows, gap, hidden, gain, patch = run(
        first_kernel,
        [
            ((tokens, half_width), BF16),
            ((channels + 16, tokens), BF16),
            ((channels, tokens), F32),
            ((4, tokens, quarter), BF16),
            ((2, quarter), F32),
            ((2, channels, quarter), BF16),
        ],
        [step, *(pltpu.with_memory_space_constraint(x, pltpu.HBM) for x in inputs)],
        [pl.BlockSpec(memory_space=pl.ANY)] + [HBM] * 5,
        [
            pltpu.SMEM((1,), jnp.int32),
            pltpu.VMEM((channels, tokens), BF16),
            pltpu.VMEM((channels, tokens), BF16),
            pltpu.VMEM((4, tokens, quarter), BF16),
            pltpu.VMEM((4, channels, quarter), BF16),
            pltpu.VMEM((4 * quarter,), F32),
            pltpu.SemaphoreType.DMA((5 + 2 * 4,)),
        ],
    )
    other_rows = lax.ppermute(rows, "seq", to_x)
    own_sent, own_kept, mix_part, down = run(
        own_kernel,
        [
            ((tokens, 6 * columns + 2 * channels), BF16),
            ((tokens, 4 * columns), F32),
            ((columns, channels), F32),
            (adapter_query_down.shape, BF16),
        ],
        (
            normed, query_matrix, key_matrix, value_matrix,
            pltpu.with_memory_space_constraint(adapter_query_down, pltpu.HBM),
            output_matrix,
            pltpu.with_memory_space_constraint(velocity_readout_weight, pltpu.HBM),
        ),
        [VMEM] * 4 + [HBM, VMEM, HBM],
        scratch=[
            pltpu.VMEM((channels, half_width), BF16),
            pltpu.VMEM((local_columns, channels), F32),
            pltpu.SemaphoreType.DMA((3,)),
        ],
        flops=partial_flops,
    )
    own_got = lax.ppermute(own_sent, "seq", to_x)
    readout_of_up, base = run(
        side_kernel,
        [((rank, channels), BF16), ((tokens, channels), F32)],
        (hidden, adapter_output_up, velocity_readout_weight, gap),
        flops=8 * tokens * half_width * channels,
    )
    far = lax.ppermute(near, "head", to_core)
    weights = (query_matrix, key_matrix, value_matrix, down)
    shared = (other_rows, patch, gain, *weights)
    near_parts = run(
        near_kernel,
        [((tokens, w.shape[1]), F32) for w in weights],
        (near, *shared),
        flops=partial_flops // 2,
    )
    small_sent, other_sent, other_kept = run(
        far_kernel,
        [
            ((tokens, rank), BF16),
            ((tokens, 3 * columns), BF16),
            ((tokens, 4 * columns), F32),
        ],
        (far, *shared, *near_parts),
        flops=partial_flops // 2,
    )
    small_got = lax.ppermute(small_sent, "seq", to_x)
    other_got = lax.ppermute(other_sent, "seq", to_x)
    (lora,) = run(
        lora_kernel,
        [((tokens, rank), BF16)],
        (own_kept, small_got, other_kept, own_got),
    )
    lora_far = lax.ppermute(lora, "head", to_core)
    half_set, mixes, low_rank = run(
        half_kernel,
        [
            ((4, tokens, columns), BF16),
            ((2, columns, 2 * channels), BF16),
            ((tokens, columns), F32),
        ],
        (
            other_kept, own_got, lora, lora_far, adapter_query_up, mix_part,
            adapter_output_down, readout_of_up,
        ),
    )
    sent, stay = run(
        attention_kernel,
        [((tokens, 2 * channels), F32)] * 2,
        (own_kept, other_got, low_rank, half_set, mixes, base),
        scratch=[
            pltpu.VMEM((4, 2 * tokens, columns), BF16),
            pltpu.VMEM((2 * tokens, 2 * channels), F32),
        ],
    )

    got = lax.ppermute(sent, "head", to_core)
    packed = ((share + share // 2, 2 * channels), BF16)
    same, cross = run(pack_kernel, [packed, packed], (stay, got))
    from_x = lax.ppermute(cross, "seq", to_x)
    from_y = lax.ppermute(same, "head", to_y)
    from_xy = lax.ppermute(cross, ("seq", "head"), to_xy)
    total = (same.astype(F32) + from_y.astype(F32)) + (
        from_x.astype(F32) + from_xy.astype(F32)
    )
    total = total.astype(BF16)
    totals = [total]
    for k in range(1, groups):
        to_group = pairs((groups,), lambda g, k=k: (g ^ k,))
        totals.append(lax.ppermute(total, "group", to_group))
    (packet,) = run(error_kernel, [((share // 2 + 8, 2 * channels), F32)], totals)
    answer = lax.ppermute(packet, "head", to_core)
    (out,) = run(
        last_kernel,
        [((channels, tokens), F32)],
        (packet, answer),
        scratch=[pltpu.VMEM((tokens, 2 * channels), F32)],
    )
    return out.T


def gathered_local(
    latents,
    noise,
    step,
    stream,
    patch_embed_weight,
    prenorm_gain_vector,
    query_matrix,
    key_matrix,
    value_matrix,
    output_matrix,
    velocity_readout_weight,
    adapter_query_down,
    adapter_query_up,
    adapter_output_down,
    adapter_output_up,
):
    tokens = latents.shape[0]
    width = query_matrix.shape[1]
    local_heads = width // HEAD_SIZE
    channels = velocity_readout_weight.shape[0]
    sigma = noise_level(step)
    noisy = (
        (1.0 - sigma) * latents.astype(F32) + sigma * noise.astype(F32)
    ).astype(BF16)
    hidden = (stream.astype(F32) + dot(noisy, patch_embed_weight)).astype(BF16)
    hidden_wide = hidden.astype(F32)
    normed = (
        hidden_wide
        * lax.rsqrt(jnp.mean(hidden_wide * hidden_wide, axis=-1, keepdims=True) + 1e-06)
        * prenorm_gain_vector
    ).astype(BF16)
    base_query, keys, values, lora_hidden = (
        dot(normed, lax.all_gather(piece, "seq", axis=0, tiled=True))
        for piece in (query_matrix, key_matrix, value_matrix, adapter_query_down)
    )
    scale = HEAD_SIZE ** (-0.5)
    lora_delta = dot(lora_hidden.astype(BF16), adapter_query_up)
    queries = (base_query * scale).astype(BF16)
    fake_queries = ((base_query + lora_delta) * scale).astype(BF16)
    both_sets = jnp.stack([queries, fake_queries]).reshape(2, tokens, local_heads, HEAD_SIZE)
    key_rows = lax.all_gather(keys.astype(BF16), "seq", axis=0, tiled=True)
    value_rows = lax.all_gather(values.astype(BF16), "seq", axis=0, tiled=True)
    key_rows = key_rows.reshape(-1, local_heads, HEAD_SIZE)
    value_rows = value_rows.reshape(-1, local_heads, HEAD_SIZE)
    scores = jnp.einsum("sthd,khd->shtk", both_sets, key_rows, preferred_element_type=F32)
    weights = jnp.exp(scores - jnp.max(scores, axis=-1, keepdims=True))
    mass = jnp.sum(weights, axis=-1)
    added = jnp.einsum(
        "shtk,khd->sthd", weights.astype(BF16), value_rows, preferred_element_type=F32
    )
    attn = (added / mass.transpose(0, 2, 1)[..., None]).astype(BF16).reshape(2, tokens, width)
    columns = output_matrix.shape[1]
    readout_part = columns_of(velocity_readout_weight, lax.axis_index("seq"), columns)
    mix_full = lax.psum(contract_final_axis(output_matrix, readout_part), "seq")
    lora_readout = contract_final_axis(adapter_output_up, velocity_readout_weight).astype(BF16)
    fake_mix = (mix_full + dot(adapter_output_down, lora_readout)).astype(BF16)
    real_sum, fake_sum = lax.psum(
        (dot(attn[0], mix_full.astype(BF16)), dot(attn[1], fake_mix)), ("group", "head")
    )
    base = contract_final_axis(hidden, velocity_readout_weight)
    noisy_wide = noisy.astype(F32)
    x0_real = noisy_wide - sigma * (base + real_sum)
    x0_fake = noisy_wide - sigma * (base + fake_sum)
    local_error = jnp.sum(jnp.abs(latents.astype(F32) - x0_real))
    weight = lax.psum(local_error, "seq") / (tokens * lax.axis_size("seq") * channels)
    return (x0_fake - x0_real) / weight


def solution(mesh):
    sizes = tuple(mesh.shape[name] for name in ("group", "seq", "head"))

    def local(*args):
        query_columns = args[6].shape[1]
        power = sizes[0] & (sizes[0] - 1) == 0
        paired = sizes[1] == 2 and sizes[2] == 4 and power
        paired = paired and args[0].shape[0] == query_columns // 2
        if paired and (query_columns // HEAD_SIZE) % 2 == 0:
            return paired_local(sizes, *args)
        return gathered_local(*args)

    split = ("group", "head")
    in_specs = (
        P("seq", None),
        P("seq", None),
        P(),
        P("seq", None),
        P(),
        P(),
        P("seq", split),
        P("seq", split),
        P("seq", split),
        P(split, "seq"),
        P(),
        P("seq", None),
        P(None, split),
        P(split, None),
        P(),
    )
    return jax.shard_map(
        local, mesh=mesh, in_specs=in_specs, out_specs=P("seq", None), check_vma=False
    )
```
